128 devices in a mesh: box: 8 (over y, core), samp: 16 (over x, z).
Axes of the slice: x: 4, y: 4, z: 4, core: 2. Of those that a mesh axis runs over, the one named last changes fastest.
Arguments:
- children: bfloat16 [2048, 2, 64, 128], P('box', None, 'samp'), may hold values from -6 to 6
- interp_theta: bfloat16 [64, 128], replicated, may hold values from -0.75 to 0.75
- interp_phi: bfloat16 [128, 256], replicated, may hold values from -0.5 to 0.5
- translator: bfloat16 [316, 2, 128, 256], P(None, None, 'samp'), may hold values from -0.1796875 to 0.1796875
- send_index: int32 [8, 8, 16], P('box'), may hold values from 0 to 31, as said below
- list_slots: int32 [256, 64], P('box'), may hold values from 0 to 127, as said below
- list_kinds: int32 [256, 64], P('box'), may hold values from 0 to 315
Outputs:
- parent_pattern: bfloat16 [256, 2, 128, 256], P('box', None, 'samp')
- local_field: float32 [256, 2, 128, 256], P('box', None, 'samp')
The draws below stay inside these ranges and needn't reach their ends.
Inputs may be any that keep to these rules, and one draw needn't show every extreme that they name: The 16 entries of send_index[s, d] are distinct, and 31 is among them. `list_slots`: each sender sends a receiver a number of live slots between 4 and 16, the first ones; codes name only live slots, senders are spread over all devices of box, and some receiver has a sender with all 16 slots live.
All inputs are finite; a program needn't handle non-finite values.
Results may differ from the reference program's by a relative error of at most 0.0049.
Values may be sent and summed in bfloat16 or wider, within the bound.
No kernel may reach another device: no remote copies, remote signals or barrier semaphores. Data moves between devices by JAX's collectives and lax.ppermute only.
A program may use at most 192 MiB of HBM per device.

```python
import math
import jax
import jax.numpy as jnp
from jax import lax

TC = 64
PC = 128
TP = 128
PP = 256
M = 64
R = 316
NP_DEV = 32
CAP = 16
NC = 2048
NP = 256


def draw_send_index(key, part):
    peer_count = NP // NP_DEV

    def one_pair(pair_key):
        first_key, second_key = jax.random.split(pair_key)
        others = jax.random.permutation(first_key, NP_DEV - 1)[:CAP - 1].astype(jnp.int32)
        filled = jnp.concatenate([jnp.full((1,), NP_DEV - 1, jnp.int32), others])
        return jnp.roll(filled, jax.random.randint(second_key, (), 0, CAP))
    pair_keys = jax.random.split(jax.random.fold_in(key, 11), peer_count * peer_count)
    return jax.vmap(one_pair)(pair_keys).reshape(peer_count, peer_count, CAP).astype(jnp.int32)


def draw_list_slots(key, part):
    peer_count = NP // NP_DEV
    key_count, key_owner, key_slot = jax.random.split(jax.random.fold_in(key, 23), 3)
    live_table = jax.random.randint(key_count, (peer_count, peer_count), CAP // 4, CAP + 1)
    live_table = live_table.at[peer_count - 1, 0].set(CAP)
    receiver = (jnp.arange(NP, dtype=jnp.int32) // NP_DEV)[:, None] + jnp.zeros((1, M), jnp.int32)
    owner_draw = jax.random.randint(key_owner, (NP, M), 0, peer_count)
    live_count = live_table[owner_draw, receiver]
    slot_draw = jax.random.randint(key_slot, (NP, M), 0, live_count)
    list_codes = owner_draw * CAP + slot_draw
    list_codes = list_codes.at[0, 0].set(peer_count * CAP - 1)
    list_codes = list_codes.at[1, 0].set(0)
    return list_codes.astype(jnp.int32)


def with_ends(array, stream_key, low, largest):
    longest = array.shape.index(max(array.shape))
    spots = []
    for shift in (0, 1):
        where = [jax.random.randint(jax.random.fold_in(stream_key, axis), (), 0, length) for axis, length in enumerate(array.shape)]
        where[longest] = (where[longest] + shift) % array.shape[longest]
        spots.append(tuple(where))
    return array.at[spots[0]].set(low).at[spots[1]].set(largest)


def block_scale(key, shape, cuts, low, high):
    loudness, own = 1.0, jax.random.fold_in(key, 6)
    for dim, blocks in cuts:
        steps = jnp.exp(jax.random.uniform(jax.random.fold_in(own, dim), (blocks,), jnp.float32, low / len(cuts), high / len(cuts)))
        loudness = loudness * jnp.repeat(steps, shape[dim] // blocks).reshape([-1 if axis == dim else 1 for axis in range(len(shape))])
    return loudness


def normal_values(rng, shape, spread, most, pieces=(), held_as=jnp.bfloat16):
    drawn = spread * jax.random.normal(rng, shape, jnp.float32)
    if pieces:
        drawn = drawn * block_scale(rng, shape, pieces, -0.22, 0.18)
    return jnp.clip(drawn, -most, most).astype(held_as)


def setup_inputs(seed: int = 0) -> dict:
    splits = jax.random.split(jax.random.key(seed), 8)
    children = normal_values(splits[0], (NC, 2, TC, PC), 1.0, 6.0, ((0, 8), (2, 16)))
    interp_theta = normal_values(splits[1], (TC, TP), TC ** -0.5, 0.75)
    interp_phi = normal_values(splits[2], (PC, PP), PC ** -0.5, 0.5)
    translator = normal_values(splits[3], (R, 2, TP, PP), 0.03, 0.1796875, ((2, 16),))
    send_index = draw_send_index(jax.random.fold_in(splits[7], 71), 0)
    list_slots = draw_list_slots(jax.random.fold_in(splits[7], 71), 0)
    list_kinds = with_ends(jax.random.randint(splits[6], (NP, M), 0, R), jax.random.fold_in(splits[6], 1), 0, R - 1).astype(jnp.int32)
    return dict(children=children, interp_theta=interp_theta, interp_phi=interp_phi, translator=translator, send_index=send_index, list_slots=list_slots, list_kinds=list_kinds)


KAPPA_H = 12.0


def octant_phase(polar_rows, polar_total, azimuth_total):
    polar = (polar_rows.astype(jnp.float32) + 0.5) * (math.pi / polar_total)
    azimuth = jnp.arange(azimuth_total, dtype=jnp.int32).astype(jnp.float32) * (2.0 * math.pi / azimuth_total)
    octant = jnp.arange(8, dtype=jnp.int32)
    sign_x = ((octant & 1) * 2 - 1).astype(jnp.float32)[:, None, None]
    sign_y = (((octant >> 1) & 1) * 2 - 1).astype(jnp.float32)[:, None, None]
    sign_z = (((octant >> 2) & 1) * 2 - 1).astype(jnp.float32)[:, None, None]
    along_x = jnp.sin(polar)[:, None] * jnp.cos(azimuth)[None, :]
    along_y = jnp.sin(polar)[:, None] * jnp.sin(azimuth)[None, :]
    along_z = jnp.cos(polar)[:, None] + jnp.zeros((1, azimuth_total), jnp.float32)
    phase_angle = KAPPA_H * (sign_x * along_x + sign_y * along_y + sign_z * along_z)
    return jnp.cos(phase_angle), jnp.sin(phase_angle)


def aggregate(group, interp_theta, interp_phi, cosine, sine_part):
    theta_int = jnp.einsum('nocta,tu->nocua', group.astype(jnp.float32), interp_theta.astype(jnp.float32)).astype(jnp.bfloat16)
    raised = jnp.einsum('nocua,ag->nocug', theta_int.astype(jnp.float32), interp_phi.astype(jnp.float32))
    real_part = raised[:, :, 0]
    imag_part = raised[:, :, 1]
    rotated_real = jnp.sum(cosine * real_part - sine_part * imag_part, axis=1)
    rotated_imag = jnp.sum(sine_part * real_part + cosine * imag_part, axis=1)
    return jnp.stack([rotated_real, rotated_imag], axis=1).astype(jnp.bfloat16)


def reference(children, interp_theta, interp_phi, translator, send_index, list_slots, list_kinds):
    cosine, sine_part = octant_phase(jnp.arange(TP, dtype=jnp.int32), TP, PP)
    grouped = children.reshape(NP // 4, 4, 8, 2, TC, PC)

    def one_block(group):
        return aggregate(group, interp_theta, interp_phi, cosine, sine_part)

    parent_pattern = lax.map(one_block, grouped).reshape(NP, 2, TP, PP)
    owner = list_slots // CAP
    slot_pick = list_slots % CAP
    receiver = (jnp.arange(NP, dtype=jnp.int32) // NP_DEV)[:, None] + jnp.zeros((1, M), jnp.int32)
    source_box = owner * NP_DEV + send_index[owner, receiver, slot_pick]

    def translate_box(pair):
        picked, picked_kinds = pair
        sources = parent_pattern[picked].astype(jnp.float32)
        factors = translator[picked_kinds].astype(jnp.float32)
        field_real = jnp.sum(factors[:, 0] * sources[:, 0] - factors[:, 1] * sources[:, 1], axis=0)
        field_imag = jnp.sum(factors[:, 0] * sources[:, 1] + factors[:, 1] * sources[:, 0], axis=0)
        return jnp.stack([field_real, field_imag])

    local_field = lax.map(translate_box, (source_box, list_kinds))
    return parent_pattern, local_field
```

```python
import math

import jax
import jax.numpy as jnp
from jax import lax
from jax.experimental import pallas as pl
from jax.experimental.pallas import tpu as pltpu
from jax.sharding import PartitionSpec as P

KAPPA_H = 12.0


def phase_tables(polar_total, azimuth_total):
    polar = (jnp.arange(polar_total, dtype=jnp.int32).astype(jnp.float32) + 0.5) * (
        math.pi / polar_total
    )
    azimuth = jnp.arange(azimuth_total, dtype=jnp.int32).astype(jnp.float32) * (
        2.0 * math.pi / azimuth_total
    )
    octant = jnp.arange(4, dtype=jnp.int32)
    sign_x = ((octant & 1) * 2 - 1).astype(jnp.float32)[:, None, None]
    sign_y = ((octant >> 1 & 1) * 2 - 1).astype(jnp.float32)[:, None, None]
    along_x = jnp.sin(polar)[:, None] * jnp.cos(azimuth)[None, :]
    along_y = jnp.sin(polar)[:, None] * jnp.sin(azimuth)[None, :]
    along_z = jnp.cos(polar)[:, None] + jnp.zeros((1, azimuth_total), jnp.float32)
    phase = KAPPA_H * (sign_x * along_x + sign_y * along_y - along_z)
    return jnp.cos(phase), jnp.sin(phase)


def aggregate_kernel(x_ref, theta_ref, phi_ref, cos_ref, sin_ref, out_ref, mid_ref, raised_ref):
    theta = theta_ref[...]
    phi = phi_ref[...]
    polar_total = theta.shape[0]
    slabs, parents = out_ref.shape[0], out_ref.shape[1]
    for p in range(parents):
        for o in range(8):
            for r in range(2):
                x = x_ref[:, p * 8 + o, r].reshape(theta.shape[1], phi.shape[0])
                mid = jnp.dot(theta, x, preferred_element_type=jnp.float32)
                k = o * 2 + r
                mid_ref[k * polar_total : (k + 1) * polar_total, :] = mid.astype(jnp.bfloat16)
        raised_ref[...] = jnp.dot(mid_ref[...], phi, preferred_element_type=jnp.float32).reshape(
            raised_ref.shape
        )

        def slab(s, carry):
            rows = pl.ds(pl.multiple_of(s * 8, 8), 8)
            real = imag = None
            for o in range(4):
                c = cos_ref[o, rows, :]
                d = sin_ref[o, rows, :]
                ar, ai = raised_ref[2 * o, rows, :], raised_ref[2 * o + 1, rows, :]
                br, bi = raised_ref[14 - 2 * o, rows, :], raised_ref[15 - 2 * o, rows, :]
                tr = c * (ar + br) - d * (ai - bi)
                ti = d * (ar - br) + c * (ai + bi)
                real = tr if real is None else real + tr
                imag = ti if imag is None else imag + ti
            for r, v in ((0, real), (1, imag)):
                both = jnp.concatenate([v[:, :128], v[:, 128:]], axis=0)
                out_ref[s, p, r] = both.astype(jnp.bfloat16)
            return carry

        lax.fori_loop(0, slabs, slab, 0)


def translate_kernel(slots_ref, kinds_ref, pool_ref, trans_ref, out_ref):
    boxes, entries = out_ref.shape[0], slots_ref.shape[1]

    def box(b, carry):
        def quad(q, acc):
            real, imag = acc
            fr = fi = None
            for j in range(4):
                code = slots_ref[b, q * 4 + j]
                kind = kinds_ref[b, q * 4 + j]
                sr, si = pool_ref[code, 0], pool_ref[code, 1]
                tr, ti = trans_ref[kind, 0], trans_ref[kind, 1]
                er = tr * sr - ti * si
                ei = tr * si + ti * sr
                if j % 2 == 0:
                    fr, fi = er, ei
                else:
                    real = real + (fr + er).astype(jnp.float32)
                    imag = imag + (fi + ei).astype(jnp.float32)
            return real, imag

        zero = jnp.zeros((16, 128), jnp.float32)
        real, imag = lax.fori_loop(0, entries // 4, quad, (zero, zero), unroll=4)
        for r, v in ((0, real), (1, imag)):
            out_ref[b, r, :, 0:128] = v[0:8]
            out_ref[b, r, :, 128:256] = v[8:16]
        return carry

    lax.fori_loop(0, boxes, box, 0)


VMEM = pl.BlockSpec(memory_space=pltpu.VMEM)
SMEM = pl.BlockSpec(memory_space=pltpu.SMEM)


def local(children, interp_theta, interp_phi, translator, send_index, list_slots, list_kinds):
    samp_count = lax.axis_size("samp")
    polar_total = interp_theta.shape[1]
    azimuth_total = interp_phi.shape[1]
    child_boxes, _, rows, child_azimuth = children.shape
    own_children = child_boxes // samp_count
    own_parents = own_children // 8
    parent_boxes = child_boxes // 8
    out_rows = polar_total // samp_count

    x = children.reshape(samp_count, own_children, 2, rows, child_azimuth)
    x = lax.all_to_all(x, "samp", split_axis=0, concat_axis=0, tiled=True)
    cosine, sine = phase_tables(polar_total, azimuth_total)
    mine = pl.pallas_call(
        aggregate_kernel,
        out_shape=jax.ShapeDtypeStruct(
            (samp_count, own_parents, 2, 2 * out_rows, azimuth_total // 2), jnp.bfloat16
        ),
        in_specs=[VMEM] * 5,
        out_specs=VMEM,
        scratch_shapes=[
            pltpu.VMEM((16 * polar_total, child_azimuth), jnp.bfloat16),
            pltpu.VMEM((16, polar_total, azimuth_total), jnp.float32),
        ],
        compiler_params=pltpu.CompilerParams(vmem_limit_bytes=16 << 20),
        name="aggregate",
    )(x, interp_theta.T, interp_phi, cosine, sine)
    mine = lax.all_to_all(mine, "samp", split_axis=0, concat_axis=0, tiled=True)
    mine = mine.reshape(parent_boxes, 2, 2 * out_rows, azimuth_total // 2)
    parents = (
        mine.reshape(parent_boxes, 2, 2, out_rows, azimuth_total // 2)
        .transpose(0, 1, 3, 2, 4)
        .reshape(parent_boxes, 2, out_rows, azimuth_total)
    )

    outgoing = mine[send_index[0].reshape(-1)]
    outgoing = outgoing.reshape(send_index.shape[1], send_index.shape[2], *mine.shape[1:])
    received = lax.all_to_all(outgoing, "box", split_axis=0, concat_axis=0, tiled=True)
    pool = received.reshape(-1, *mine.shape[1:])
    trans = (
        translator.reshape(-1, 2, out_rows, 2, azimuth_total // 2)
        .transpose(0, 1, 3, 2, 4)
        .reshape(-1, 2, 2 * out_rows, azimuth_total // 2)
    )
    field = pl.pallas_call(
        translate_kernel,
        out_shape=jax.ShapeDtypeStruct((parent_boxes, 2, out_rows, azimuth_total), jnp.float32),
        in_specs=[SMEM, SMEM, VMEM, VMEM],
        out_specs=VMEM,
        compiler_params=pltpu.CompilerParams(vmem_limit_bytes=16 << 20),
        name="translate",
    )(list_slots, list_kinds, pool, trans)
    return parents, field


def solution(mesh):
    return jax.shard_map(
        local,
        mesh=mesh,
        in_specs=(
            P("box", None, "samp", None),
            P(),
            P(),
            P(None, None, "samp", None),
            P("box", None, None),
            P("box", None),
            P("box", None),
        ),
        out_specs=(P("box", None, "samp", None), P("box", None, "samp", None)),
        check_vma=False,
    )
```

```python
import functools
import math

import jax
import jax.numpy as jnp
from jax import lax
from jax.experimental import pallas as pl
from jax.experimental.pallas import tpu as pltpu
from jax.sharding import Mesh, PartitionSpec as P

KAPPA_H = 12.0
SAMP = ("x", "z")
BOX = ("y", "c")
STEP = 4
WIDTH = 128
POOL_BLOCKS = (2, 4, 2)
VMEM = pl.BlockSpec(memory_space=pltpu.VMEM)
SMEM = pl.BlockSpec(memory_space=pltpu.SMEM)


def phase_tables(polar_total, azimuth_total):
    polar = (jnp.arange(polar_total, dtype=jnp.int32).astype(jnp.float32) + 0.5) * (
        math.pi / polar_total
    )
    azimuth = jnp.arange(azimuth_total, dtype=jnp.int32).astype(jnp.float32) * (
        2.0 * math.pi / azimuth_total
    )
    octant = jnp.arange(4, dtype=jnp.int32)
    sign_x = ((octant & 1) * 2 - 1).astype(jnp.float32)[:, None, None]
    sign_y = ((octant >> 1 & 1) * 2 - 1).astype(jnp.float32)[:, None, None]
    along_x = jnp.sin(polar)[:, None] * jnp.cos(azimuth)[None, :]
    along_y = jnp.sin(polar)[:, None] * jnp.sin(azimuth)[None, :]
    along_z = jnp.cos(polar)[:, None] + jnp.zeros((1, azimuth_total), jnp.float32)
    phase = KAPPA_H * (sign_x * along_x + sign_y * along_y - along_z)
    return jnp.cos(phase), jnp.sin(phase)


def aggregate_kernel(x_ref, theta_ref, phi_ref, cos_ref, sin_ref, out_ref, mid_ref, raised_ref):
    theta = theta_ref[...]
    phi = phi_ref[...]
    polar_total = theta.shape[0]
    for p in range(out_ref.shape[1]):
        for o in range(8):
            for r in range(2):
                x = x_ref[:, p * 8 + o, r].reshape(theta.shape[1], phi.shape[0])
                mid = jnp.dot(theta, x, preferred_element_type=jnp.float32)
                k = o * 2 + r
                mid_ref[k * polar_total : (k + 1) * polar_total, :] = mid.astype(jnp.bfloat16)
        raised_ref[...] = jnp.dot(mid_ref[...], phi, preferred_element_type=jnp.float32).reshape(
            raised_ref.shape
        )

        def slab(s, carry):
            rows = pl.ds(pl.multiple_of(s * 8, 8), 8)
            real = imag = None
            for o in range(4):
                c = cos_ref[o, rows, :]
                d = sin_ref[o, rows, :]
                ar, ai = raised_ref[2 * o, rows, :], raised_ref[2 * o + 1, rows, :]
                br, bi = raised_ref[14 - 2 * o, rows, :], raised_ref[15 - 2 * o, rows, :]
                tr = c * (ar + br) - d * (ai - bi)
                ti = d * (ar - br) + c * (ai + bi)
                real = tr if real is None else real + tr
                imag = ti if imag is None else imag + ti
            out_ref[s, p, 0] = real.astype(jnp.bfloat16)
            out_ref[s, p, 1] = imag.astype(jnp.bfloat16)
            return carry

        lax.fori_loop(0, out_ref.shape[0], slab, 0)


def widen_kernel(x_ref, out_ref, buffer, sems):
    parts = sems.shape[0]
    size = x_ref.shape[0] // parts

    def copy(i):
        at = pl.ds(i * size, size)
        return pltpu.make_async_copy(x_ref.at[at], buffer.at[at], sems.at[i])

    for i in range(parts):
        copy(i).start()
    for i in range(parts):
        copy(i).wait()

        def widen(k, carry):
            out_ref[k] = buffer[k].astype(jnp.float32)
            return carry

        lax.fori_loop(i * size, (i + 1) * size, widen, 0)


def translate_kernel(k, at_ref, kind_ref, bound_ref, trans_ref, *refs):
    first = k == 0
    if first:
        *blocks, out_ref, parents_ref, pool_ref, sem = refs
        copy = pltpu.make_async_copy(blocks[0], parents_ref, sem)
        copy.start()
    else:
        sum_ref, *blocks, out_ref, pool_ref = refs
    start = 0
    for block in blocks:

        def widen(i, carry, block=block, start=start):
            pool_ref[start + i] = block[i].astype(jnp.float32)
            return carry

        lax.fori_loop(0, block.shape[0], widen, 0, unroll=4)
        start += block.shape[0]
    pool_ref[start] = jnp.zeros(pool_ref.shape[1:], jnp.float32)

    def box(b, carry):
        def group(g, acc):
            real, imag = acc
            for j in range(STEP):
                at, kind = at_ref[g * STEP + j], kind_ref[g * STEP + j]
                sr, si = pool_ref[at, 0], pool_ref[at, 1]
                tr, ti = trans_ref[kind, 0], trans_ref[kind, 1]
                real = real + (tr * sr - ti * si)
                imag = imag + (tr * si + ti * sr)
            return real, imag

        if first:
            zero = jnp.zeros(out_ref.shape[2:], jnp.float32)
            acc = (zero, zero)
        else:
            acc = (sum_ref[b, 0], sum_ref[b, 1])
        real, imag = lax.fori_loop(bound_ref[b, 2 * k], bound_ref[b, 2 * k + 1], group, acc)
        out_ref[b, 0] = real
        out_ref[b, 1] = imag
        return carry

    lax.fori_loop(0, out_ref.shape[0], box, 0)
    if first:
        copy.wait()


def shift(x, axis, step):
    size = lax.axis_size(axis)
    return lax.ppermute(x, axis, [(i, (i + step) % size) for i in range(size)])


def plan_kernel(place_ref, own_ref, after_ref, far_ref, before_ref, slots_ref, kinds_ref, *outs):
    at_ref, kind_ref, bound_ref = outs
    y, c = place_ref[0], place_ref[1]
    cores, receivers, cap = own_ref.shape
    local_boxes = slots_ref.shape[0]
    me = y * cores + c
    slots = slots_ref[...]
    sender = lax.shift_right_logical(slots, 4)
    dy = (lax.shift_right_logical(sender, 1) - y) & 3
    dc = (sender & 1) ^ c
    code = (dy * cores + dc) * cap + (slots & (cap - 1))
    row = jnp.zeros_like(slots)
    tables = (own_ref, after_ref, far_ref, before_ref)
    for k, table in enumerate(tables):
        side = cores if k == 3 else 0
        for core in range(cores):
            for u in range(cap):
                value = table[core, me, u] + (side + core) * local_boxes
                row = jnp.where(code == (k * cores + core) * cap + u, value, row)
    entries = slots.shape[1]
    klass = jnp.where(dy == 0, 0, jnp.where(dy == 2, 2, 1))
    first = lax.broadcasted_iota(jnp.int32, (entries, entries), 0)
    second = lax.broadcasted_iota(jnp.int32, (entries, entries), 1)
    ahead = (first < second).astype(jnp.float32)
    lane = lax.broadcasted_iota(jnp.int32, (local_boxes, WIDTH), 1)
    begin = jnp.zeros((local_boxes, 1), jnp.int32)
    spot = jnp.zeros_like(slots)
    fill = jnp.zeros((local_boxes, WIDTH), jnp.int32)
    line = lax.broadcasted_iota(jnp.int32, (local_boxes, WIDTH), 0) * (WIDTH // STEP)
    bound = line
    for k, rows in enumerate(POOL_BLOCKS):
        mine = klass == k
        ones = mine.astype(jnp.float32)
        inside = jnp.dot(ones, ahead, preferred_element_type=jnp.float32).astype(jnp.int32)
        count = jnp.sum(mine.astype(jnp.int32), axis=1, keepdims=True)
        spot = jnp.where(mine, begin + inside, spot)
        end = begin + ((count + STEP - 1) & -STEP)
        fill = jnp.where((lane >= begin) & (lane < end), rows * local_boxes, fill)
        bound = bound + jnp.where(lane == 2 * k, lax.shift_right_logical(begin, 2), 0)
        bound = bound + jnp.where(lane == 2 * k + 1, lax.shift_right_logical(end, 2), 0)
        begin = end
    bound_ref[...] = bound
    value = (row * 512 + kinds_ref[...] + 1).astype(jnp.float32)
    value = jnp.transpose(value).astype(jnp.int32)
    spot = jnp.transpose(spot.astype(jnp.float32)).astype(jnp.int32)
    wide_lane = lax.broadcasted_iota(jnp.int32, (entries, WIDTH), 1)
    lines = []
    for b in range(local_boxes):
        hit = spot[:, b : b + 1] == wide_lane
        got = jnp.where(hit, value[:, b : b + 1], 0)
        lines.append(jnp.sum(got, axis=0, keepdims=True))
    packed = jnp.concatenate(lines, axis=0)
    packed = jnp.where(packed == 0, fill * 512, packed - 1)
    at_ref[...] = lax.shift_right_logical(packed, 9)
    kind_ref[...] = packed & 511


def slot_tables(send_index):
    own = jnp.concatenate([send_index, shift(send_index, "c", 1)], axis=0)
    return own, shift(own, "y", -1), shift(own, "y", 2), shift(own, "y", 1)


def plan_lists(tables, list_slots, list_kinds):
    place = jnp.stack([lax.axis_index("y"), lax.axis_index("c")]).astype(jnp.int32)
    shape = jax.ShapeDtypeStruct((list_slots.shape[0], WIDTH), jnp.int32)
    at, kind, bound = pl.pallas_call(
        plan_kernel,
        out_shape=[shape] * 3,
        in_specs=[SMEM] * 5 + [VMEM] * 2,
        out_specs=[VMEM] * 3,
        compiler_params=pltpu.CompilerParams(vmem_limit_bytes=4 << 20),
        cost_estimate=pl.CostEstimate(flops=1 << 20, bytes_accessed=1 << 20, transcendentals=0),
        name="plan",
    )(place, *tables, list_slots, list_kinds)
    return at.reshape(-1), kind.reshape(-1), bound


def local(children, interp_theta, interp_phi, translator, send_index, list_slots, list_kinds):
    samp_count = lax.axis_size(SAMP)
    polar_total = interp_theta.shape[1]
    azimuth_total = interp_phi.shape[1]
    child_boxes, _, rows, child_azimuth = children.shape
    own_children = child_boxes // samp_count
    parent_boxes = child_boxes // 8
    out_rows = polar_total // samp_count
    pattern = (2, out_rows, azimuth_total)
    half = parent_boxes // 2

    x = children.reshape(samp_count, own_children, 2, rows, child_azimuth)
    x = lax.all_to_all(x, SAMP, split_axis=0, concat_axis=0, tiled=True)

    cosine, sine = phase_tables(polar_total, azimuth_total)
    theta = interp_theta.T
    tables = slot_tables(send_index)
    x, *tables = lax.optimization_barrier((x, *tables))
    mine = pl.pallas_call(
        aggregate_kernel,
        out_shape=jax.ShapeDtypeStruct((samp_count, own_children // 8) + pattern, jnp.bfloat16),
        in_specs=[VMEM] * 5,
        out_specs=VMEM,
        scratch_shapes=[
            pltpu.VMEM((16 * polar_total, child_azimuth), jnp.bfloat16),
            pltpu.VMEM((16, polar_total, azimuth_total), jnp.float32),
        ],
        compiler_params=pltpu.CompilerParams(vmem_limit_bytes=12 << 20),
        cost_estimate=pl.CostEstimate(flops=335 << 20, bytes_accessed=4 << 20, transcendentals=0),
        name="aggregate",
    )(x, theta, interp_phi, cosine, sine)
    mine = lax.all_to_all(mine, SAMP, split_axis=0, concat_axis=0, tiled=True)
    at, kind, bound = plan_lists(tables, list_slots, list_kinds)
    mine, at, kind, bound = lax.optimization_barrier((mine, at, kind, bound))
    own = mine.reshape((parent_boxes,) + pattern)
    after = shift(own, "y", -1)
    before = shift(own, "y", 1)
    other = shift(own, "c", 1)
    source, own = lax.optimization_barrier((translator, own))
    wide = pl.pallas_call(
        widen_kernel,
        out_shape=pltpu.VMEM(translator.shape, jnp.float32),
        in_specs=[pl.BlockSpec(memory_space=pltpu.HBM)],
        out_specs=VMEM,
        scratch_shapes=[
            pltpu.VMEM(translator.shape, jnp.bfloat16),
            pltpu.SemaphoreType.DMA((4,)),
        ],
        compiler_params=pltpu.CompilerParams(vmem_limit_bytes=56 << 20),
        cost_estimate=pl.CostEstimate(flops=4 << 20, bytes_accessed=8 << 20, transcendentals=0),
        name="widen",
    )(source)

    def translate(k, blocks, so_far):
        shape = (parent_boxes,) + pattern
        out = [(pltpu.VMEM if k < 2 else jax.ShapeDtypeStruct)(shape, jnp.float32)]
        specs = [VMEM]
        scratch = [pltpu.VMEM((POOL_BLOCKS[k] * parent_boxes + 1,) + pattern, jnp.float32)]
        if k == 0:
            out.append(jax.ShapeDtypeStruct(shape, jnp.bfloat16))
            specs.append(pl.BlockSpec(memory_space=pltpu.HBM))
            scratch.append(pltpu.SemaphoreType.DMA)
        return pl.pallas_call(
            functools.partial(translate_kernel, k),
            out_shape=out,
            in_specs=[SMEM] * 3 + [VMEM] * (1 + len(so_far) + len(blocks)),
            out_specs=specs,
            scratch_shapes=scratch,
            compiler_params=pltpu.CompilerParams(vmem_limit_bytes=8 << 20),
            cost_estimate=pl.CostEstimate(
                flops=16 << 20, bytes_accessed=8 << 20, transcendentals=0
            ),
            name=f"translate_{k}",
        )(at, kind, bound, wide, *so_far, *blocks)

    field, parents = translate(0, [own, other], [])
    after, before, field = lax.optimization_barrier((after, before, field))
    far = [shift(before[:half], "y", 1), shift(after[half:], "y", -1)]
    near = [after, shift(after, "c", 1), before, shift(before, "c", 1)]
    (field,) = translate(1, near, [field])
    *far, field = lax.optimization_barrier((*far, field))
    across = [shift(v, "c", 1) for v in far]
    (field,) = translate(2, far + across, [field])
    return parents, field


def solution(mesh):
    y_count, x_count = 4, 4
    fine = Mesh(
        mesh.devices.reshape(y_count, mesh.shape["box"] // y_count, x_count, -1),
        BOX + SAMP,
    )
    return jax.shard_map(
        local,
        mesh=fine,
        in_specs=(
            P(BOX, None, SAMP, None),
            P(),
            P(),
            P(None, None, SAMP, None),
            P(BOX, None, None),
            P(BOX, None),
            P(BOX, None),
        ),
        out_specs=(P(BOX, None, SAMP, None), P(BOX, None, SAMP, None)),
        check_vma=False,
    )
```

```python
import functools
import math

import jax
import jax.numpy as jnp
from jax import lax
from jax.experimental import pallas as pl
from jax.experimental.pallas import tpu as pltpu
from jax.sharding import Mesh, PartitionSpec as P


KAPPA_H = 12.0
SAMP = ("x", "z")
BOX = ("y", "c")
STEP = 4
WIDTH = 128
POOL_BLOCKS = (2, 2, 2, 1, 1)
VMEM = pl.BlockSpec(memory_space=pltpu.VMEM)
SMEM = pl.BlockSpec(memory_space=pltpu.SMEM)
HBM = pl.BlockSpec(memory_space=pltpu.HBM)


def phase_tables(polar_total, azimuth_total):
    polar = (jnp.arange(polar_total, dtype=jnp.int32).astype(jnp.float32) + 0.5) * (
        math.pi / polar_total
    )
    azimuth = jnp.arange(azimuth_total, dtype=jnp.int32).astype(jnp.float32) * (
        2.0 * math.pi / azimuth_total
    )
    octant = jnp.arange(4, dtype=jnp.int32)
    sign_x = ((octant & 1) * 2 - 1).astype(jnp.float32)[:, None, None]
    sign_y = ((octant >> 1 & 1) * 2 - 1).astype(jnp.float32)[:, None, None]
    along_x = jnp.sin(polar)[:, None] * jnp.cos(azimuth)[None, :]
    along_y = jnp.sin(polar)[:, None] * jnp.sin(azimuth)[None, :]
    along_z = jnp.cos(polar)[:, None] + jnp.zeros((1, azimuth_total), jnp.float32)
    phase = KAPPA_H * (sign_x * along_x + sign_y * along_y - along_z)
    return jnp.cos(phase), jnp.sin(phase)


def prepare_kernel(theta_ref, phi_ref, turned_ref, copy_ref):
    turned_ref[...] = jnp.transpose(theta_ref[...].astype(jnp.float32)).astype(jnp.bfloat16)
    copy_ref[...] = phi_ref[...]


def aggregate_kernel(x_ref, theta_ref, phi_ref, cos_ref, sin_ref, out_ref, mid_ref, raised_ref):
    theta = theta_ref[...]
    polar_total = theta.shape[0]
    for p in range(out_ref.shape[1]):
        for o in range(8):
            for r in range(2):
                x = x_ref[:, p * 8 + o, r].reshape(theta.shape[1], phi_ref.shape[0])
                mid = jnp.dot(theta, x, preferred_element_type=jnp.float32)
                k = o * 2 + r
                mid_ref[k * polar_total : (k + 1) * polar_total, :] = mid.astype(jnp.bfloat16)
        raised_ref[...] = jnp.dot(mid_ref[...], phi_ref[...], preferred_element_type=jnp.float32).reshape(
            raised_ref.shape
        )

        def slab(s, carry):
            rows = pl.ds(pl.multiple_of(s * 8, 8), 8)
            real = imag = None
            for o in range(4):
                c = cos_ref[o, rows, :]
                d = sin_ref[o, rows, :]
                ar, ai = raised_ref[2 * o, rows, :], raised_ref[2 * o + 1, rows, :]
                br, bi = raised_ref[14 - 2 * o, rows, :], raised_ref[15 - 2 * o, rows, :]
                tr = c * (ar + br) - d * (ai - bi)
                ti = d * (ar - br) + c * (ai + bi)
                real = tr if real is None else real + tr
                imag = ti if imag is None else imag + ti
            out_ref[s, p, 0] = real.astype(jnp.bfloat16)
            out_ref[s, p, 1] = imag.astype(jnp.bfloat16)
            return carry

        lax.fori_loop(0, out_ref.shape[0], slab, 0)


def widen_kernel(x_ref, out_ref, buffer, sems):
    parts = sems.shape[0]
    size = x_ref.shape[0] // parts

    def copy(i):
        at = pl.ds(i * size, size)
        return pltpu.make_async_copy(x_ref.at[at], buffer.at[at], sems.at[i])

    for i in range(parts):
        copy(i).start()
    for i in range(parts):
        copy(i).wait()

        def widen(k, carry):
            out_ref[k] = buffer[k].astype(jnp.float32)
            return carry

        lax.fori_loop(i * size, (i + 1) * size, widen, 0)


def translate_kernel(k, at_ref, kind_ref, bound_ref, trans_ref, *refs):
    first, last = k == 0, k == len(POOL_BLOCKS) - 1
    if first:
        *blocks, out_ref, parents_ref, pool_ref, sem = refs
        copy = pltpu.make_async_copy(blocks[0], parents_ref, sem)
        copy.start()
    elif last:
        sum_ref, *blocks, final_ref, pool_ref, out_ref, sems = refs
    else:
        sum_ref, *blocks, out_ref, pool_ref = refs
    start = 0
    for block in blocks:

        def widen(i, carry, block=block, start=start):
            pool_ref[start + i] = block[i].astype(jnp.float32)
            return carry

        lax.fori_loop(0, block.shape[0], widen, 0, unroll=4)
        start += block.shape[0]
    pool_ref[start] = jnp.zeros(pool_ref.shape[1:], jnp.float32)

    def entries(g):
        spots = [g * STEP + j for j in range(STEP)]
        return tuple(at_ref[i] for i in spots) + tuple(kind_ref[i] for i in spots)

    def box(b, carry):
        def group(g, acc):
            real, imag, now = acc
            later = entries(g + 1)
            for j in range(STEP):
                at, kind = now[j], now[STEP + j]
                sr, si = pool_ref[at, 0], pool_ref[at, 1]
                tr, ti = trans_ref[kind, 0], trans_ref[kind, 1]
                real = real + (tr * sr - ti * si)
                imag = imag + (tr * si + ti * sr)
            return real, imag, later

        if first:
            zero = jnp.zeros(out_ref.shape[2:], jnp.float32)
            acc = (zero, zero)
        else:
            acc = (sum_ref[b, 0], sum_ref[b, 1])
        begin, end = bound_ref[b, 2 * k], bound_ref[b, 2 * k + 1]
        real, imag, _ = lax.fori_loop(begin, end, group, acc + (entries(begin),))
        out_ref[b, 0] = real
        out_ref[b, 1] = imag
        return carry

    boxes = out_ref.shape[0]
    if not last:
        lax.fori_loop(0, boxes, box, 0)
    else:
        parts = sems.shape[0]
        size = boxes // parts
        copies = []
        for i in range(parts):
            lax.fori_loop(i * size, (i + 1) * size, box, 0)
            rows = pl.ds(i * size, size)
            out = pltpu.make_async_copy(out_ref.at[rows], final_ref.at[rows], sems.at[i])
            out.start()
            copies.append(out)
        for out in copies:
            out.wait()
    if first:
        copy.wait()


def shift(x, axis, step):
    size = lax.axis_size(axis)
    return lax.ppermute(x, axis, [(i, (i + step) % size) for i in range(size)])


def plan_kernel(place_ref, own_ref, after_ref, far_ref, before_ref, slots_ref, kinds_ref, *outs):
    at_ref, kind_ref, bound_ref = outs
    y, c = place_ref[0], place_ref[1]
    cores, _, cap = own_ref.shape
    local_boxes = slots_ref.shape[0]
    me = y * cores + c
    slots = slots_ref[...]
    sender = lax.shift_right_logical(slots, 4)
    dy = (lax.shift_right_logical(sender, 1) - y) & 3
    dc = (sender & 1) ^ c
    code = (dy * cores + dc) * cap + (slots & (cap - 1))
    row = jnp.zeros_like(slots)
    tables = (own_ref, after_ref, far_ref, before_ref)
    for k, table in enumerate(tables):
        for core in range(cores):
            side = core if k == 0 else int(k == 3)
            for u in range(cap):
                value = table[core, me, u] + side * local_boxes
                row = jnp.where(code == (k * cores + core) * cap + u, value, row)
    entries = slots.shape[1]
    klass = jnp.where(dy == 0, 0, jnp.where(dy == 2, 3, 1) + dc)
    first = lax.broadcasted_iota(jnp.int32, (entries, entries), 0)
    second = lax.broadcasted_iota(jnp.int32, (entries, entries), 1)
    ahead = (first < second).astype(jnp.float32)
    lane = lax.broadcasted_iota(jnp.int32, (local_boxes, WIDTH), 1)
    begin = jnp.zeros((local_boxes, 1), jnp.int32)
    spot = jnp.zeros_like(slots)
    fill = jnp.zeros((local_boxes, WIDTH), jnp.int32)
    line = lax.broadcasted_iota(jnp.int32, (local_boxes, WIDTH), 0) * (WIDTH // STEP)
    bound = line
    for k, rows in enumerate(POOL_BLOCKS):
        mine = klass == k
        ones = mine.astype(jnp.float32)
        inside = jnp.dot(ones, ahead, preferred_element_type=jnp.float32).astype(jnp.int32)
        count = jnp.sum(mine.astype(jnp.int32), axis=1, keepdims=True)
        spot = jnp.where(mine, begin + inside, spot)
        end = begin + ((count + STEP - 1) & -STEP)
        fill = jnp.where((lane >= begin) & (lane < end), rows * local_boxes, fill)
        bound = bound + jnp.where(lane == 2 * k, lax.shift_right_logical(begin, 2), 0)
        bound = bound + jnp.where(lane == 2 * k + 1, lax.shift_right_logical(end, 2), 0)
        begin = end
    bound_ref[...] = bound
    value = (row * 512 + kinds_ref[...] + 1).astype(jnp.float32)
    value = jnp.transpose(value).astype(jnp.int32)
    spot = jnp.transpose(spot.astype(jnp.float32)).astype(jnp.int32)
    wide_lane = lax.broadcasted_iota(jnp.int32, (entries, WIDTH), 1)
    lines = []
    for b in range(local_boxes):
        hit = spot[:, b : b + 1] == wide_lane
        got = jnp.where(hit, value[:, b : b + 1], 0)
        lines.append(jnp.sum(got, axis=0, keepdims=True))
    packed = jnp.concatenate(lines, axis=0)
    packed = jnp.where(packed == 0, fill * 512, packed - 1)
    at_ref[...] = lax.shift_right_logical(packed, 9)
    kind_ref[...] = packed & 511


def slot_tables(send_index):
    own = jnp.concatenate([send_index, shift(send_index, "c", 1)], axis=0)
    return own, shift(own, "y", -1), shift(own, "y", 2), shift(own, "y", 1)


def plan_lists(tables, list_slots, list_kinds):
    place = jnp.stack([lax.axis_index("y"), lax.axis_index("c")]).astype(jnp.int32)
    shape = jax.ShapeDtypeStruct((list_slots.shape[0], WIDTH), jnp.int32)
    at, kind, bound = pl.pallas_call(
        plan_kernel,
        out_shape=[shape] * 3,
        in_specs=[SMEM] * 5 + [VMEM] * 2,
        out_specs=[VMEM] * 3,
        compiler_params=pltpu.CompilerParams(vmem_limit_bytes=4 << 20),
        cost_estimate=pl.CostEstimate(flops=1 << 20, bytes_accessed=1 << 20, transcendentals=0),
        name="plan",
    )(place, *tables, list_slots, list_kinds)
    return at.reshape(-1), kind.reshape(-1), bound


def local(children, interp_theta, interp_phi, translator, send_index, list_slots, list_kinds):
    samp_count = lax.axis_size(SAMP)
    polar_total = interp_theta.shape[1]
    azimuth_total = interp_phi.shape[1]
    child_boxes, _, rows, child_azimuth = children.shape
    own_children = child_boxes // samp_count
    parent_boxes = child_boxes // 8
    out_rows = polar_total // samp_count
    pattern = (2, out_rows, azimuth_total)

    x = children.reshape(samp_count, own_children, 2, rows, child_azimuth)
    x = lax.all_to_all(x, SAMP, split_axis=0, concat_axis=0, tiled=True)

    cosine, sine = phase_tables(polar_total, azimuth_total)
    theta, phi = pl.pallas_call(
        prepare_kernel,
        out_shape=[
            pltpu.VMEM(interp_theta.shape[::-1], jnp.bfloat16),
            pltpu.VMEM(interp_phi.shape, jnp.bfloat16),
        ],
        in_specs=[VMEM] * 2,
        out_specs=[VMEM] * 2,
        compiler_params=pltpu.CompilerParams(vmem_limit_bytes=4 << 20),
        cost_estimate=pl.CostEstimate(flops=1 << 20, bytes_accessed=1 << 18, transcendentals=0),
        name="prepare",
    )(interp_theta, interp_phi)
    tables = slot_tables(send_index)
    x, theta, phi, *tables = lax.optimization_barrier((x, theta, phi, *tables))
    mine = pl.pallas_call(
        aggregate_kernel,
        out_shape=jax.ShapeDtypeStruct((samp_count, own_children // 8) + pattern, jnp.bfloat16),
        in_specs=[VMEM] * 5,
        out_specs=VMEM,
        scratch_shapes=[
            pltpu.VMEM((16 * polar_total, child_azimuth), jnp.bfloat16),
            pltpu.VMEM((16, polar_total, azimuth_total), jnp.float32),
        ],
        compiler_params=pltpu.CompilerParams(vmem_limit_bytes=12 << 20),
        cost_estimate=pl.CostEstimate(flops=335 << 20, bytes_accessed=4 << 20, transcendentals=0),
        name="aggregate",
    )(x, theta, phi, cosine, sine)
    mine = lax.all_to_all(mine, SAMP, split_axis=0, concat_axis=0, tiled=True)
    at, kind, bound = plan_lists(tables, list_slots, list_kinds)
    mine, at, kind, bound = lax.optimization_barrier((mine, at, kind, bound))
    own = mine.reshape((parent_boxes,) + pattern)
    after = shift(own, "y", -1)
    before = shift(own, "y", 1)
    far = shift(own, "y", 2)
    other = shift(own, "c", 1)
    source, own = lax.optimization_barrier((translator, own))
    wide = pl.pallas_call(
        widen_kernel,
        out_shape=pltpu.VMEM(translator.shape, jnp.float32),
        in_specs=[HBM],
        out_specs=VMEM,
        scratch_shapes=[
            pltpu.VMEM(translator.shape, jnp.bfloat16),
            pltpu.SemaphoreType.DMA((4,)),
        ],
        compiler_params=pltpu.CompilerParams(vmem_limit_bytes=56 << 20),
        cost_estimate=pl.CostEstimate(flops=4 << 20, bytes_accessed=8 << 20, transcendentals=0),
        name="widen",
    )(source)

    def translate(k, blocks, so_far):
        first, last = k == 0, k == len(POOL_BLOCKS) - 1
        shape = (parent_boxes,) + pattern
        out = [(jax.ShapeDtypeStruct if last else pltpu.VMEM)(shape, jnp.float32)]
        specs = [HBM if last else VMEM]
        scratch = [pltpu.VMEM((POOL_BLOCKS[k] * parent_boxes + 1,) + pattern, jnp.float32)]
        if first:
            out.append(jax.ShapeDtypeStruct(shape, jnp.bfloat16))
            specs.append(HBM)
            scratch.append(pltpu.SemaphoreType.DMA)
        if last:
            scratch += [pltpu.VMEM(shape, jnp.float32), pltpu.SemaphoreType.DMA((4,))]
        return pl.pallas_call(
            functools.partial(translate_kernel, k),
            out_shape=out,
            in_specs=[SMEM] * 3 + [VMEM] * (1 + len(so_far) + len(blocks)),
            out_specs=specs,
            scratch_shapes=scratch,
            compiler_params=pltpu.CompilerParams(vmem_limit_bytes=8 << 20),
            cost_estimate=pl.CostEstimate(
                flops=16 << 20, bytes_accessed=8 << 20, transcendentals=0
            ),
        )(at, kind, bound, wide, *so_far, *blocks)

    field, parents = translate(0, [own, other], [])
    after, before, field = lax.optimization_barrier((after, before, field))
    across = [shift(after, "c", 1), shift(before, "c", 1)]
    (field,) = translate(1, [after, before], [field])
    (field,) = translate(2, across, [field])
    far, field = lax.optimization_barrier((far, field))
    across = shift(far, "c", 1)
    (field,) = translate(3, [far], [field])
    (field,) = translate(4, [across], [field])
    return parents, field


def solution(mesh):
    y_count, x_count = 4, 4
    fine = Mesh(
        mesh.devices.reshape(y_count, mesh.shape["box"] // y_count, x_count, -1),
        BOX + SAMP,
    )
    return jax.shard_map(
        local,
        mesh=fine,
        in_specs=(
            P(BOX, None, SAMP, None),
            P(),
            P(),
            P(None, None, SAMP, None),
            P(BOX, None, None),
            P(BOX, None),
            P(BOX, None),
        ),
        out_specs=(P(BOX, None, SAMP, None), P(BOX, None, SAMP, None)),
        check_vma=False,
    )
```

```python
import math

import jax
import jax.numpy as jnp
from jax import lax
from jax.experimental import pallas as pl
from jax.experimental.pallas import tpu as pltpu
from jax.sharding import Mesh, PartitionSpec as P


KAPPA_H = 12.0
SAMP = ("x", "z")
BOX = ("y", "c")
WIDTH = 128
EARLY = 40
VMEM = pl.BlockSpec(memory_space=pltpu.VMEM)
SMEM = pl.BlockSpec(memory_space=pltpu.SMEM)
HBM = pl.BlockSpec(memory_space=pltpu.HBM)


def phase_tables(polar_total, azimuth_total):
    polar = (jnp.arange(polar_total, dtype=jnp.int32).astype(jnp.float32) + 0.5) * (
        math.pi / polar_total
    )
    azimuth = jnp.arange(azimuth_total, dtype=jnp.int32).astype(jnp.float32) * (
        2.0 * math.pi / azimuth_total
    )
    octant = jnp.arange(4, dtype=jnp.int32)
    sign_x = ((octant & 1) * 2 - 1).astype(jnp.float32)[:, None, None]
    sign_y = ((octant >> 1 & 1) * 2 - 1).astype(jnp.float32)[:, None, None]
    along_x = jnp.sin(polar)[:, None] * jnp.cos(azimuth)[None, :]
    along_y = jnp.sin(polar)[:, None] * jnp.sin(azimuth)[None, :]
    along_z = jnp.cos(polar)[:, None] + jnp.zeros((1, azimuth_total), jnp.float32)
    phase = KAPPA_H * (sign_x * along_x + sign_y * along_y - along_z)
    return jnp.cos(phase), jnp.sin(phase)


def prepare_kernel(theta_ref, phi_ref, turned_ref, copy_ref):
    turned_ref[...] = jnp.transpose(theta_ref[...].astype(jnp.float32)).astype(jnp.bfloat16)
    copy_ref[...] = phi_ref[...]


def aggregate_kernel(x_ref, theta_ref, phi_ref, cos_ref, sin_ref, out_ref, mid_ref, raised_ref):
    theta = theta_ref[...]
    polar_total = theta.shape[0]
    for p in range(out_ref.shape[1]):
        for o in range(8):
            for r in range(2):
                x = x_ref[:, p * 8 + o, r].reshape(theta.shape[1], phi_ref.shape[0])
                mid = jnp.dot(theta, x, preferred_element_type=jnp.float32)
                k = o * 2 + r
                mid_ref[k * polar_total : (k + 1) * polar_total, :] = mid.astype(jnp.bfloat16)
        raised_ref[...] = jnp.dot(mid_ref[...], phi_ref[...], preferred_element_type=jnp.float32).reshape(
            raised_ref.shape
        )

        def slab(s, carry):
            rows = pl.ds(pl.multiple_of(s * 8, 8), 8)
            real = imag = None
            for o in range(4):
                c = cos_ref[o, rows, :]
                d = sin_ref[o, rows, :]
                ar, ai = raised_ref[2 * o, rows, :], raised_ref[2 * o + 1, rows, :]
                br, bi = raised_ref[14 - 2 * o, rows, :], raised_ref[15 - 2 * o, rows, :]
                tr = c * (ar + br) - d * (ai - bi)
                ti = d * (ar - br) + c * (ai + bi)
                real = tr if real is None else real + tr
                imag = ti if imag is None else imag + ti
            out_ref[s, p, 0] = real.astype(jnp.bfloat16)
            out_ref[s, p, 1] = imag.astype(jnp.bfloat16)
            return carry

        lax.fori_loop(0, out_ref.shape[0], slab, 0)


def widen_kernel(x_ref, out_ref, buffer, sems):
    parts = sems.shape[0]
    size = x_ref.shape[0] // parts

    def copy(i):
        at = pl.ds(i * size, size)
        return pltpu.make_async_copy(x_ref.at[at], buffer.at[at], sems.at[i])

    for i in range(parts):
        copy(i).start()
    for i in range(parts):
        copy(i).wait()

        def widen(k, carry):
            out_ref[k] = buffer[k].astype(jnp.float32)
            return carry

        lax.fori_loop(i * size, (i + 1) * size, widen, 0)


def widen_rows(block, pool_ref, start):
    def widen(i, carry):
        pool_ref[start + i] = block[i].astype(jnp.float32)
        return carry

    lax.fori_loop(0, block.shape[0], widen, 0, unroll=4)


def pool_kernel(own_ref, other_ref, pool_ref, parents_ref, sem):
    copy = pltpu.make_async_copy(own_ref, parents_ref, sem)
    copy.start()
    boxes = own_ref.shape[0]
    widen_rows(own_ref, pool_ref, 0)
    widen_rows(other_ref, pool_ref, boxes)
    pool_ref[pool_ref.shape[0] - 1] = jnp.zeros(pool_ref.shape[1:], jnp.float32)
    copy.wait()


def add_entry(list_ref, trans_ref, pool_ref, b, j, real, imag):
    value = list_ref[b, j]
    at, kind = lax.shift_right_logical(value, 9), value & 511
    sr, si = pool_ref[at, 0], pool_ref[at, 1]
    tr, ti = trans_ref[kind, 0], trans_ref[kind, 1]
    return real + (tr * sr - ti * si), imag + (tr * si + ti * sr)


def early_kernel(lists, trans_ref, *refs):
    *blocks, _, out_ref, pool_ref, list_ref, sem = refs
    copy = pltpu.make_async_copy(lists, list_ref, sem)
    copy.start()
    boxes = out_ref.shape[0]
    for i, block in enumerate(blocks):
        widen_rows(block, pool_ref, (2 + i) * boxes)
    copy.wait()

    def box(b, carry):
        real = imag = jnp.zeros(out_ref.shape[2:], jnp.float32)
        for j in range(EARLY):
            real, imag = add_entry(list_ref, trans_ref, pool_ref, b, 64 + j, real, imag)
        out_ref[b, 0] = real
        out_ref[b, 1] = imag
        return carry

    lax.fori_loop(0, boxes, box, 0)


def late_kernel(lists, trans_ref, sum_ref, *refs):
    *blocks, _, final_ref, pool_ref, out_ref, list_ref, sem, sems = refs
    copy = pltpu.make_async_copy(lists, list_ref, sem)
    copy.start()
    boxes = out_ref.shape[0]
    for i, block in enumerate(blocks):
        widen_rows(block, pool_ref, (6 + i) * boxes)
    copy.wait()

    def box(b, carry):
        def more(j, acc):
            return add_entry(list_ref, trans_ref, pool_ref, b, j, *acc)

        acc = (sum_ref[b, 0], sum_ref[b, 1])
        real, imag = lax.fori_loop(list_ref[b, WIDTH - 1], EARLY, more, acc)
        for j in range(EARLY, 64):
            real, imag = add_entry(list_ref, trans_ref, pool_ref, b, j, real, imag)
        out_ref[b, 0] = real
        out_ref[b, 1] = imag
        return carry

    parts = sems.shape[0]
    size = boxes // parts
    copies = []
    for i in range(parts):
        lax.fori_loop(i * size, (i + 1) * size, box, 0)
        rows = pl.ds(i * size, size)
        out = pltpu.make_async_copy(out_ref.at[rows], final_ref.at[rows], sems.at[i])
        out.start()
        copies.append(out)
    for out in copies:
        out.wait()


def shift(x, axis, step):
    size = lax.axis_size(axis)
    return lax.ppermute(x, axis, [(i, (i + step) % size) for i in range(size)])


def plan_kernel(place_ref, own_ref, after_ref, far_ref, before_ref, slots_ref, kinds_ref, out_ref):
    y, c = place_ref[0], place_ref[1]
    cores, _, cap = own_ref.shape
    boxes, entries = slots_ref.shape
    me = y * cores + c
    slots = slots_ref[...]
    sender = lax.shift_right_logical(slots, 4)
    dy = (lax.shift_right_logical(sender, 1) - y) & 3
    dc = (sender & 1) ^ c
    code = (dy * cores + dc) * cap + (slots & (cap - 1))
    row = jnp.zeros_like(slots)
    for k, (table, block) in enumerate(
        ((own_ref, 0), (after_ref, 2), (far_ref, 6), (before_ref, 4))
    ):
        for core in range(cores):
            for u in range(cap):
                value = table[core, me, u] + (block + core) * boxes
                row = jnp.where(code == (k * cores + core) * cap + u, value, row)
    near = dy != 2
    first = lax.broadcasted_iota(jnp.int32, (entries, entries), 0)
    second = lax.broadcasted_iota(jnp.int32, (entries, entries), 1)
    ahead = (first < second).astype(jnp.float32)
    inside = jnp.dot(near.astype(jnp.float32), ahead, preferred_element_type=jnp.float32)
    inside = inside.astype(jnp.int32)
    own_spot = lax.broadcasted_iota(jnp.int32, slots.shape, 1)
    count = jnp.sum(near.astype(jnp.int32), axis=1, keepdims=True)
    spot = jnp.where(near, inside, count + own_spot - inside)
    value = jnp.transpose((row * 512 + kinds_ref[...]).astype(jnp.float32)).astype(jnp.int32)
    spot = jnp.transpose(spot.astype(jnp.float32)).astype(jnp.int32)
    lane = lax.broadcasted_iota(jnp.int32, (entries, WIDTH), 1) & (entries - 1)
    lines = []
    for b in range(boxes):
        got = jnp.where(spot[:, b : b + 1] == lane, value[:, b : b + 1], 0)
        lines.append(jnp.sum(got, axis=0, keepdims=True))
    packed = jnp.concatenate(lines, axis=0)
    lane = lax.broadcasted_iota(jnp.int32, (boxes, WIDTH), 1)
    packed = jnp.where(lane >= entries + count, 8 * boxes * 512, packed)
    out_ref[...] = jnp.where(lane == WIDTH - 1, count, packed)


def slot_tables(send_index):
    own = jnp.concatenate([send_index, shift(send_index, "c", 1)], axis=0)
    return own, shift(own, "y", -1), shift(own, "y", 2), shift(own, "y", 1)


def plan_lists(tables, list_slots, list_kinds):
    place = jnp.stack([lax.axis_index("y"), lax.axis_index("c")]).astype(jnp.int32)
    return pl.pallas_call(
        plan_kernel,
        out_shape=jax.ShapeDtypeStruct((list_slots.shape[0], WIDTH), jnp.int32),
        in_specs=[SMEM] * 5 + [VMEM] * 2,
        out_specs=VMEM,
        compiler_params=pltpu.CompilerParams(vmem_limit_bytes=4 << 20),
        cost_estimate=pl.CostEstimate(flops=1 << 20, bytes_accessed=1 << 20, transcendentals=0),
        name="plan",
    )(place, *tables, list_slots, list_kinds)


def local(children, interp_theta, interp_phi, translator, send_index, list_slots, list_kinds):
    samp_count = lax.axis_size(SAMP)
    polar_total = interp_theta.shape[1]
    azimuth_total = interp_phi.shape[1]
    child_boxes, _, rows, child_azimuth = children.shape
    own_children = child_boxes // samp_count
    parent_boxes = child_boxes // 8
    out_rows = polar_total // samp_count
    pattern = (2, out_rows, azimuth_total)

    x = children.reshape(samp_count, own_children, 2, rows, child_azimuth)
    x = lax.all_to_all(x, SAMP, split_axis=0, concat_axis=0, tiled=True)

    cosine, sine = phase_tables(polar_total, azimuth_total)
    theta, phi = pl.pallas_call(
        prepare_kernel,
        out_shape=[
            pltpu.VMEM(interp_theta.shape[::-1], jnp.bfloat16),
            pltpu.VMEM(interp_phi.shape, jnp.bfloat16),
        ],
        in_specs=[VMEM] * 2,
        out_specs=[VMEM] * 2,
        compiler_params=pltpu.CompilerParams(vmem_limit_bytes=4 << 20),
        cost_estimate=pl.CostEstimate(flops=1 << 20, bytes_accessed=1 << 18, transcendentals=0),
        name="prepare",
    )(interp_theta, interp_phi)
    tables = slot_tables(send_index)
    x, theta, phi, *tables = lax.optimization_barrier((x, theta, phi, *tables))
    mine = pl.pallas_call(
        aggregate_kernel,
        out_shape=jax.ShapeDtypeStruct((samp_count, own_children // 8) + pattern, jnp.bfloat16),
        in_specs=[VMEM] * 5,
        out_specs=VMEM,
        scratch_shapes=[
            pltpu.VMEM((16 * polar_total, child_azimuth), jnp.bfloat16),
            pltpu.VMEM((16, polar_total, azimuth_total), jnp.float32),
        ],
        compiler_params=pltpu.CompilerParams(vmem_limit_bytes=12 << 20),
        cost_estimate=pl.CostEstimate(flops=335 << 20, bytes_accessed=4 << 20, transcendentals=0),
        name="aggregate",
    )(x, theta, phi, cosine, sine)
    mine = lax.all_to_all(mine, SAMP, split_axis=0, concat_axis=0, tiled=True)
    lists = plan_lists(tables, list_slots, list_kinds)
    mine, lists = lax.optimization_barrier((mine, lists))
    own = mine.reshape((parent_boxes,) + pattern)
    after = shift(own, "y", -1)
    before = shift(own, "y", 1)
    other = shift(own, "c", 1)
    source, own = lax.optimization_barrier((translator, own))
    wide = pl.pallas_call(
        widen_kernel,
        out_shape=pltpu.VMEM(translator.shape, jnp.float32),
        in_specs=[HBM],
        out_specs=VMEM,
        scratch_shapes=[
            pltpu.VMEM(translator.shape, jnp.bfloat16),
            pltpu.SemaphoreType.DMA((4,)),
        ],
        compiler_params=pltpu.CompilerParams(vmem_limit_bytes=56 << 20),
        cost_estimate=pl.CostEstimate(flops=4 << 20, bytes_accessed=8 << 20, transcendentals=0),
        name="widen",
    )(source)

    own, wide = lax.optimization_barrier((own, wide))
    far = shift(own, "y", 2)

    shape = (parent_boxes,) + pattern
    pool_shape = pltpu.VMEM((8 * parent_boxes + 1,) + pattern, jnp.float32)
    params = pltpu.CompilerParams(vmem_limit_bytes=8 << 20)
    cost = pl.CostEstimate(flops=16 << 20, bytes_accessed=8 << 20, transcendentals=0)
    list_scratch = [pltpu.SMEM(lists.shape, jnp.int32), pltpu.SemaphoreType.DMA]
    pool, parents = pl.pallas_call(
        pool_kernel,
        out_shape=[pool_shape, jax.ShapeDtypeStruct(shape, jnp.bfloat16)],
        in_specs=[VMEM] * 2,
        out_specs=[VMEM, HBM],
        scratch_shapes=[pltpu.SemaphoreType.DMA],
        compiler_params=params,
        cost_estimate=cost,
        name="pool",
    )(own, other)
    after, before, pool = lax.optimization_barrier((after, before, pool))
    near = [after, shift(after, "c", 1), before, shift(before, "c", 1)]
    early, pool = pl.pallas_call(
        early_kernel,
        out_shape=[pltpu.VMEM(shape, jnp.float32), pool_shape],
        in_specs=[VMEM] * 7,
        out_specs=[VMEM] * 2,
        input_output_aliases={6: 1},
        scratch_shapes=list_scratch,
        compiler_params=params,
        cost_estimate=cost,
        name="early",
    )(lists, wide, *near, pool)
    far, early = lax.optimization_barrier((far, early))
    field, _ = pl.pallas_call(
        late_kernel,
        out_shape=[jax.ShapeDtypeStruct(shape, jnp.float32), pool_shape],
        in_specs=[VMEM] * 6,
        out_specs=[HBM, VMEM],
        input_output_aliases={5: 1},
        scratch_shapes=[pltpu.VMEM(shape, jnp.float32)]
        + list_scratch
        + [pltpu.SemaphoreType.DMA((4,))],
        compiler_params=params,
        cost_estimate=cost,
        name="late",
    )(lists, wide, early, far, shift(far, "c", 1), pool)
    return parents, field


def solution(mesh):
    y_count, x_count = 4, 4
    fine = Mesh(
        mesh.devices.reshape(y_count, mesh.shape["box"] // y_count, x_count, -1),
        BOX + SAMP,
    )
    return jax.shard_map(
        local,
        mesh=fine,
        in_specs=(
            P(BOX, None, SAMP, None),
            P(),
            P(),
            P(None, None, SAMP, None),
            P(BOX, None, None),
            P(BOX, None),
            P(BOX, None),
        ),
        out_specs=(P(BOX, None, SAMP, None), P(BOX, None, SAMP, None)),
        check_vma=False,
    )
```

```python
import math

import jax
import jax.numpy as jnp
from jax import lax
from jax.experimental import pallas as pl
from jax.experimental.pallas import tpu as pltpu
from jax.sharding import Mesh, PartitionSpec as P


KAPPA_H = 12.0
SAMP = ("x", "z")
BOX = ("y", "c")
WIDTH = 128
FIRST = 12
EARLY = 44
CHUNK = 16
VMEM = pl.BlockSpec(memory_space=pltpu.VMEM)
SMEM = pl.BlockSpec(memory_space=pltpu.SMEM)
HBM = pl.BlockSpec(memory_space=pltpu.HBM)


def phase_tables(polar_total, azimuth_total):
    polar = (jnp.arange(polar_total, dtype=jnp.int32).astype(jnp.float32) + 0.5) * (
        math.pi / polar_total
    )
    azimuth = jnp.arange(azimuth_total, dtype=jnp.int32).astype(jnp.float32) * (
        2.0 * math.pi / azimuth_total
    )
    octant = jnp.arange(4, dtype=jnp.int32)
    sign_x = ((octant & 1) * 2 - 1).astype(jnp.float32)[:, None, None]
    sign_y = ((octant >> 1 & 1) * 2 - 1).astype(jnp.float32)[:, None, None]
    along_x = jnp.sin(polar)[:, None] * jnp.cos(azimuth)[None, :]
    along_y = jnp.sin(polar)[:, None] * jnp.sin(azimuth)[None, :]
    along_z = jnp.cos(polar)[:, None] + jnp.zeros((1, azimuth_total), jnp.float32)
    phase = KAPPA_H * (sign_x * along_x + sign_y * along_y - along_z)
    return jnp.cos(phase), jnp.sin(phase)


def aggregate_kernel(x_ref, theta_ref, phi_ref, cos_ref, sin_ref, out_ref, mid_ref):
    theta = jnp.transpose(theta_ref[...].astype(jnp.float32)).astype(jnp.bfloat16)
    phi = phi_ref[...]
    chunks = theta.shape[0] // CHUNK
    for p in range(out_ref.shape[1]):
        for o in range(8):
            for r in range(2):
                x = x_ref[:, p * 8 + o, r].reshape(theta.shape[1], phi.shape[0])
                mid = jnp.dot(theta, x, preferred_element_type=jnp.float32).astype(jnp.bfloat16)
                for h in range(chunks):
                    at = (h * 16 + o * 2 + r) * CHUNK
                    mid_ref[at : at + CHUNK, :] = mid[h * CHUNK : (h + 1) * CHUNK]
        for h in range(chunks):
            mid = mid_ref[h * 16 * CHUNK : (h + 1) * 16 * CHUNK, :]
            raised = jnp.dot(mid, phi, preferred_element_type=jnp.float32)
            for s in range(CHUNK // 8):
                row = h * CHUNK + s * 8
                real = imag = None
                for o in range(4):
                    c = cos_ref[o, row : row + 8, :]
                    d = sin_ref[o, row : row + 8, :]
                    ar, ai, br, bi = (
                        raised[k * CHUNK + s * 8 : k * CHUNK + s * 8 + 8]
                        for k in (2 * o, 2 * o + 1, 14 - 2 * o, 15 - 2 * o)
                    )
                    tr = c * (ar + br) - d * (ai - bi)
                    ti = d * (ar - br) + c * (ai + bi)
                    real = tr if real is None else real + tr
                    imag = ti if imag is None else imag + ti
                out_ref[row // 8, p, 0] = real.astype(jnp.bfloat16)
                out_ref[row // 8, p, 1] = imag.astype(jnp.bfloat16)


def widen_kernel(x_ref, out_ref, buffer, sems):
    parts = sems.shape[0]
    size = x_ref.shape[0] // parts

    def copy(i):
        at = pl.ds(i * size, size)
        return pltpu.make_async_copy(x_ref.at[at], buffer.at[at], sems.at[i])

    for i in range(parts):
        copy(i).start()
    for i in range(parts):
        copy(i).wait()

        def widen(k, carry):
            out_ref[k] = buffer[k].astype(jnp.float32)
            return carry

        lax.fori_loop(i * size, (i + 1) * size, widen, 0)


def widen_rows(block, pool_ref, start):
    def widen(i, carry):
        pool_ref[start + i] = block[i].astype(jnp.float32)
        return carry

    lax.fori_loop(0, block.shape[0], widen, 0, unroll=4)


def add_entry(list_ref, trans_ref, pool_ref, b, j, real, imag):
    value = list_ref[b, j]
    at, kind = lax.shift_right_logical(value, 9), value & 511
    sr, si = pool_ref[at, 0], pool_ref[at, 1]
    tr, ti = trans_ref[kind, 0], trans_ref[kind, 1]
    return real + (tr * sr - ti * si), imag + (tr * si + ti * sr)


def add_box(list_ref, trans_ref, pool_ref, b, some, rest, acc):
    def more(j, acc):
        return add_entry(list_ref, trans_ref, pool_ref, b, j, *acc)

    if rest is not None:
        acc = lax.fori_loop(*rest, more, acc)
    for j in some:
        acc = add_entry(list_ref, trans_ref, pool_ref, b, j, *acc)
    return acc


def first_kernel(lists, trans_ref, own_ref, other_ref, out_ref, pool_ref, parents_ref, *scratch):
    list_ref, sem, out_sem = scratch
    copy = pltpu.make_async_copy(lists, list_ref, sem)
    copy.start()
    store = pltpu.make_async_copy(own_ref, parents_ref, out_sem)
    store.start()
    boxes = own_ref.shape[0]
    widen_rows(own_ref, pool_ref, 0)
    widen_rows(other_ref, pool_ref, boxes)
    pool_ref[pool_ref.shape[0] - 1] = jnp.zeros(pool_ref.shape[1:], jnp.float32)
    copy.wait()

    def box(b, carry):
        zero = jnp.zeros(out_ref.shape[2:], jnp.float32)
        some = range(64, 64 + FIRST)
        out_ref[b, 0], out_ref[b, 1] = add_box(
            list_ref, trans_ref, pool_ref, b, some, None, (zero, zero)
        )
        return carry

    lax.fori_loop(0, boxes, box, 0)
    store.wait()


def early_kernel(lists, trans_ref, sum_ref, *refs):
    *blocks, _, out_ref, pool_ref, list_ref, sem = refs
    copy = pltpu.make_async_copy(lists, list_ref, sem)
    copy.start()
    boxes = out_ref.shape[0]
    for i, block in enumerate(blocks):
        widen_rows(block, pool_ref, (2 + i) * boxes)
    copy.wait()

    def box(b, carry):
        rest = (list_ref[b, WIDTH - 2], jnp.minimum(list_ref[b, WIDTH - 1], FIRST))
        some = range(64 + FIRST, 64 + EARLY)
        acc = (sum_ref[b, 0], sum_ref[b, 1])
        out_ref[b, 0], out_ref[b, 1] = add_box(
            list_ref, trans_ref, pool_ref, b, some, rest, acc
        )
        return carry

    lax.fori_loop(0, boxes, box, 0)


def late_kernel(lists, trans_ref, sum_ref, *refs):
    *blocks, _, final_ref, pool_ref, out_ref, list_ref, sem, sems = refs
    copy = pltpu.make_async_copy(lists, list_ref, sem)
    copy.start()
    boxes = out_ref.shape[0]
    for i, block in enumerate(blocks):
        widen_rows(block, pool_ref, (6 + i) * boxes)
    copy.wait()

    def box(b, carry):
        rest = (list_ref[b, WIDTH - 1], EARLY)
        acc = (sum_ref[b, 0], sum_ref[b, 1])
        out_ref[b, 0], out_ref[b, 1] = add_box(
            list_ref, trans_ref, pool_ref, b, range(EARLY, 64), rest, acc
        )
        return carry

    parts = sems.shape[0]
    size = boxes // parts
    copies = []
    for i in range(parts):
        lax.fori_loop(i * size, (i + 1) * size, box, 0)
        rows = pl.ds(i * size, size)
        out = pltpu.make_async_copy(out_ref.at[rows], final_ref.at[rows], sems.at[i])
        out.start()
        copies.append(out)
    for out in copies:
        out.wait()


def shift(x, axis, step):
    size = lax.axis_size(axis)
    return lax.ppermute(x, axis, [(i, (i + step) % size) for i in range(size)])


def plan_kernel(place_ref, own_ref, after_ref, before_ref, far_ref, slots_ref, kinds_ref, out_ref):
    y, c = place_ref[0], place_ref[1]
    cores, _, cap = own_ref.shape
    boxes, entries = slots_ref.shape
    me = y * cores + c
    slots = slots_ref[...]
    sender = lax.shift_right_logical(slots, 4)
    dy = (lax.shift_right_logical(sender, 1) - y) & 3
    dc = (sender & 1) ^ c
    code = (dy * cores + dc) * cap + (slots & (cap - 1))
    row = jnp.zeros_like(slots)
    for k, (table, block) in enumerate(
        ((own_ref, 0), (after_ref, 2), (far_ref, 6), (before_ref, 4))
    ):
        for core in range(cores):
            for u in range(cap):
                value = table[core, me, u] + (block + core) * boxes
                row = jnp.where(code == (k * cores + core) * cap + u, value, row)
    first = lax.broadcasted_iota(jnp.int32, (entries, entries), 0)
    second = lax.broadcasted_iota(jnp.int32, (entries, entries), 1)
    ahead = (first < second).astype(jnp.float32)
    spot = jnp.zeros_like(slots)
    begin = jnp.zeros((boxes, 1), jnp.int32)
    ends = []
    for mine in (dy == 0, (dy & 1) == 1, dy == 2):
        inside = jnp.dot(mine.astype(jnp.float32), ahead, preferred_element_type=jnp.float32)
        spot = jnp.where(mine, begin + inside.astype(jnp.int32), spot)
        begin = begin + jnp.sum(mine.astype(jnp.int32), axis=1, keepdims=True)
        ends.append(begin)
    value = jnp.transpose((row * 512 + kinds_ref[...]).astype(jnp.float32)).astype(jnp.int32)
    spot = jnp.transpose(spot.astype(jnp.float32)).astype(jnp.int32)
    lane = lax.broadcasted_iota(jnp.int32, (entries, WIDTH), 1) & (entries - 1)
    lines = []
    for b in range(boxes):
        got = jnp.where(spot[:, b : b + 1] == lane, value[:, b : b + 1], 0)
        lines.append(jnp.sum(got, axis=0, keepdims=True))
    packed = jnp.concatenate(lines, axis=0)
    lane = lax.broadcasted_iota(jnp.int32, (boxes, WIDTH), 1)
    masked = (lane >= entries) & (lane >= entries + jnp.where(lane < entries + FIRST, *ends[:2]))
    packed = jnp.where(masked, 8 * boxes * 512, packed)
    packed = jnp.where(lane == WIDTH - 2, ends[0], packed)
    out_ref[...] = jnp.where(lane == WIDTH - 1, ends[1], packed)


def slot_tables(send_index):
    own = jnp.concatenate([send_index, shift(send_index, "c", 1)], axis=0)
    return own, shift(own, "y", -1), shift(own, "y", 1)


def plan_lists(tables, list_slots, list_kinds):
    place = jnp.stack([lax.axis_index("y"), lax.axis_index("c")]).astype(jnp.int32)
    return pl.pallas_call(
        plan_kernel,
        out_shape=jax.ShapeDtypeStruct((list_slots.shape[0], WIDTH), jnp.int32),
        in_specs=[SMEM] * 5 + [VMEM] * 2,
        out_specs=VMEM,
        compiler_params=pltpu.CompilerParams(vmem_limit_bytes=4 << 20),
        cost_estimate=pl.CostEstimate(flops=1 << 20, bytes_accessed=1 << 20, transcendentals=0),
        name="plan",
    )(place, *tables, list_slots, list_kinds)


def local(children, interp_theta, interp_phi, translator, send_index, list_slots, list_kinds):
    samp_count = lax.axis_size(SAMP)
    polar_total = interp_theta.shape[1]
    azimuth_total = interp_phi.shape[1]
    child_boxes, _, rows, child_azimuth = children.shape
    own_children = child_boxes // samp_count
    parent_boxes = child_boxes // 8
    out_rows = polar_total // samp_count
    pattern = (2, out_rows, azimuth_total)

    x = children.reshape(samp_count, own_children, 2, rows, child_azimuth)
    x = lax.all_to_all(x, SAMP, split_axis=0, concat_axis=0, tiled=True)

    cosine, sine = phase_tables(polar_total, azimuth_total)
    nothing = lax.optimization_barrier(jnp.zeros((), jnp.bfloat16))
    theta, phi = interp_theta + nothing, interp_phi + nothing
    near_tables = slot_tables(send_index)
    x, theta, phi, *near_tables = lax.optimization_barrier((x, theta, phi, *near_tables))
    mine = pl.pallas_call(
        aggregate_kernel,
        out_shape=jax.ShapeDtypeStruct((samp_count, own_children // 8) + pattern, jnp.bfloat16),
        in_specs=[VMEM] * 5,
        out_specs=VMEM,
        scratch_shapes=[
            pltpu.VMEM((16 * polar_total, child_azimuth), jnp.bfloat16),
        ],
        compiler_params=pltpu.CompilerParams(vmem_limit_bytes=12 << 20),
        cost_estimate=pl.CostEstimate(flops=335 << 20, bytes_accessed=4 << 20, transcendentals=0),
        name="aggregate",
    )(x, theta, phi, cosine, sine)
    mine = lax.all_to_all(mine, SAMP, split_axis=0, concat_axis=0, tiled=True)
    far_table = shift(near_tables[0], "y", 2)
    mine, far_table = lax.optimization_barrier((mine, far_table))
    own = mine.reshape((parent_boxes,) + pattern)
    after = shift(own, "y", -1)
    before = shift(own, "y", 1)
    other = shift(own, "c", 1)
    source, own = lax.optimization_barrier((translator, own))
    wide = pl.pallas_call(
        widen_kernel,
        out_shape=pltpu.VMEM(translator.shape, jnp.float32),
        in_specs=[HBM],
        out_specs=VMEM,
        scratch_shapes=[
            pltpu.VMEM(translator.shape, jnp.bfloat16),
            pltpu.SemaphoreType.DMA((4,)),
        ],
        compiler_params=pltpu.CompilerParams(vmem_limit_bytes=56 << 20),
        cost_estimate=pl.CostEstimate(flops=4 << 20, bytes_accessed=8 << 20, transcendentals=0),
        name="widen",
    )(source)

    own, wide, far_table = lax.optimization_barrier((own, wide, far_table))
    lists = plan_lists((*near_tables, far_table), list_slots, list_kinds)
    far = shift(own, "y", 2)

    shape = (parent_boxes,) + pattern
    pool_shape = pltpu.VMEM((8 * parent_boxes + 1,) + pattern, jnp.float32)
    params = pltpu.CompilerParams(vmem_limit_bytes=8 << 20)
    cost = pl.CostEstimate(flops=16 << 20, bytes_accessed=8 << 20, transcendentals=0)
    list_scratch = [pltpu.SMEM(lists.shape, jnp.int32), pltpu.SemaphoreType.DMA]
    field, pool, parents = pl.pallas_call(
        first_kernel,
        out_shape=[
            pltpu.VMEM(shape, jnp.float32),
            pool_shape,
            jax.ShapeDtypeStruct(shape, jnp.bfloat16),
        ],
        in_specs=[VMEM] * 4,
        out_specs=[VMEM, VMEM, HBM],
        scratch_shapes=list_scratch + [pltpu.SemaphoreType.DMA],
        compiler_params=params,
        cost_estimate=cost,
        name="first",
    )(lists, wide, own, other)
    after, before, pool = lax.optimization_barrier((after, before, pool))
    near = [after, shift(after, "c", 1), before, shift(before, "c", 1)]
    early, pool = pl.pallas_call(
        early_kernel,
        out_shape=[pltpu.VMEM(shape, jnp.float32), pool_shape],
        in_specs=[VMEM] * 8,
        out_specs=[VMEM] * 2,
        input_output_aliases={7: 1},
        scratch_shapes=list_scratch,
        compiler_params=params,
        cost_estimate=cost,
        name="early",
    )(lists, wide, field, *near, pool)
    far, early = lax.optimization_barrier((far, early))
    field, _ = pl.pallas_call(
        late_kernel,
        out_shape=[jax.ShapeDtypeStruct(shape, jnp.float32), pool_shape],
        in_specs=[VMEM] * 6,
        out_specs=[HBM, VMEM],
        input_output_aliases={5: 1},
        scratch_shapes=[pltpu.VMEM(shape, jnp.float32)]
        + list_scratch
        + [pltpu.SemaphoreType.DMA((4,))],
        compiler_params=params,
        cost_estimate=cost,
        name="late",
    )(lists, wide, early, far, shift(far, "c", 1), pool)
    return parents, field


def solution(mesh):
    y_count, x_count = 4, 4
    fine = Mesh(
        mesh.devices.reshape(y_count, mesh.shape["box"] // y_count, x_count, -1),
        BOX + SAMP,
    )
    return jax.shard_map(
        local,
        mesh=fine,
        in_specs=(
            P(BOX, None, SAMP, None),
            P(),
            P(),
            P(None, None, SAMP, None),
            P(BOX, None, None),
            P(BOX, None),
            P(BOX, None),
        ),
        out_specs=(P(BOX, None, SAMP, None), P(BOX, None, SAMP, None)),
        check_vma=False,
    )
```

```python
import functools
import math

import jax
import jax.numpy as jnp
from jax import lax
from jax.experimental import pallas as pl
from jax.experimental.pallas import tpu as pltpu
from jax.sharding import Mesh, PartitionSpec as P


KAPPA_H = 12.0
SAMP = ("x", "z")
BOX = ("y", "c")
WIDTH = 128
ROWS = (0, 2, 4, 6, 7)
CUTS = (0, 14, 28, 46, 54, 64)
CHUNK = 16
VMEM = pl.BlockSpec(memory_space=pltpu.VMEM)
SMEM = pl.BlockSpec(memory_space=pltpu.SMEM)
HBM = pl.BlockSpec(memory_space=pltpu.HBM)


def phase_tables(polar_total, azimuth_total):
    polar = (jnp.arange(polar_total, dtype=jnp.int32).astype(jnp.float32) + 0.5) * (
        math.pi / polar_total
    )
    azimuth = jnp.arange(azimuth_total, dtype=jnp.int32).astype(jnp.float32) * (
        2.0 * math.pi / azimuth_total
    )
    octant = jnp.arange(4, dtype=jnp.int32)
    sign_x = ((octant & 1) * 2 - 1).astype(jnp.float32)[:, None, None]
    sign_y = ((octant >> 1 & 1) * 2 - 1).astype(jnp.float32)[:, None, None]
    along_x = jnp.sin(polar)[:, None] * jnp.cos(azimuth)[None, :]
    along_y = jnp.sin(polar)[:, None] * jnp.sin(azimuth)[None, :]
    along_z = jnp.cos(polar)[:, None] + jnp.zeros((1, azimuth_total), jnp.float32)
    phase = KAPPA_H * (sign_x * along_x + sign_y * along_y - along_z)
    return jnp.cos(phase), jnp.sin(phase)


def aggregate_kernel(x_ref, theta_ref, phi_ref, cos_ref, sin_ref, out_ref, mid_ref):
    theta = jnp.transpose(theta_ref[...].astype(jnp.float32)).astype(jnp.bfloat16)
    phi = phi_ref[...]
    chunks = theta.shape[0] // CHUNK
    for p in range(out_ref.shape[1]):
        for o in range(8):
            for r in range(2):
                x = x_ref[:, p * 8 + o, r].reshape(theta.shape[1], phi.shape[0])
                mid = jnp.dot(theta, x, preferred_element_type=jnp.float32).astype(jnp.bfloat16)
                for h in range(chunks):
                    at = (h * 16 + o * 2 + r) * CHUNK
                    mid_ref[at : at + CHUNK, :] = mid[h * CHUNK : (h + 1) * CHUNK]
        for h in range(chunks):
            mid = mid_ref[h * 16 * CHUNK : (h + 1) * 16 * CHUNK, :]
            raised = jnp.dot(mid, phi, preferred_element_type=jnp.float32)
            for s in range(CHUNK // 8):
                row = h * CHUNK + s * 8
                real = imag = None
                for o in range(4):
                    c = cos_ref[o, row : row + 8, :]
                    d = sin_ref[o, row : row + 8, :]
                    ar, ai, br, bi = (
                        raised[k * CHUNK + s * 8 : k * CHUNK + s * 8 + 8]
                        for k in (2 * o, 2 * o + 1, 14 - 2 * o, 15 - 2 * o)
                    )
                    tr = c * (ar + br) - d * (ai - bi)
                    ti = d * (ar - br) + c * (ai + bi)
                    real = tr if real is None else real + tr
                    imag = ti if imag is None else imag + ti
                out_ref[row // 8, p, 0] = real.astype(jnp.bfloat16)
                out_ref[row // 8, p, 1] = imag.astype(jnp.bfloat16)


def stage_kernel(x_ref, out_ref, sem):
    copy = pltpu.make_async_copy(x_ref, out_ref, sem)
    copy.start()
    copy.wait()


def widen_kernel(x_ref, out_ref):
    def widen(k, carry):
        out_ref[k] = x_ref[k].astype(jnp.float32)
        return carry

    lax.fori_loop(0, x_ref.shape[0], widen, 0, unroll=4)


def class_kernel(k, list_ref, trans_ref, *refs):
    first, last = k == 0, k == len(CUTS) - 2
    if first:
        *blocks, out_ref, pool_ref, parents_ref, sem = refs
        store = pltpu.make_async_copy(blocks[0], parents_ref, sem)
        store.start()
    elif last:
        sum_ref, *blocks, _, final_ref, pool_ref, out_ref, sems = refs
    else:
        sum_ref, *blocks, _, out_ref, pool_ref = refs
    boxes = out_ref.shape[0]
    for i, block in enumerate(blocks):

        def widen(n, carry, block=block, start=(ROWS[k] + i) * boxes):
            pool_ref[start + n] = block[n].astype(jnp.float32)
            return carry

        lax.fori_loop(0, boxes, widen, 0, unroll=4)
    if first:
        pool_ref[pool_ref.shape[0] - 1] = jnp.zeros(pool_ref.shape[1:], jnp.float32)

    def add(b, j, acc):
        value = list_ref[b, j]
        at, kind = lax.shift_right_logical(value, 9), value & 511
        sr, si = pool_ref[at, 0], pool_ref[at, 1]
        tr, ti = trans_ref[kind, 0], trans_ref[kind, 1]
        return acc[0] + (tr * sr - ti * si), acc[1] + (tr * si + ti * sr)

    def box(b, carry):
        if first:
            zero = jnp.zeros(out_ref.shape[2:], jnp.float32)
            acc = (zero, zero)
        else:
            acc = (sum_ref[b, 0], sum_ref[b, 1])
            begin = list_ref[boxes + b, k - 1]
            end = CUTS[k] if last else jnp.minimum(list_ref[boxes + b, k], CUTS[k])
            acc = lax.fori_loop(begin, end, lambda j, acc: add(b, j, acc), acc)
        for j in range(CUTS[k], CUTS[k + 1]):
            acc = add(b, CUTS[-1] + j, acc)
        out_ref[b, 0], out_ref[b, 1] = acc
        return carry

    if not last:
        lax.fori_loop(0, boxes, box, 0)
    else:
        parts = sems.shape[0]
        size = boxes // parts
        copies = []
        for i in range(parts):
            lax.fori_loop(i * size, (i + 1) * size, box, 0)
            rows = pl.ds(i * size, size)
            out = pltpu.make_async_copy(out_ref.at[rows], final_ref.at[rows], sems.at[i])
            out.start()
            copies.append(out)
        for out in copies:
            out.wait()
    if first:
        store.wait()


def shift(x, axis, step):
    size = lax.axis_size(axis)
    return lax.ppermute(x, axis, [(i, (i + step) % size) for i in range(size)])


def plan_kernel(me_ref, own_ref, after_ref, before_ref, far_ref, slots_ref, kinds_ref, *rest):
    out_ref, list_ref, sem = rest
    cores, receivers, cap = own_ref.shape
    boxes, entries = slots_ref.shape
    me = me_ref[:, :entries]
    slots = slots_ref[...]
    sender = lax.shift_right_logical(slots, 4)
    dy = (lax.shift_right_logical(sender, 1) - lax.shift_right_logical(me, 1)) & 3
    dc = (sender & 1) ^ (me & 1)
    code = (dy * cores + dc) * cap + (slots & (cap - 1))
    is_me = lax.broadcasted_iota(jnp.int32, (receivers, cap), 0) == me[:receivers, :cap]
    pieces = []
    for table, block, step in (
        (own_ref, 0, 1),
        (after_ref, 2, 2),
        (far_ref, 6, 1),
        (before_ref, 3, 2),
    ):
        for core in range(cores):
            mine = jnp.sum(jnp.where(is_me, table[core], 0), axis=0, keepdims=True)
            pieces.append(mine + (block + step * core) * boxes)
    table = jnp.broadcast_to(jnp.concatenate(pieces, axis=1), (boxes, WIDTH))
    row = jnp.take_along_axis(table, jnp.concatenate([code, code], axis=1), axis=1)
    row = row[:, :entries]
    far = dy == 2
    klass = jnp.where(dy == 0, 0, jnp.where(far, 3, 1) + dc)
    first = lax.broadcasted_iota(jnp.int32, (entries, entries), 0)
    second = lax.broadcasted_iota(jnp.int32, (entries, entries), 1)
    ahead = (first < second).astype(jnp.float32)
    lane = lax.broadcasted_iota(jnp.int32, (boxes, WIDTH), 1)
    slot = lane - entries
    spot = jnp.zeros_like(slots)
    begin = jnp.zeros((boxes, 1), jnp.int32)
    keep = slot < 0
    ends = jnp.zeros((boxes, WIDTH), jnp.int32)
    for k in range(len(CUTS) - 1):
        mine = klass == k
        inside = jnp.dot(mine.astype(jnp.float32), ahead, preferred_element_type=jnp.float32)
        spot = jnp.where(mine, begin + inside.astype(jnp.int32), spot)
        begin = begin + jnp.sum(mine.astype(jnp.int32), axis=1, keepdims=True)
        keep = keep | ((slot >= CUTS[k]) & (slot < CUTS[k + 1]) & (slot < begin))
        ends = jnp.where(lane == k, begin, ends)
    value = jnp.transpose((row * 512 + kinds_ref[...]).astype(jnp.float32)).astype(jnp.int32)
    spot = jnp.transpose(spot.astype(jnp.float32)).astype(jnp.int32)
    target = lax.broadcasted_iota(jnp.int32, (entries, WIDTH), 1) & (entries - 1)
    for b in range(boxes):
        got = jnp.where(spot[:, b : b + 1] == target, value[:, b : b + 1], 0)
        list_ref[b : b + 1, :] = jnp.sum(got, axis=0, keepdims=True)
    list_ref[:boxes, :] = jnp.where(keep, list_ref[:boxes, :], 8 * boxes * 512)
    list_ref[boxes:, :] = ends
    copy = pltpu.make_async_copy(list_ref, out_ref, sem)
    copy.start()
    copy.wait()


def slot_tables(send_index):
    own = jnp.concatenate([send_index, shift(send_index, "c", 1)], axis=0)
    return own, shift(own, "y", -1), shift(own, "y", 1)


def plan_lists(tables, list_slots, list_kinds):
    boxes = list_slots.shape[0]
    me = lax.axis_index("y") * lax.axis_size("c") + lax.axis_index("c")
    me = jnp.broadcast_to(me.astype(jnp.int32), (boxes, WIDTH))
    return pl.pallas_call(
        plan_kernel,
        out_shape=pltpu.SMEM((2 * boxes, WIDTH), jnp.int32),
        in_specs=[VMEM] * 7,
        out_specs=SMEM,
        scratch_shapes=[pltpu.VMEM((2 * boxes, WIDTH), jnp.int32), pltpu.SemaphoreType.DMA],
        compiler_params=pltpu.CompilerParams(vmem_limit_bytes=4 << 20),
        cost_estimate=pl.CostEstimate(flops=1 << 20, bytes_accessed=1 << 20, transcendentals=0),
        name="plan",
    )(me, *tables, list_slots, list_kinds)


def local(children, interp_theta, interp_phi, translator, send_index, list_slots, list_kinds):
    samp_count = lax.axis_size(SAMP)
    polar_total = interp_theta.shape[1]
    azimuth_total = interp_phi.shape[1]
    child_boxes, _, rows, child_azimuth = children.shape
    own_children = child_boxes // samp_count
    parent_boxes = child_boxes // 8
    out_rows = polar_total // samp_count
    pattern = (2, out_rows, azimuth_total)

    x = children.reshape(samp_count, own_children, 2, rows, child_azimuth)
    x = lax.all_to_all(x, SAMP, split_axis=0, concat_axis=0, tiled=True)

    cosine, sine = phase_tables(polar_total, azimuth_total)
    nothing = lax.optimization_barrier(jnp.zeros((), jnp.bfloat16))
    theta, phi = interp_theta + nothing, interp_phi + nothing
    near_tables = slot_tables(send_index)
    x, theta, phi, *near_tables = lax.optimization_barrier((x, theta, phi, *near_tables))
    mine = pl.pallas_call(
        aggregate_kernel,
        out_shape=jax.ShapeDtypeStruct((samp_count, own_children // 8) + pattern, jnp.bfloat16),
        in_specs=[VMEM] * 5,
        out_specs=VMEM,
        scratch_shapes=[
            pltpu.VMEM((16 * polar_total, child_azimuth), jnp.bfloat16),
        ],
        compiler_params=pltpu.CompilerParams(vmem_limit_bytes=12 << 20),
        cost_estimate=pl.CostEstimate(flops=335 << 20, bytes_accessed=4 << 20, transcendentals=0),
        name="aggregate",
    )(x, theta, phi, cosine, sine)
    source, mine = lax.optimization_barrier((translator, mine))
    mine = lax.all_to_all(mine, SAMP, split_axis=0, concat_axis=0, tiled=True)
    staged = pl.pallas_call(
        stage_kernel,
        out_shape=pltpu.VMEM(translator.shape, translator.dtype),
        in_specs=[HBM],
        out_specs=VMEM,
        scratch_shapes=[pltpu.SemaphoreType.DMA],
        compiler_params=pltpu.CompilerParams(vmem_limit_bytes=56 << 20),
        cost_estimate=pl.CostEstimate(flops=1, bytes_accessed=5 << 20, transcendentals=0),
        name="stage",
    )(source)
    far_table = shift(near_tables[0], "y", 2)
    mine, far_table, staged = lax.optimization_barrier((mine, far_table, staged))
    own = mine.reshape((parent_boxes,) + pattern)
    after = shift(own, "y", -1)
    before = shift(own, "y", 1)
    other = shift(own, "c", 1)
    staged, own = lax.optimization_barrier((staged, own))
    params = pltpu.CompilerParams(vmem_limit_bytes=4 << 20)
    cost = pl.CostEstimate(flops=16 << 20, bytes_accessed=8 << 20, transcendentals=0)
    wide = pl.pallas_call(
        widen_kernel,
        out_shape=pltpu.VMEM(translator.shape, jnp.float32),
        in_specs=[VMEM],
        out_specs=VMEM,
        compiler_params=params,
        cost_estimate=cost,
        name="widen",
    )(staged)
    own, wide, far_table = lax.optimization_barrier((own, wide, far_table))
    lists = plan_lists((*near_tables, far_table), list_slots, list_kinds)
    own, lists = lax.optimization_barrier((own, lists))
    far = shift(own, "y", 2)

    shape = (parent_boxes,) + pattern

    def translate(k, blocks, so_far):
        first, last = k == 0, k == len(CUTS) - 2
        field = (jax.ShapeDtypeStruct if last else pltpu.VMEM)(shape, jnp.float32)
        out = [field, pltpu.VMEM((8 * parent_boxes + 1,) + pattern, jnp.float32)]
        out_specs, scratch, aliases = [HBM if last else VMEM, VMEM], [], {}
        if first:
            out.append(jax.ShapeDtypeStruct(shape, jnp.bfloat16))
            out_specs.append(HBM)
            scratch = [pltpu.SemaphoreType.DMA]
            operands = blocks
        else:
            operands = [so_far[0], *blocks, so_far[1]]
            aliases = {1 + len(operands): 1}
        if last:
            scratch = [pltpu.VMEM(shape, jnp.float32), pltpu.SemaphoreType.DMA((4,))]
        return pl.pallas_call(
            functools.partial(class_kernel, k),
            out_shape=out,
            in_specs=[SMEM] + [VMEM] * (1 + len(operands)),
            out_specs=out_specs,
            scratch_shapes=scratch,
            input_output_aliases=aliases,
            compiler_params=params,
            cost_estimate=cost,
        )(lists, wide, *operands)

    *state, parents = translate(0, [own, other], None)
    after, before, *state = lax.optimization_barrier((after, before, *state))
    across = [shift(after, "c", 1), shift(before, "c", 1)]
    state = translate(1, [after, before], state)
    state = translate(2, across, state)
    far, *state = lax.optimization_barrier((far, *state))
    across = shift(far, "c", 1)
    state = translate(3, [far], state)
    field, _ = translate(4, [across], state)
    return parents, field


def solution(mesh):
    y_count, x_count = 4, 4
    fine = Mesh(
        mesh.devices.reshape(y_count, mesh.shape["box"] // y_count, x_count, -1),
        BOX + SAMP,
    )
    return jax.shard_map(
        local,
        mesh=fine,
        in_specs=(
            P(BOX, None, SAMP, None),
            P(),
            P(),
            P(None, None, SAMP, None),
            P(BOX, None, None),
            P(BOX, None),
            P(BOX, None),
        ),
        out_specs=(P(BOX, None, SAMP, None), P(BOX, None, SAMP, None)),
        check_vma=False,
    )
```

```python
import functools
import math

import jax
import jax.numpy as jnp
from jax import lax
from jax.experimental import pallas as pl
from jax.experimental.pallas import tpu as pltpu
from jax.sharding import Mesh, PartitionSpec as P


KAPPA_H = 12.0
SAMP = ("x", "z")
BOX = ("y", "c")
WIDTH = 128
ROWS = (0, 2, 3, 4, 5, 6, 7)
CUTS = (0, 14, 22, 30, 38, 46, 54, 64)
CHUNK = 16
VMEM = pl.BlockSpec(memory_space=pltpu.VMEM)
SMEM = pl.BlockSpec(memory_space=pltpu.SMEM)
HBM = pl.BlockSpec(memory_space=pltpu.HBM)


def phase_tables(polar_total, azimuth_total):
    polar = (jnp.arange(polar_total, dtype=jnp.int32).astype(jnp.float32) + 0.5) * (
        math.pi / polar_total
    )
    azimuth = jnp.arange(azimuth_total, dtype=jnp.int32).astype(jnp.float32) * (
        2.0 * math.pi / azimuth_total
    )
    octant = jnp.arange(4, dtype=jnp.int32)
    sign_x = ((octant & 1) * 2 - 1).astype(jnp.float32)[:, None, None]
    sign_y = ((octant >> 1 & 1) * 2 - 1).astype(jnp.float32)[:, None, None]
    along_x = jnp.sin(polar)[:, None] * jnp.cos(azimuth)[None, :]
    along_y = jnp.sin(polar)[:, None] * jnp.sin(azimuth)[None, :]
    along_z = jnp.cos(polar)[:, None] + jnp.zeros((1, azimuth_total), jnp.float32)
    phase = KAPPA_H * (sign_x * along_x + sign_y * along_y - along_z)
    return jnp.cos(phase), jnp.sin(phase)


def aggregate_kernel(x_ref, theta_ref, phi_ref, cos_ref, sin_ref, out_ref, mid_ref):
    theta = jnp.transpose(theta_ref[...].astype(jnp.float32)).astype(jnp.bfloat16)
    phi = phi_ref[...]
    chunks = theta.shape[0] // CHUNK
    for p in range(out_ref.shape[1]):
        for o in range(8):
            for r in range(2):
                x = x_ref[:, p * 8 + o, r].reshape(theta.shape[1], phi.shape[0])
                mid = jnp.dot(theta, x, preferred_element_type=jnp.float32).astype(jnp.bfloat16)
                for h in range(chunks):
                    at = (h * 16 + o * 2 + r) * CHUNK
                    mid_ref[at : at + CHUNK, :] = mid[h * CHUNK : (h + 1) * CHUNK]
        for h in range(chunks):
            mid = mid_ref[h * 16 * CHUNK : (h + 1) * 16 * CHUNK, :]
            raised = jnp.dot(mid, phi, preferred_element_type=jnp.float32)
            for s in range(CHUNK // 8):
                row = h * CHUNK + s * 8
                real = imag = None
                for o in range(4):
                    c = cos_ref[o, row : row + 8, :]
                    d = sin_ref[o, row : row + 8, :]
                    ar, ai, br, bi = (
                        raised[k * CHUNK + s * 8 : k * CHUNK + s * 8 + 8]
                        for k in (2 * o, 2 * o + 1, 14 - 2 * o, 15 - 2 * o)
                    )
                    tr = c * (ar + br) - d * (ai - bi)
                    ti = d * (ar - br) + c * (ai + bi)
                    real = tr if real is None else real + tr
                    imag = ti if imag is None else imag + ti
                out_ref[row // 8, p, 0] = real.astype(jnp.bfloat16)
                out_ref[row // 8, p, 1] = imag.astype(jnp.bfloat16)


def stage_kernel(x_ref, out_ref, sem):
    copy = pltpu.make_async_copy(x_ref, out_ref, sem)
    copy.start()
    copy.wait()


def widen_kernel(x_ref, out_ref):
    def widen(k, carry):
        out_ref[k] = x_ref[k].astype(jnp.float32)
        return carry

    lax.fori_loop(0, x_ref.shape[0], widen, 0, unroll=4)


def class_kernel(k, list_ref, trans_ref, *refs):
    first, last = k == 0, k == len(CUTS) - 2
    if first:
        *blocks, out_ref, pool_ref, parents_ref, sem = refs
        store = pltpu.make_async_copy(blocks[0], parents_ref, sem)
        store.start()
    elif last:
        sum_ref, *blocks, _, final_ref, pool_ref, out_ref, sems = refs
    else:
        sum_ref, *blocks, _, out_ref, pool_ref = refs
    boxes = out_ref.shape[0]
    for i, block in enumerate(blocks):

        def widen(n, carry, block=block, start=(ROWS[k] + i) * boxes):
            pool_ref[start + n] = block[n].astype(jnp.float32)
            return carry

        lax.fori_loop(0, boxes, widen, 0, unroll=4)
    if first:
        pool_ref[pool_ref.shape[0] - 1] = jnp.zeros(pool_ref.shape[1:], jnp.float32)

    def add(b, j, acc):
        value = list_ref[b, j]
        at, kind = lax.shift_right_logical(value, 9), value & 511
        sr, si = pool_ref[at, 0], pool_ref[at, 1]
        tr, ti = trans_ref[kind, 0], trans_ref[kind, 1]
        return acc[0] + (tr * sr - ti * si), acc[1] + (tr * si + ti * sr)

    def start(b):
        if first:
            zero = jnp.zeros(out_ref.shape[2:], jnp.float32)
            return zero, zero
        begin = list_ref[boxes + b, k - 1]
        end = CUTS[k] if last else jnp.minimum(list_ref[boxes + b, k], CUTS[k])
        acc = (sum_ref[b, 0], sum_ref[b, 1])
        return lax.fori_loop(begin, end, lambda j, acc: add(b, j, acc), acc)

    def pair(i, carry):
        places = (2 * i, 2 * i + 1)
        acc = [start(b) for b in places]
        for j in range(CUTS[k], CUTS[k + 1]):
            acc = [add(b, CUTS[-1] + j, a) for b, a in zip(places, acc)]
        for b, a in zip(places, acc):
            out_ref[b, 0], out_ref[b, 1] = a
        return carry

    if not last:
        lax.fori_loop(0, boxes // 2, pair, 0)
    else:
        parts = sems.shape[0]
        size = boxes // parts
        copies = []
        for i in range(parts):
            lax.fori_loop(i * size // 2, (i + 1) * size // 2, pair, 0)
            rows = pl.ds(i * size, size)
            out = pltpu.make_async_copy(out_ref.at[rows], final_ref.at[rows], sems.at[i])
            out.start()
            copies.append(out)
        for out in copies:
            out.wait()
    if first:
        store.wait()


def shift(x, axis, step):
    size = lax.axis_size(axis)
    return lax.ppermute(x, axis, [(i, (i + step) % size) for i in range(size)])


def plan_kernel(me_ref, own_ref, after_ref, before_ref, far_ref, slots_ref, kinds_ref, *rest):
    out_ref, list_ref, sem = rest
    cores, receivers, cap = own_ref.shape
    boxes, entries = slots_ref.shape
    me = me_ref[:, :entries]
    slots = slots_ref[...]
    sender = lax.shift_right_logical(slots, 4)
    dy = (lax.shift_right_logical(sender, 1) - lax.shift_right_logical(me, 1)) & 3
    dc = (sender & 1) ^ (me & 1)
    code = (dy * cores + dc) * cap + (slots & (cap - 1))
    is_me = lax.broadcasted_iota(jnp.int32, (receivers, cap), 0) == me[:receivers, :cap]
    pieces = []
    for table, block in ((own_ref, 0), (after_ref, 4), (far_ref, 6), (before_ref, 2)):
        for core in range(cores):
            mine = jnp.sum(jnp.where(is_me, table[core], 0), axis=0, keepdims=True)
            pieces.append(mine + (block + core) * boxes)
    table = jnp.broadcast_to(jnp.concatenate(pieces, axis=1), (boxes, WIDTH))
    row = jnp.take_along_axis(table, jnp.concatenate([code, code], axis=1), axis=1)
    row = row[:, :entries]
    klass = jnp.where(dy == 3, 1, jnp.where(dy == 1, 3, 5)) + dc
    klass = jnp.where(dy == 0, 0, klass)
    first = lax.broadcasted_iota(jnp.int32, (entries, entries), 0)
    second = lax.broadcasted_iota(jnp.int32, (entries, entries), 1)
    ahead = (first < second).astype(jnp.float32)
    lane = lax.broadcasted_iota(jnp.int32, (boxes, WIDTH), 1)
    slot = lane - entries
    spot = jnp.zeros_like(slots)
    begin = jnp.zeros((boxes, 1), jnp.int32)
    keep = slot < 0
    ends = jnp.zeros((boxes, WIDTH), jnp.int32)
    for k in range(len(CUTS) - 1):
        mine = klass == k
        inside = jnp.dot(mine.astype(jnp.float32), ahead, preferred_element_type=jnp.float32)
        spot = jnp.where(mine, begin + inside.astype(jnp.int32), spot)
        begin = begin + jnp.sum(mine.astype(jnp.int32), axis=1, keepdims=True)
        keep = keep | ((slot >= CUTS[k]) & (slot < CUTS[k + 1]) & (slot < begin))
        ends = jnp.where(lane == k, begin, ends)
    value = jnp.transpose((row * 512 + kinds_ref[...]).astype(jnp.float32)).astype(jnp.int32)
    spot = jnp.transpose(spot.astype(jnp.float32)).astype(jnp.int32)
    target = lax.broadcasted_iota(jnp.int32, (entries, WIDTH), 1) & (entries - 1)
    for b in range(boxes):
        got = jnp.where(spot[:, b : b + 1] == target, value[:, b : b + 1], 0)
        list_ref[b : b + 1, :] = jnp.sum(got, axis=0, keepdims=True)
    list_ref[:boxes, :] = jnp.where(keep, list_ref[:boxes, :], 8 * boxes * 512)
    list_ref[boxes:, :] = ends
    copy = pltpu.make_async_copy(list_ref, out_ref, sem)
    copy.start()
    copy.wait()


def slot_tables(send_index):
    own = jnp.concatenate([send_index, shift(send_index, "c", 1)], axis=0)
    return own, shift(own, "y", -1), shift(own, "y", 1)


def plan_lists(tables, list_slots, list_kinds):
    boxes = list_slots.shape[0]
    me = lax.axis_index("y") * lax.axis_size("c") + lax.axis_index("c")
    me = jnp.broadcast_to(me.astype(jnp.int32), (boxes, WIDTH))
    return pl.pallas_call(
        plan_kernel,
        out_shape=pltpu.SMEM((2 * boxes, WIDTH), jnp.int32),
        in_specs=[VMEM] * 7,
        out_specs=SMEM,
        scratch_shapes=[pltpu.VMEM((2 * boxes, WIDTH), jnp.int32), pltpu.SemaphoreType.DMA],
        compiler_params=pltpu.CompilerParams(vmem_limit_bytes=4 << 20),
        cost_estimate=pl.CostEstimate(flops=1 << 20, bytes_accessed=1 << 20, transcendentals=0),
        name="plan",
    )(me, *tables, list_slots, list_kinds)


def local(children, interp_theta, interp_phi, translator, send_index, list_slots, list_kinds):
    samp_count = lax.axis_size(SAMP)
    polar_total = interp_theta.shape[1]
    azimuth_total = interp_phi.shape[1]
    child_boxes, _, rows, child_azimuth = children.shape
    own_children = child_boxes // samp_count
    parent_boxes = child_boxes // 8
    out_rows = polar_total // samp_count
    pattern = (2, out_rows, azimuth_total)

    x = children.reshape(samp_count, own_children, 2, rows, child_azimuth)
    x = lax.all_to_all(x, SAMP, split_axis=0, concat_axis=0, tiled=True)

    cosine, sine = phase_tables(polar_total, azimuth_total)
    nothing = lax.optimization_barrier(jnp.zeros((), jnp.bfloat16))
    theta, phi = interp_theta + nothing, interp_phi + nothing
    near_tables = slot_tables(send_index)
    x, theta, phi, *near_tables = lax.optimization_barrier((x, theta, phi, *near_tables))
    mine = pl.pallas_call(
        aggregate_kernel,
        out_shape=jax.ShapeDtypeStruct((samp_count, own_children // 8) + pattern, jnp.bfloat16),
        in_specs=[VMEM] * 5,
        out_specs=VMEM,
        scratch_shapes=[
            pltpu.VMEM((16 * polar_total, child_azimuth), jnp.bfloat16),
        ],
        compiler_params=pltpu.CompilerParams(vmem_limit_bytes=12 << 20),
        cost_estimate=pl.CostEstimate(flops=335 << 20, bytes_accessed=4 << 20, transcendentals=0),
        name="aggregate",
    )(x, theta, phi, cosine, sine)
    source, mine = lax.optimization_barrier((translator, mine))
    mine = lax.all_to_all(mine, SAMP, split_axis=0, concat_axis=0, tiled=True)
    staged = pl.pallas_call(
        stage_kernel,
        out_shape=pltpu.VMEM(translator.shape, translator.dtype),
        in_specs=[HBM],
        out_specs=VMEM,
        scratch_shapes=[pltpu.SemaphoreType.DMA],
        compiler_params=pltpu.CompilerParams(vmem_limit_bytes=56 << 20),
        cost_estimate=pl.CostEstimate(flops=1, bytes_accessed=5 << 20, transcendentals=0),
        name="stage",
    )(source)
    far_table = shift(near_tables[0], "y", 2)
    mine, far_table, staged = lax.optimization_barrier((mine, far_table, staged))
    own = mine.reshape((parent_boxes,) + pattern)
    after = shift(own, "y", -1)
    before = shift(own, "y", 1)
    other = shift(own, "c", 1)
    staged, own = lax.optimization_barrier((staged, own))
    params = pltpu.CompilerParams(vmem_limit_bytes=4 << 20)
    cost = pl.CostEstimate(flops=16 << 20, bytes_accessed=8 << 20, transcendentals=0)
    wide = pl.pallas_call(
        widen_kernel,
        out_shape=pltpu.VMEM(translator.shape, jnp.float32),
        in_specs=[VMEM],
        out_specs=VMEM,
        compiler_params=params,
        cost_estimate=cost,
        name="widen",
    )(staged)
    own, wide, far_table = lax.optimization_barrier((own, wide, far_table))
    lists = plan_lists((*near_tables, far_table), list_slots, list_kinds)
    far = shift(own, "y", 2)

    shape = (parent_boxes,) + pattern

    def translate(k, blocks, so_far):
        first, last = k == 0, k == len(CUTS) - 2
        field = (jax.ShapeDtypeStruct if last else pltpu.VMEM)(shape, jnp.float32)
        out = [field, pltpu.VMEM((8 * parent_boxes + 1,) + pattern, jnp.float32)]
        out_specs, scratch, aliases = [HBM if last else VMEM, VMEM], [], {}
        if first:
            out.append(jax.ShapeDtypeStruct(shape, jnp.bfloat16))
            out_specs.append(HBM)
            scratch = [pltpu.SemaphoreType.DMA]
            operands = blocks
        else:
            operands = [so_far[0], *blocks, so_far[1]]
            aliases = {1 + len(operands): 1}
        if last:
            scratch = [pltpu.VMEM(shape, jnp.float32), pltpu.SemaphoreType.DMA((4,))]
        return pl.pallas_call(
            functools.partial(class_kernel, k),
            out_shape=out,
            in_specs=[SMEM] + [VMEM] * (1 + len(operands)),
            out_specs=out_specs,
            scratch_shapes=scratch,
            input_output_aliases=aliases,
            compiler_params=params,
            cost_estimate=cost,
        )(lists, wide, *operands)

    *state, parents = translate(0, [own, other], None)
    for k, block in ((1, before), (3, after), (5, far)):
        block, *state = lax.optimization_barrier((block, *state))
        across = shift(block, "c", 1)
        state = translate(k, [block], state)
        state = translate(k + 1, [across], state)
    field, _ = state
    return parents, field


def solution(mesh):
    y_count, x_count = 4, 4
    fine = Mesh(
        mesh.devices.reshape(y_count, mesh.shape["box"] // y_count, x_count, -1),
        BOX + SAMP,
    )
    return jax.shard_map(
        local,
        mesh=fine,
        in_specs=(
            P(BOX, None, SAMP, None),
            P(),
            P(),
            P(None, None, SAMP, None),
            P(BOX, None, None),
            P(BOX, None),
            P(BOX, None),
        ),
        out_specs=(P(BOX, None, SAMP, None), P(BOX, None, SAMP, None)),
        check_vma=False,
    )
```

```python
import functools
import math

import jax
import jax.numpy as jnp
from jax import lax
from jax.experimental import pallas as pl
from jax.experimental.pallas import tpu as pltpu
from jax.sharding import Mesh, PartitionSpec as P


KAPPA_H = 12.0
SAMP = ("x", "z")
BOX = ("y", "c")
WIDTH = 128
ROWS = (0, 2, 4, 6, 7)
CUTS = (0, 14, 28, 46, 54, 64)
CHUNK = 16
VMEM = pl.BlockSpec(memory_space=pltpu.VMEM)
SMEM = pl.BlockSpec(memory_space=pltpu.SMEM)
HBM = pl.BlockSpec(memory_space=pltpu.HBM)


def phase_tables(polar_total, azimuth_total):
    polar = (jnp.arange(polar_total, dtype=jnp.int32).astype(jnp.float32) + 0.5) * (
        math.pi / polar_total
    )
    azimuth = jnp.arange(azimuth_total, dtype=jnp.int32).astype(jnp.float32) * (
        2.0 * math.pi / azimuth_total
    )
    along_x = KAPPA_H * jnp.sin(polar)[:, None] * jnp.cos(azimuth)[None, :]
    along_y = KAPPA_H * jnp.sin(polar)[:, None] * jnp.sin(azimuth)[None, :]
    along_z = (KAPPA_H * jnp.cos(polar))[:, None]
    parts = (jnp.cos(along_x), jnp.sin(along_x), jnp.cos(along_y), jnp.sin(along_y))
    cos_x, sin_x, cos_y, sin_y = lax.optimization_barrier(parts)
    octant = jnp.arange(4, dtype=jnp.int32)
    sign_x = ((octant & 1) * 2 - 1).astype(jnp.float32)[:, None, None]
    sign_y = ((octant >> 1 & 1) * 2 - 1).astype(jnp.float32)[:, None, None]
    x, y = (cos_x[None], sign_x * sin_x), (cos_y[None], sign_y * sin_y)
    return turn(turn(x, y), (jnp.cos(along_z), -jnp.sin(along_z)))


def turn(a, b):
    return a[0] * b[0] - a[1] * b[1], a[1] * b[0] + a[0] * b[1]


def prepare_kernel(theta_hbm, phi_hbm, turned_ref, phi_ref, theta_ref, sems):
    copies = [
        pltpu.make_async_copy(theta_hbm, theta_ref, sems.at[0]),
        pltpu.make_async_copy(phi_hbm, phi_ref, sems.at[1]),
    ]
    for copy in copies:
        copy.start()
    for copy in copies:
        copy.wait()
    turned_ref[...] = jnp.transpose(theta_ref[...].astype(jnp.float32)).astype(jnp.bfloat16)


def aggregate_kernel(x_ref, theta_ref, phi_ref, cos_ref, sin_ref, out_ref, mid_ref):
    theta = theta_ref[...]
    phi = phi_ref[...]
    chunks = theta.shape[0] // CHUNK
    for p in range(out_ref.shape[1]):
        for o in range(8):
            for r in range(2):
                x = x_ref[:, p * 8 + o, r].reshape(theta.shape[1], phi.shape[0])
                mid = jnp.dot(theta, x, preferred_element_type=jnp.float32).astype(jnp.bfloat16)
                for h in range(chunks):
                    at = (h * 16 + o * 2 + r) * CHUNK
                    mid_ref[at : at + CHUNK, :] = mid[h * CHUNK : (h + 1) * CHUNK]
        for h in range(chunks):
            mid = mid_ref[h * 16 * CHUNK : (h + 1) * 16 * CHUNK, :]
            raised = jnp.dot(mid, phi, preferred_element_type=jnp.float32)
            for s in range(CHUNK // 8):
                row = h * CHUNK + s * 8
                real = imag = None
                for o in range(4):
                    c = cos_ref[o, row : row + 8, :]
                    d = sin_ref[o, row : row + 8, :]
                    ar, ai, br, bi = (
                        raised[k * CHUNK + s * 8 : k * CHUNK + s * 8 + 8]
                        for k in (2 * o, 2 * o + 1, 14 - 2 * o, 15 - 2 * o)
                    )
                    tr = c * (ar + br) - d * (ai - bi)
                    ti = d * (ar - br) + c * (ai + bi)
                    real = tr if real is None else real + tr
                    imag = ti if imag is None else imag + ti
                out_ref[row // 8, p, 0] = real.astype(jnp.bfloat16)
                out_ref[row // 8, p, 1] = imag.astype(jnp.bfloat16)


def stage_kernel(x_ref, out_ref, sem):
    copy = pltpu.make_async_copy(x_ref, out_ref, sem)
    copy.start()
    copy.wait()


def widen_kernel(x_ref, out_ref):
    def widen(k, carry):
        out_ref[k] = x_ref[k].astype(jnp.float32)
        return carry

    lax.fori_loop(0, x_ref.shape[0], widen, 0, unroll=4)


def class_kernel(k, list_ref, trans_ref, *refs):
    first, last = k == 0, k == len(CUTS) - 2
    if first:
        *blocks, out_ref, pool_ref, parents_ref, sem = refs
        store = pltpu.make_async_copy(blocks[0], parents_ref, sem)
        store.start()
    elif last:
        sum_ref, *blocks, _, final_ref, pool_ref, out_ref, sems = refs
    else:
        sum_ref, *blocks, _, out_ref, pool_ref = refs
    boxes = out_ref.shape[0]
    groups = [blocks] if k > 2 else [[block] for block in blocks]
    for i, group in enumerate(groups):

        def widen(n, carry, group=group, start=(ROWS[k] + i) * boxes):
            pool_ref[start + n] = sum(block[n].astype(jnp.float32) for block in group)
            return carry

        lax.fori_loop(0, boxes, widen, 0, unroll=4)
    if first:
        pool_ref[pool_ref.shape[0] - 1] = jnp.zeros(pool_ref.shape[1:], jnp.float32)

    def add(b, j, acc):
        value = list_ref[b, j]
        at, kind = lax.shift_right_logical(value, 9), value & 511
        sr, si = pool_ref[at, 0], pool_ref[at, 1]
        tr, ti = trans_ref[kind, 0], trans_ref[kind, 1]
        return acc[0] + (tr * sr - ti * si), acc[1] + (tr * si + ti * sr)

    def start(b):
        if first:
            zero = jnp.zeros(out_ref.shape[2:], jnp.float32)
            return zero, zero
        begin = list_ref[boxes + b, k - 1]
        end = CUTS[k] if last else jnp.minimum(list_ref[boxes + b, k], CUTS[k])
        acc = (sum_ref[b, 0], sum_ref[b, 1])
        return lax.fori_loop(begin, end, lambda j, acc: add(b, j, acc), acc)

    def pair(i, carry):
        places = (2 * i, 2 * i + 1)
        acc = [start(b) for b in places]
        for j in range(CUTS[k], CUTS[k + 1]):
            acc = [add(b, CUTS[-1] + j, a) for b, a in zip(places, acc)]
        for b, a in zip(places, acc):
            out_ref[b, 0], out_ref[b, 1] = a
        return carry

    if not last:
        lax.fori_loop(0, boxes // 2, pair, 0)
    else:
        parts = sems.shape[0]
        size = boxes // parts
        copies = []
        for i in range(parts):
            lax.fori_loop(i * size // 2, (i + 1) * size // 2, pair, 0)
            rows = pl.ds(i * size, size)
            out = pltpu.make_async_copy(out_ref.at[rows], final_ref.at[rows], sems.at[i])
            out.start()
            copies.append(out)
        for out in copies:
            out.wait()
    if first:
        store.wait()


def shift(x, axis, step):
    size = lax.axis_size(axis)
    return lax.ppermute(x, axis, [(i, (i + step) % size) for i in range(size)])


def plan_kernel(me_ref, own_ref, after_ref, before_ref, far_ref, slots_ref, kinds_ref, *rest):
    out_ref, list_ref, sem = rest
    cores, receivers, cap = own_ref.shape
    boxes, entries = slots_ref.shape
    me = me_ref[:, :entries]
    slots = slots_ref[...]
    sender = lax.shift_right_logical(slots, 4)
    dy = (lax.shift_right_logical(sender, 1) - lax.shift_right_logical(me, 1)) & 3
    dc = (sender & 1) ^ (me & 1)
    code = (dy * cores + dc) * cap + (slots & (cap - 1))
    is_me = lax.broadcasted_iota(jnp.int32, (receivers, cap), 0) == me[:receivers, :cap]
    pieces = []
    side = me[:1, :cap] & 1
    for table, block in ((own_ref, (0, 1)), (after_ref, (2, 4)), (far_ref, None), (before_ref, (3, 5))):
        for core in range(cores):
            mine = jnp.sum(jnp.where(is_me, table[core], 0), axis=0, keepdims=True)
            pieces.append(mine + ((6 + (side ^ core)) if block is None else block[core]) * boxes)
    table = jnp.broadcast_to(jnp.concatenate(pieces, axis=1), (boxes, WIDTH))
    row = jnp.take_along_axis(table, jnp.concatenate([code, code], axis=1), axis=1)
    row = row[:, :entries]
    klass = jnp.where(dy == 2, 3 + (sender & 1), jnp.where(dy == 0, 0, 1 + dc))
    first = lax.broadcasted_iota(jnp.int32, (entries, entries), 0)
    second = lax.broadcasted_iota(jnp.int32, (entries, entries), 1)
    ahead = (first < second).astype(jnp.float32)
    lane = lax.broadcasted_iota(jnp.int32, (boxes, WIDTH), 1)
    slot = lane - entries
    spot = jnp.zeros_like(slots)
    begin = jnp.zeros((boxes, 1), jnp.int32)
    keep = slot < 0
    ends = jnp.zeros((boxes, WIDTH), jnp.int32)
    for k in range(len(CUTS) - 1):
        mine = klass == k
        inside = jnp.dot(mine.astype(jnp.float32), ahead, preferred_element_type=jnp.float32)
        spot = jnp.where(mine, begin + inside.astype(jnp.int32), spot)
        begin = begin + jnp.sum(mine.astype(jnp.int32), axis=1, keepdims=True)
        keep = keep | ((slot >= CUTS[k]) & (slot < CUTS[k + 1]) & (slot < begin))
        ends = jnp.where(lane == k, begin, ends)
    value = jnp.transpose((row * 512 + kinds_ref[...]).astype(jnp.float32)).astype(jnp.int32)
    spot = jnp.transpose(spot.astype(jnp.float32)).astype(jnp.int32)
    target = lax.broadcasted_iota(jnp.int32, (entries, WIDTH), 1) & (entries - 1)
    for b in range(boxes):
        got = jnp.where(spot[:, b : b + 1] == target, value[:, b : b + 1], 0)
        list_ref[b : b + 1, :] = jnp.sum(got, axis=0, keepdims=True)
    list_ref[:boxes, :] = jnp.where(keep, list_ref[:boxes, :], 8 * boxes * 512)
    list_ref[boxes:, :] = ends
    copy = pltpu.make_async_copy(list_ref, out_ref, sem)
    copy.start()
    copy.wait()


def some_pairs(x, pairs, core):
    cores = lax.axis_size("c")
    pairs = [(a * cores + core, b * cores + core) for a, b in pairs]
    return lax.ppermute(x, BOX, pairs)


def slot_tables(send_index):
    own = jnp.concatenate([send_index, shift(send_index, "c", 1)], axis=0)
    return own, shift(own, "y", -1), shift(own, "y", 1)


def plan_lists(me, tables, list_slots, list_kinds):
    boxes = list_slots.shape[0]
    return pl.pallas_call(
        plan_kernel,
        out_shape=pltpu.SMEM((2 * boxes, WIDTH), jnp.int32),
        in_specs=[VMEM] * 7,
        out_specs=SMEM,
        scratch_shapes=[pltpu.VMEM((2 * boxes, WIDTH), jnp.int32), pltpu.SemaphoreType.DMA],
        compiler_params=pltpu.CompilerParams(vmem_limit_bytes=4 << 20),
        cost_estimate=pl.CostEstimate(flops=1 << 20, bytes_accessed=1 << 20, transcendentals=0),
        name="plan",
    )(me, *tables, list_slots, list_kinds)


def local(children, interp_theta, interp_phi, translator, send_index, list_slots, list_kinds):
    samp_count = lax.axis_size(SAMP)
    polar_total = interp_theta.shape[1]
    azimuth_total = interp_phi.shape[1]
    child_boxes, _, rows, child_azimuth = children.shape
    own_children = child_boxes // samp_count
    parent_boxes = child_boxes // 8
    out_rows = polar_total // samp_count
    pattern = (2, out_rows, azimuth_total)

    x = children.reshape(samp_count, own_children, 2, rows, child_azimuth)
    x = lax.all_to_all(x, SAMP, split_axis=0, concat_axis=0, tiled=True)

    cosine, sine = phase_tables(polar_total, azimuth_total)
    theta, phi = pl.pallas_call(
        prepare_kernel,
        out_shape=[
            pltpu.VMEM(interp_theta.shape[::-1], jnp.bfloat16),
            pltpu.VMEM(interp_phi.shape, jnp.bfloat16),
        ],
        in_specs=[HBM] * 2,
        out_specs=[VMEM] * 2,
        scratch_shapes=[
            pltpu.VMEM(interp_theta.shape, jnp.bfloat16),
            pltpu.SemaphoreType.DMA((2,)),
        ],
        compiler_params=pltpu.CompilerParams(vmem_limit_bytes=61 << 20),
        cost_estimate=pl.CostEstimate(flops=1 << 20, bytes_accessed=1 << 18, transcendentals=0),
        name="prepare",
    )(interp_theta, interp_phi)
    me = lax.axis_index("y") * lax.axis_size("c") + lax.axis_index("c")
    me = jnp.broadcast_to(me.astype(jnp.int32), (parent_boxes, WIDTH))
    near_tables = slot_tables(send_index)
    x, theta, phi, me, *near_tables = lax.optimization_barrier((x, theta, phi, me, *near_tables))
    mine = pl.pallas_call(
        aggregate_kernel,
        out_shape=jax.ShapeDtypeStruct((samp_count, own_children // 8) + pattern, jnp.bfloat16),
        in_specs=[VMEM] * 5,
        out_specs=VMEM,
        scratch_shapes=[
            pltpu.VMEM((16 * polar_total, child_azimuth), jnp.bfloat16),
        ],
        compiler_params=pltpu.CompilerParams(vmem_limit_bytes=12 << 20),
        cost_estimate=pl.CostEstimate(flops=335 << 20, bytes_accessed=4 << 20, transcendentals=0),
        name="aggregate",
    )(x, theta, phi, cosine, sine)
    source, mine = lax.optimization_barrier((translator, mine))
    mine = lax.all_to_all(mine, SAMP, split_axis=0, concat_axis=0, tiled=True)
    staged = pl.pallas_call(
        stage_kernel,
        out_shape=pltpu.VMEM(translator.shape, translator.dtype),
        in_specs=[HBM],
        out_specs=VMEM,
        scratch_shapes=[pltpu.SemaphoreType.DMA],
        compiler_params=pltpu.CompilerParams(vmem_limit_bytes=56 << 20),
        cost_estimate=pl.CostEstimate(flops=1, bytes_accessed=5 << 20, transcendentals=0),
        name="stage",
    )(source)
    far_table = shift(near_tables[0], "y", 2)
    mine, far_table, staged = lax.optimization_barrier((mine, far_table, staged))
    own = mine.reshape((parent_boxes,) + pattern)
    after = shift(own, "y", -1)
    before = shift(own, "y", 1)
    other = shift(own, "c", 1)
    staged, own = lax.optimization_barrier((staged, own))
    params = pltpu.CompilerParams(vmem_limit_bytes=4 << 20)
    cost = pl.CostEstimate(flops=16 << 20, bytes_accessed=8 << 20, transcendentals=0)
    wide = pl.pallas_call(
        widen_kernel,
        out_shape=pltpu.VMEM(translator.shape, jnp.float32),
        in_specs=[VMEM],
        out_specs=VMEM,
        compiler_params=params,
        cost_estimate=cost,
        name="widen",
    )(staged)
    own, wide, far_table = lax.optimization_barrier((own, wide, far_table))
    lists = plan_lists(me, (*near_tables, far_table), list_slots, list_kinds)
    far = some_pairs(own, [(y, (y + 2) % 4) for y in range(4)], 0)

    shape = (parent_boxes,) + pattern

    def translate(k, blocks, so_far):
        first, last = k == 0, k == len(CUTS) - 2
        field = (jax.ShapeDtypeStruct if last else pltpu.VMEM)(shape, jnp.float32)
        out = [field, pltpu.VMEM((8 * parent_boxes + 1,) + pattern, jnp.float32)]
        out_specs, scratch, aliases = [HBM if last else VMEM, VMEM], [], {}
        if first:
            out.append(jax.ShapeDtypeStruct(shape, jnp.bfloat16))
            out_specs.append(HBM)
            scratch = [pltpu.SemaphoreType.DMA]
            operands = blocks
        else:
            operands = [so_far[0], *blocks, so_far[1]]
            aliases = {1 + len(operands): 1}
        if last:
            scratch = [pltpu.VMEM(shape, jnp.float32), pltpu.SemaphoreType.DMA((4,))]
        return pl.pallas_call(
            functools.partial(class_kernel, k),
            out_shape=out,
            in_specs=[SMEM] + [VMEM] * (1 + len(operands)),
            out_specs=out_specs,
            scratch_shapes=scratch,
            input_output_aliases=aliases,
            compiler_params=params,
            cost_estimate=cost,
        )(lists, wide, *operands)

    *state, parents = translate(0, [own, other], None)
    after, before, *state = lax.optimization_barrier((after, before, *state))
    up = some_pairs(before, ((1, 2), (2, 3)), 1)
    down = some_pairs(after, ((1, 0), (2, 1)), 1)
    across = [shift(after, "c", 1), shift(before, "c", 1)]
    state = translate(1, [after, before], state)
    far, *state = lax.optimization_barrier((far, *state))
    far_across = shift(far, "c", 1)
    state = translate(2, across, state)
    state = translate(3, [far, far_across], state)
    up, down, *state = lax.optimization_barrier((up, down, *state))
    relayed = [up, down]
    relayed += [shift(v, "c", 1) for v in relayed]
    field, _ = translate(4, relayed, state)
    return parents, field


def solution(mesh):
    y_count, x_count = 4, 4
    fine = Mesh(
        mesh.devices.reshape(y_count, mesh.shape["box"] // y_count, x_count, -1),
        BOX + SAMP,
    )
    return jax.shard_map(
        local,
        mesh=fine,
        in_specs=(
            P(BOX, None, SAMP, None),
            P(),
            P(),
            P(None, None, SAMP, None),
            P(BOX, None, None),
            P(BOX, None),
            P(BOX, None),
        ),
        out_specs=(P(BOX, None, SAMP, None), P(BOX, None, SAMP, None)),
        check_vma=False,
    )
```

```python
import functools
import math

import jax
import jax.numpy as jnp
from jax import lax
from jax.experimental import pallas as pl
from jax.experimental.pallas import tpu as pltpu
from jax.sharding import Mesh, PartitionSpec as P


KAPPA_H = 12.0
SAMP = ("x", "z")
BOX = ("y", "c")
WIDTH = 128
ROWS = (0, 2, 4, 0, 1)
FAR = 3
CUTS = (0, 14, 28, 46, 54, 64)
CHUNK = 16
VMEM = pl.BlockSpec(memory_space=pltpu.VMEM)
SMEM = pl.BlockSpec(memory_space=pltpu.SMEM)
HBM = pl.BlockSpec(memory_space=pltpu.HBM)


def phase_tables(polar_total, azimuth_total):
    polar = (jnp.arange(polar_total, dtype=jnp.int32).astype(jnp.float32) + 0.5) * (
        math.pi / polar_total
    )
    azimuth = jnp.arange(azimuth_total, dtype=jnp.int32).astype(jnp.float32) * (
        2.0 * math.pi / azimuth_total
    )
    along_x = KAPPA_H * jnp.sin(polar)[:, None] * jnp.cos(azimuth)[None, :]
    along_y = KAPPA_H * jnp.sin(polar)[:, None] * jnp.sin(azimuth)[None, :]
    along_z = (KAPPA_H * jnp.cos(polar))[:, None]
    parts = (jnp.cos(along_x), jnp.sin(along_x), jnp.cos(along_y), jnp.sin(along_y))
    cos_x, sin_x, cos_y, sin_y = lax.optimization_barrier(parts)
    octant = jnp.arange(4, dtype=jnp.int32)
    sign_x = ((octant & 1) * 2 - 1).astype(jnp.float32)[:, None, None]
    sign_y = ((octant >> 1 & 1) * 2 - 1).astype(jnp.float32)[:, None, None]
    x, y = (cos_x[None], sign_x * sin_x), (cos_y[None], sign_y * sin_y)
    return turn(turn(x, y), (jnp.cos(along_z), -jnp.sin(along_z)))


def turn(a, b):
    return a[0] * b[0] - a[1] * b[1], a[1] * b[0] + a[0] * b[1]


def prepare_kernel(theta_hbm, phi_hbm, turned_ref, phi_ref, theta_ref, sems):
    copies = [
        pltpu.make_async_copy(theta_hbm, theta_ref, sems.at[0]),
        pltpu.make_async_copy(phi_hbm, phi_ref, sems.at[1]),
    ]
    for copy in copies:
        copy.start()
    for copy in copies:
        copy.wait()
    turned_ref[...] = jnp.transpose(theta_ref[...].astype(jnp.float32)).astype(jnp.bfloat16)


def aggregate_kernel(x_ref, theta_ref, phi_ref, cos_ref, sin_ref, out_ref, mid_ref):
    theta = theta_ref[...]
    phi = phi_ref[...]
    chunks = theta.shape[0] // CHUNK
    for p in range(out_ref.shape[1]):
        for o in range(8):
            for r in range(2):
                x = x_ref[:, p * 8 + o, r].reshape(theta.shape[1], phi.shape[0])
                mid = jnp.dot(theta, x, preferred_element_type=jnp.float32).astype(jnp.bfloat16)
                for h in range(chunks):
                    at = (h * 16 + o * 2 + r) * CHUNK
                    mid_ref[at : at + CHUNK, :] = mid[h * CHUNK : (h + 1) * CHUNK]
        for h in range(chunks):
            mid = mid_ref[h * 16 * CHUNK : (h + 1) * 16 * CHUNK, :]
            raised = jnp.dot(mid, phi, preferred_element_type=jnp.float32)
            for s in range(CHUNK // 8):
                row = h * CHUNK + s * 8
                real = imag = None
                for o in range(4):
                    c = cos_ref[o, row : row + 8, :]
                    d = sin_ref[o, row : row + 8, :]
                    ar, ai, br, bi = (
                        raised[k * CHUNK + s * 8 : k * CHUNK + s * 8 + 8]
                        for k in (2 * o, 2 * o + 1, 14 - 2 * o, 15 - 2 * o)
                    )
                    tr = c * (ar + br) - d * (ai - bi)
                    ti = d * (ar - br) + c * (ai + bi)
                    real = tr if real is None else real + tr
                    imag = ti if imag is None else imag + ti
                out_ref[row // 8, p, 0] = real.astype(jnp.bfloat16)
                out_ref[row // 8, p, 1] = imag.astype(jnp.bfloat16)


def stage_kernel(x_ref, out_ref, sem):
    copy = pltpu.make_async_copy(x_ref, out_ref, sem)
    copy.start()
    copy.wait()


def widen_kernel(x_ref, out_ref):
    def widen(k, carry):
        out_ref[k] = x_ref[k].astype(jnp.float32)
        return carry

    lax.fori_loop(0, x_ref.shape[0], widen, 0, unroll=4)


def class_kernel(k, list_ref, trans_ref, *refs):
    first, last = k == 0, k == len(CUTS) - 2
    if first:
        *blocks, out_ref, pool_ref, parents_ref, sem = refs
        store = pltpu.make_async_copy(blocks[0], parents_ref, sem)
        store.start()
    elif last:
        sum_ref, *blocks, _, final_ref, pool_ref, out_ref, sems = refs
    elif k == FAR:
        sum_ref, *blocks, out_ref, pool_ref = refs
    else:
        sum_ref, *blocks, _, out_ref, pool_ref = refs
    boxes = out_ref.shape[0]
    for i, block in enumerate(blocks):

        def widen(n, carry, block=block, start=(ROWS[k] + i) * boxes):
            pool_ref[start + n] = block[n].astype(jnp.float32)
            return carry

        lax.fori_loop(0, boxes, widen, 0, unroll=4)
    if k in (0, FAR):
        pool_ref[pool_ref.shape[0] - 1] = jnp.zeros(pool_ref.shape[1:], jnp.float32)

    def add(b, j, acc):
        value = list_ref[b, j]
        at, kind = lax.shift_right_logical(value, 9), value & 511
        sr, si = pool_ref[at, 0], pool_ref[at, 1]
        tr, ti = trans_ref[kind, 0], trans_ref[kind, 1]
        return acc[0] + (tr * sr - ti * si), acc[1] + (tr * si + ti * sr)

    def start(b):
        if first:
            zero = jnp.zeros(out_ref.shape[2:], jnp.float32)
            return zero, zero
        begin = list_ref[boxes + b, k - 1]
        end = CUTS[k] if last else jnp.minimum(list_ref[boxes + b, k], CUTS[k])
        acc = (sum_ref[b, 0], sum_ref[b, 1])
        acc = lax.fori_loop(begin, end, lambda j, acc: add(b, j, acc), acc)
        if k == FAR - 1:
            end = list_ref[boxes + b, k]
            acc = lax.fori_loop(CUTS[FAR], end, lambda j, acc: add(b, j, acc), acc)
        return acc

    def pair(i, carry):
        places = (2 * i, 2 * i + 1)
        acc = [start(b) for b in places]
        for j in range(CUTS[k], CUTS[k + 1]):
            acc = [add(b, CUTS[-1] + j, a) for b, a in zip(places, acc)]
        for b, a in zip(places, acc):
            out_ref[b, 0], out_ref[b, 1] = a
        return carry

    if not last:
        lax.fori_loop(0, boxes // 2, pair, 0)
    else:
        parts = sems.shape[0]
        size = boxes // parts
        copies = []
        for i in range(parts):
            lax.fori_loop(i * size // 2, (i + 1) * size // 2, pair, 0)
            rows = pl.ds(i * size, size)
            out = pltpu.make_async_copy(out_ref.at[rows], final_ref.at[rows], sems.at[i])
            out.start()
            copies.append(out)
        for out in copies:
            out.wait()
    if first:
        store.wait()


def shift(x, axis, step):
    size = lax.axis_size(axis)
    return lax.ppermute(x, axis, [(i, (i + step) % size) for i in range(size)])


def plan_kernel(me_ref, own_ref, after_ref, before_ref, far_ref, slots_ref, kinds_ref, *rest):
    out_ref, list_ref, sem = rest
    cores, receivers, cap = own_ref.shape
    boxes, entries = slots_ref.shape
    me = me_ref[:, :entries]
    slots = slots_ref[...]
    sender = lax.shift_right_logical(slots, 4)
    dy = (lax.shift_right_logical(sender, 1) - lax.shift_right_logical(me, 1)) & 3
    dc = (sender & 1) ^ (me & 1)
    code = (dy * cores + dc) * cap + (slots & (cap - 1))
    is_me = lax.broadcasted_iota(jnp.int32, (receivers, cap), 0) == me[:receivers, :cap]
    pieces = []
    for table, block, step in (
        (own_ref, 0, 1),
        (after_ref, 2, 2),
        (far_ref, 0, 1),
        (before_ref, 3, 2),
    ):
        for core in range(cores):
            mine = jnp.sum(jnp.where(is_me, table[core], 0), axis=0, keepdims=True)
            pieces.append(mine + (block + step * core) * boxes)
    table = jnp.broadcast_to(jnp.concatenate(pieces, axis=1), (boxes, WIDTH))
    row = jnp.take_along_axis(table, jnp.concatenate([code, code], axis=1), axis=1)
    row = row[:, :entries]
    klass = jnp.where(dy == 0, 0, jnp.where(dy == 2, 3, 1) + dc)
    first = lax.broadcasted_iota(jnp.int32, (entries, entries), 0)
    second = lax.broadcasted_iota(jnp.int32, (entries, entries), 1)
    ahead = (first < second).astype(jnp.float32)
    lane = lax.broadcasted_iota(jnp.int32, (boxes, WIDTH), 1)
    slot = lane - entries
    spot = jnp.zeros_like(slots)
    begin = jnp.zeros((boxes, 1), jnp.int32)
    keep = slot < 0
    ends = jnp.zeros((boxes, WIDTH), jnp.int32)
    for k in range(len(CUTS) - 1):
        mine = klass == k
        inside = jnp.dot(mine.astype(jnp.float32), ahead, preferred_element_type=jnp.float32)
        spot = jnp.where(mine, begin + inside.astype(jnp.int32), spot)
        begin = begin + jnp.sum(mine.astype(jnp.int32), axis=1, keepdims=True)
        here = (slot >= CUTS[k]) & (slot < CUTS[k + 1]) & (slot < begin)
        if k < FAR:
            near_end = begin
        else:
            here = here & (slot >= near_end)
        keep = keep | here
        ends = jnp.where(lane == k, begin, ends)
    value = jnp.transpose((row * 512 + kinds_ref[...]).astype(jnp.float32)).astype(jnp.int32)
    spot = jnp.transpose(spot.astype(jnp.float32)).astype(jnp.int32)
    target = lax.broadcasted_iota(jnp.int32, (entries, WIDTH), 1) & (entries - 1)
    for b in range(boxes):
        got = jnp.where(spot[:, b : b + 1] == target, value[:, b : b + 1], 0)
        list_ref[b : b + 1, :] = jnp.sum(got, axis=0, keepdims=True)
    zero_row = jnp.where(slot < CUTS[FAR], 6 * boxes, 2 * boxes)
    list_ref[:boxes, :] = jnp.where(keep, list_ref[:boxes, :], zero_row * 512)
    list_ref[boxes:, :] = ends
    copy = pltpu.make_async_copy(list_ref, out_ref, sem)
    copy.start()
    copy.wait()


def slot_tables(send_index):
    own = jnp.concatenate([send_index, shift(send_index, "c", 1)], axis=0)
    return own, shift(own, "y", -1), shift(own, "y", 1)


def plan_lists(me, tables, list_slots, list_kinds):
    boxes = list_slots.shape[0]
    return pl.pallas_call(
        plan_kernel,
        out_shape=pltpu.SMEM((2 * boxes, WIDTH), jnp.int32),
        in_specs=[VMEM] * 7,
        out_specs=SMEM,
        scratch_shapes=[pltpu.VMEM((2 * boxes, WIDTH), jnp.int32), pltpu.SemaphoreType.DMA],
        compiler_params=pltpu.CompilerParams(vmem_limit_bytes=4 << 20),
        cost_estimate=pl.CostEstimate(flops=1 << 20, bytes_accessed=1 << 20, transcendentals=0),
        name="plan",
    )(me, *tables, list_slots, list_kinds)


def local(children, interp_theta, interp_phi, translator, send_index, list_slots, list_kinds):
    samp_count = lax.axis_size(SAMP)
    polar_total = interp_theta.shape[1]
    azimuth_total = interp_phi.shape[1]
    child_boxes, _, rows, child_azimuth = children.shape
    own_children = child_boxes // samp_count
    parent_boxes = child_boxes // 8
    out_rows = polar_total // samp_count
    pattern = (2, out_rows, azimuth_total)

    x = children.reshape(samp_count, own_children, 2, rows, child_azimuth)
    x = lax.all_to_all(x, SAMP, split_axis=0, concat_axis=0, tiled=True)

    cosine, sine = phase_tables(polar_total, azimuth_total)
    theta, phi = pl.pallas_call(
        prepare_kernel,
        out_shape=[
            pltpu.VMEM(interp_theta.shape[::-1], jnp.bfloat16),
            pltpu.VMEM(interp_phi.shape, jnp.bfloat16),
        ],
        in_specs=[HBM] * 2,
        out_specs=[VMEM] * 2,
        scratch_shapes=[
            pltpu.VMEM(interp_theta.shape, jnp.bfloat16),
            pltpu.SemaphoreType.DMA((2,)),
        ],
        compiler_params=pltpu.CompilerParams(vmem_limit_bytes=61 << 20),
        cost_estimate=pl.CostEstimate(flops=1 << 20, bytes_accessed=1 << 18, transcendentals=0),
        name="prepare",
    )(interp_theta, interp_phi)
    me = lax.axis_index("y") * lax.axis_size("c") + lax.axis_index("c")
    me = jnp.broadcast_to(me.astype(jnp.int32), (parent_boxes, WIDTH))
    near_tables = slot_tables(send_index)
    x, theta, phi, me, *near_tables = lax.optimization_barrier((x, theta, phi, me, *near_tables))
    mine = pl.pallas_call(
        aggregate_kernel,
        out_shape=jax.ShapeDtypeStruct((samp_count, own_children // 8) + pattern, jnp.bfloat16),
        in_specs=[VMEM] * 5,
        out_specs=VMEM,
        scratch_shapes=[
            pltpu.VMEM((16 * polar_total, child_azimuth), jnp.bfloat16),
        ],
        compiler_params=pltpu.CompilerParams(vmem_limit_bytes=12 << 20),
        cost_estimate=pl.CostEstimate(flops=335 << 20, bytes_accessed=4 << 20, transcendentals=0),
        name="aggregate",
    )(x, theta, phi, cosine, sine)
    source, mine = lax.optimization_barrier((translator, mine))
    whole = mine
    mine = lax.all_to_all(whole, SAMP, split_axis=0, concat_axis=0, tiled=True)
    far_whole = shift(whole, "y", 2)
    staged = pl.pallas_call(
        stage_kernel,
        out_shape=pltpu.VMEM(translator.shape, translator.dtype),
        in_specs=[HBM],
        out_specs=VMEM,
        scratch_shapes=[pltpu.SemaphoreType.DMA],
        compiler_params=pltpu.CompilerParams(vmem_limit_bytes=56 << 20),
        cost_estimate=pl.CostEstimate(flops=1, bytes_accessed=5 << 20, transcendentals=0),
        name="stage",
    )(source)
    far_table = shift(near_tables[0], "y", 2)
    lists = plan_lists(me, (*near_tables, far_table), list_slots, list_kinds)
    mine, lists, staged = lax.optimization_barrier((mine, lists, staged))
    own = mine.reshape((parent_boxes,) + pattern)
    after = shift(own, "y", -1)
    before = shift(own, "y", 1)
    other = shift(own, "c", 1)
    far_whole, staged, own = lax.optimization_barrier((far_whole, staged, own))
    far = lax.all_to_all(far_whole, SAMP, split_axis=0, concat_axis=0, tiled=True)
    far = far.reshape((parent_boxes,) + pattern)
    params = pltpu.CompilerParams(vmem_limit_bytes=4 << 20)
    cost = pl.CostEstimate(flops=16 << 20, bytes_accessed=8 << 20, transcendentals=0)

    def widen_tables(tables):
        return pl.pallas_call(
            widen_kernel,
            out_shape=pltpu.VMEM(translator.shape, jnp.float32),
            in_specs=[VMEM],
            out_specs=VMEM,
            compiler_params=params,
            cost_estimate=cost,
        )(tables)

    wide = widen_tables(staged)
    shape = (parent_boxes,) + pattern

    def translate(k, wide, blocks, so_far):
        first, last = k == 0, k == len(CUTS) - 2
        field = (jax.ShapeDtypeStruct if last else pltpu.VMEM)(shape, jnp.float32)
        rows = (2 if k >= FAR else 6) * parent_boxes + 1
        out = [field, pltpu.VMEM((rows,) + pattern, jnp.float32)]
        out_specs, scratch, aliases = [HBM if last else VMEM, VMEM], [], {}
        if first:
            out.append(jax.ShapeDtypeStruct(shape, jnp.bfloat16))
            out_specs.append(HBM)
            scratch = [pltpu.SemaphoreType.DMA]
            operands = blocks
        elif k == FAR:
            operands = [so_far[0], *blocks]
        else:
            operands = [so_far[0], *blocks, so_far[1]]
            aliases = {1 + len(operands): 1}
        if last:
            scratch = [pltpu.VMEM(shape, jnp.float32), pltpu.SemaphoreType.DMA((4,))]
        return pl.pallas_call(
            functools.partial(class_kernel, k),
            out_shape=out,
            in_specs=[SMEM] + [VMEM] * (1 + len(operands)),
            out_specs=out_specs,
            scratch_shapes=scratch,
            input_output_aliases=aliases,
            compiler_params=params,
            cost_estimate=cost,
        )(lists, wide, *operands)

    *state, parents = translate(0, wide, [own, other], None)
    after, before, *state = lax.optimization_barrier((after, before, *state))
    across = [shift(after, "c", 1), shift(before, "c", 1)]
    state = translate(1, wide, [after, before], state)
    state = translate(2, wide, across, state)
    far, staged, *state = lax.optimization_barrier((far, staged, *state))
    across = shift(far, "c", 1)
    wide = widen_tables(staged)
    state = translate(3, wide, [far], state)
    field, _ = translate(4, wide, [across], state)
    return parents, field


def solution(mesh):
    y_count, x_count = 4, 4
    fine = Mesh(
        mesh.devices.reshape(y_count, mesh.shape["box"] // y_count, x_count, -1),
        BOX + SAMP,
    )
    return jax.shard_map(
        local,
        mesh=fine,
        in_specs=(
            P(BOX, None, SAMP, None),
            P(),
            P(),
            P(None, None, SAMP, None),
            P(BOX, None, None),
            P(BOX, None),
            P(BOX, None),
        ),
        out_specs=(P(BOX, None, SAMP, None), P(BOX, None, SAMP, None)),
        check_vma=False,
    )
```

```python
import functools
import math

import jax
import jax.numpy as jnp
from jax import lax
from jax.experimental import pallas as pl
from jax.experimental.pallas import tpu as pltpu
from jax.sharding import Mesh, PartitionSpec as P


KAPPA_H = 12.0
SAMP = ("x", "z")
BOX = ("y", "c")
WIDTH = 128
ROWS = (0, 2, 4, 0, 1)
FAR = 3
CUTS = (0, 14, 28, 46, 54, 64)
CHUNK = 16
VMEM = pl.BlockSpec(memory_space=pltpu.VMEM)
SMEM = pl.BlockSpec(memory_space=pltpu.SMEM)
HBM = pl.BlockSpec(memory_space=pltpu.HBM)


def phase_tables(polar_total, azimuth_total):
    polar = (jnp.arange(polar_total, dtype=jnp.int32).astype(jnp.float32) + 0.5) * (
        math.pi / polar_total
    )
    azimuth = jnp.arange(azimuth_total, dtype=jnp.int32).astype(jnp.float32) * (
        2.0 * math.pi / azimuth_total
    )
    along_x = KAPPA_H * jnp.sin(polar)[:, None] * jnp.cos(azimuth)[None, :]
    along_y = KAPPA_H * jnp.sin(polar)[:, None] * jnp.sin(azimuth)[None, :]
    along_z = (KAPPA_H * jnp.cos(polar))[:, None]
    parts = (jnp.cos(along_x), jnp.sin(along_x), jnp.cos(along_y), jnp.sin(along_y))
    cos_x, sin_x, cos_y, sin_y = lax.optimization_barrier(parts)
    octant = jnp.arange(4, dtype=jnp.int32)
    sign_x = ((octant & 1) * 2 - 1).astype(jnp.float32)[:, None, None]
    sign_y = ((octant >> 1 & 1) * 2 - 1).astype(jnp.float32)[:, None, None]
    x, y = (cos_x[None], sign_x * sin_x), (cos_y[None], sign_y * sin_y)
    return turn(turn(x, y), (jnp.cos(along_z), -jnp.sin(along_z)))


def turn(a, b):
    return a[0] * b[0] - a[1] * b[1], a[1] * b[0] + a[0] * b[1]


def prepare_kernel(theta_hbm, phi_hbm, turned_ref, phi_ref, theta_ref, sems):
    copies = [
        pltpu.make_async_copy(theta_hbm, theta_ref, sems.at[0]),
        pltpu.make_async_copy(phi_hbm, phi_ref, sems.at[1]),
    ]
    for copy in copies:
        copy.start()
    for copy in copies:
        copy.wait()
    turned_ref[...] = jnp.transpose(theta_ref[...].astype(jnp.float32)).astype(jnp.bfloat16)


def aggregate_kernel(x_ref, theta_ref, phi_ref, cos_ref, sin_ref, out_ref, mid_ref):
    theta = theta_ref[...]
    phi = phi_ref[...]
    chunks = theta.shape[0] // CHUNK
    for p in range(out_ref.shape[1]):
        for o in range(8):
            for r in range(2):
                x = x_ref[:, p * 8 + o, r].reshape(theta.shape[1], phi.shape[0])
                mid = jnp.dot(theta, x, preferred_element_type=jnp.float32).astype(jnp.bfloat16)
                for h in range(chunks):
                    at = (h * 16 + o * 2 + r) * CHUNK
                    mid_ref[at : at + CHUNK, :] = mid[h * CHUNK : (h + 1) * CHUNK]
        for h in range(chunks):
            mid = mid_ref[h * 16 * CHUNK : (h + 1) * 16 * CHUNK, :]
            raised = jnp.dot(mid, phi, preferred_element_type=jnp.float32)
            for s in range(CHUNK // 8):
                row = h * CHUNK + s * 8
                real = imag = None
                for o in range(4):
                    c = cos_ref[o, row : row + 8, :]
                    d = sin_ref[o, row : row + 8, :]
                    ar, ai, br, bi = (
                        raised[k * CHUNK + s * 8 : k * CHUNK + s * 8 + 8]
                        for k in (2 * o, 2 * o + 1, 14 - 2 * o, 15 - 2 * o)
                    )
                    tr = c * (ar + br) - d * (ai - bi)
                    ti = d * (ar - br) + c * (ai + bi)
                    real = tr if real is None else real + tr
                    imag = ti if imag is None else imag + ti
                out_ref[row // 8, p, 0] = real.astype(jnp.bfloat16)
                out_ref[row // 8, p, 1] = imag.astype(jnp.bfloat16)


def stage_kernel(x_ref, out_ref, sem):
    copy = pltpu.make_async_copy(x_ref, out_ref, sem)
    copy.start()
    copy.wait()


def widen_kernel(x_ref, out_ref):
    def widen(k, carry):
        out_ref[k] = x_ref[k].astype(jnp.float32)
        return carry

    lax.fori_loop(0, x_ref.shape[0], widen, 0, unroll=4)


def class_kernel(k, list_ref, trans_ref, *refs):
    first, last = k == 0, k == len(CUTS) - 2
    if first:
        *blocks, out_ref, pool_ref, parents_ref, sem = refs
        store = pltpu.make_async_copy(blocks[0], parents_ref, sem)
        store.start()
    elif last:
        sum_ref, *blocks, _, final_ref, pool_ref, out_ref, sems = refs
    elif k == FAR:
        sum_ref, *blocks, out_ref, pool_ref = refs
    else:
        sum_ref, *blocks, _, out_ref, pool_ref = refs
    boxes = out_ref.shape[0]
    for i, block in enumerate(blocks):

        def widen(n, carry, block=block, start=(ROWS[k] + i) * boxes):
            pool_ref[start + n] = block[n].astype(jnp.float32)
            return carry

        lax.fori_loop(0, boxes, widen, 0, unroll=4)
    if k in (0, FAR):
        pool_ref[pool_ref.shape[0] - 1] = jnp.zeros(pool_ref.shape[1:], jnp.float32)

    def add(b, j, acc):
        value = list_ref[b, j]
        at, kind = lax.shift_right_logical(value, 9), value & 511
        sr, si = pool_ref[at, 0], pool_ref[at, 1]
        tr, ti = trans_ref[kind, 0], trans_ref[kind, 1]
        return acc[0] + (tr * sr - ti * si), acc[1] + (tr * si + ti * sr)

    def start(b):
        if first:
            zero = jnp.zeros(out_ref.shape[2:], jnp.float32)
            return zero, zero
        begin = list_ref[boxes + b, k - 1]
        end = CUTS[k] if last else jnp.minimum(list_ref[boxes + b, k], CUTS[k])
        acc = (sum_ref[b, 0], sum_ref[b, 1])
        acc = lax.fori_loop(begin, end, lambda j, acc: add(b, j, acc), acc)
        if k == FAR - 1:
            end = list_ref[boxes + b, k]
            acc = lax.fori_loop(CUTS[FAR], end, lambda j, acc: add(b, j, acc), acc)
        return acc

    def pair(i, carry):
        places = (2 * i, 2 * i + 1)
        acc = [start(b) for b in places]
        for j in range(CUTS[k], CUTS[k + 1]):
            acc = [add(b, CUTS[-1] + j, a) for b, a in zip(places, acc)]
        for b, a in zip(places, acc):
            out_ref[b, 0], out_ref[b, 1] = a
        return carry

    if not last:
        lax.fori_loop(0, boxes // 2, pair, 0)
    else:
        parts = sems.shape[0]
        size = boxes // parts
        copies = []
        for i in range(parts):
            lax.fori_loop(i * size // 2, (i + 1) * size // 2, pair, 0)
            rows = pl.ds(i * size, size)
            out = pltpu.make_async_copy(out_ref.at[rows], final_ref.at[rows], sems.at[i])
            out.start()
            copies.append(out)
        for out in copies:
            out.wait()
    if first:
        store.wait()


def shift(x, axis, step):
    size = lax.axis_size(axis)
    return lax.ppermute(x, axis, [(i, (i + step) % size) for i in range(size)])


def plan_kernel(me_ref, own_ref, after_ref, before_ref, far_ref, slots_ref, kinds_ref, *rest):
    out_ref, list_ref, sem = rest
    cores, receivers, cap = own_ref.shape
    boxes, entries = slots_ref.shape
    me = me_ref[:, :entries]
    slots = slots_ref[...]
    sender = lax.shift_right_logical(slots, 4)
    dy = (lax.shift_right_logical(sender, 1) - lax.shift_right_logical(me, 1)) & 3
    dc = (sender & 1) ^ (me & 1)
    code = (dy * cores + dc) * cap + (slots & (cap - 1))
    is_me = lax.broadcasted_iota(jnp.int32, (receivers, cap), 0) == me[:receivers, :cap]
    pieces = []
    for table, block, step in (
        (own_ref, 0, 1),
        (after_ref, 2, 2),
        (far_ref, 0, 1),
        (before_ref, 3, 2),
    ):
        for core in range(cores):
            mine = jnp.sum(jnp.where(is_me, table[core], 0), axis=0, keepdims=True)
            pieces.append(mine + (block + step * core) * boxes)
    table = jnp.broadcast_to(jnp.concatenate(pieces, axis=1), (boxes, WIDTH))
    row = jnp.take_along_axis(table, jnp.concatenate([code, code], axis=1), axis=1)
    row = row[:, :entries]
    klass = jnp.where(dy == 0, 0, jnp.where(dy == 2, 3, 1) + dc)
    first = lax.broadcasted_iota(jnp.int32, (entries, entries), 0)
    second = lax.broadcasted_iota(jnp.int32, (entries, entries), 1)
    ahead = (first < second).astype(jnp.float32)
    lane = lax.broadcasted_iota(jnp.int32, (boxes, WIDTH), 1)
    slot = lane - entries
    spot = jnp.zeros_like(slots)
    begin = jnp.zeros((boxes, 1), jnp.int32)
    keep = slot < 0
    ends = jnp.zeros((boxes, WIDTH), jnp.int32)
    for k in range(len(CUTS) - 1):
        mine = klass == k
        inside = jnp.dot(mine.astype(jnp.float32), ahead, preferred_element_type=jnp.float32)
        spot = jnp.where(mine, begin + inside.astype(jnp.int32), spot)
        begin = begin + jnp.sum(mine.astype(jnp.int32), axis=1, keepdims=True)
        here = (slot >= CUTS[k]) & (slot < CUTS[k + 1]) & (slot < begin)
        if k < FAR:
            near_end = begin
        else:
            here = here & (slot >= near_end)
        keep = keep | here
        ends = jnp.where(lane == k, begin, ends)
    value = jnp.transpose((row * 512 + kinds_ref[...]).astype(jnp.float32)).astype(jnp.int32)
    spot = jnp.transpose(spot.astype(jnp.float32)).astype(jnp.int32)
    target = lax.broadcasted_iota(jnp.int32, (entries, WIDTH), 1) & (entries - 1)
    for b in range(boxes):
        got = jnp.where(spot[:, b : b + 1] == target, value[:, b : b + 1], 0)
        list_ref[b : b + 1, :] = jnp.sum(got, axis=0, keepdims=True)
    zero_row = jnp.where(slot < CUTS[FAR], 6 * boxes, 2 * boxes)
    list_ref[:boxes, :] = jnp.where(keep, list_ref[:boxes, :], zero_row * 512)
    list_ref[boxes:, :] = ends
    copy = pltpu.make_async_copy(list_ref, out_ref, sem)
    copy.start()
    copy.wait()


def slot_tables(send_index):
    own = jnp.concatenate([send_index, shift(send_index, "c", 1)], axis=0)
    return own, shift(own, "y", -1), shift(own, "y", 1), shift(own, "y", 2)


def plan_lists(me, tables, list_slots, list_kinds):
    boxes = list_slots.shape[0]
    return pl.pallas_call(
        plan_kernel,
        out_shape=pltpu.SMEM((2 * boxes, WIDTH), jnp.int32),
        in_specs=[VMEM] * 7,
        out_specs=SMEM,
        scratch_shapes=[pltpu.VMEM((2 * boxes, WIDTH), jnp.int32), pltpu.SemaphoreType.DMA],
        compiler_params=pltpu.CompilerParams(vmem_limit_bytes=4 << 20),
        cost_estimate=pl.CostEstimate(flops=1 << 20, bytes_accessed=1 << 20, transcendentals=0),
        name="plan",
    )(me, *tables, list_slots, list_kinds)


def local(children, interp_theta, interp_phi, translator, send_index, list_slots, list_kinds):
    samp_count = lax.axis_size(SAMP)
    polar_total = interp_theta.shape[1]
    azimuth_total = interp_phi.shape[1]
    child_boxes, _, rows, child_azimuth = children.shape
    own_children = child_boxes // samp_count
    parent_boxes = child_boxes // 8
    out_rows = polar_total // samp_count
    pattern = (2, out_rows, azimuth_total)

    x = children.reshape(samp_count, own_children, 2, rows, child_azimuth)
    x = lax.all_to_all(x, SAMP, split_axis=0, concat_axis=0, tiled=True)

    cosine, sine = phase_tables(polar_total, azimuth_total)
    theta, phi = pl.pallas_call(
        prepare_kernel,
        out_shape=[
            pltpu.VMEM(interp_theta.shape[::-1], jnp.bfloat16),
            pltpu.VMEM(interp_phi.shape, jnp.bfloat16),
        ],
        in_specs=[HBM] * 2,
        out_specs=[VMEM] * 2,
        scratch_shapes=[
            pltpu.VMEM(interp_theta.shape, jnp.bfloat16),
            pltpu.SemaphoreType.DMA((2,)),
        ],
        compiler_params=pltpu.CompilerParams(vmem_limit_bytes=61 << 20),
        cost_estimate=pl.CostEstimate(flops=1 << 20, bytes_accessed=1 << 18, transcendentals=0),
        name="prepare",
    )(interp_theta, interp_phi)
    me = lax.axis_index("y") * lax.axis_size("c") + lax.axis_index("c")
    me = jnp.broadcast_to(me.astype(jnp.int32), (parent_boxes, WIDTH))
    tables = slot_tables(send_index)
    x, theta, phi, me, *tables = lax.optimization_barrier((x, theta, phi, me, *tables))
    mine = pl.pallas_call(
        aggregate_kernel,
        out_shape=jax.ShapeDtypeStruct((samp_count, own_children // 8) + pattern, jnp.bfloat16),
        in_specs=[VMEM] * 5,
        out_specs=VMEM,
        scratch_shapes=[
            pltpu.VMEM((16 * polar_total, child_azimuth), jnp.bfloat16),
        ],
        compiler_params=pltpu.CompilerParams(vmem_limit_bytes=12 << 20),
        cost_estimate=pl.CostEstimate(flops=335 << 20, bytes_accessed=4 << 20, transcendentals=0),
        name="aggregate",
    )(x, theta, phi, cosine, sine)
    source, mine = lax.optimization_barrier((translator, mine))
    whole = mine
    mine = lax.all_to_all(whole, SAMP, split_axis=0, concat_axis=0, tiled=True)
    far_whole = shift(whole, "y", 2)
    staged = pl.pallas_call(
        stage_kernel,
        out_shape=pltpu.VMEM(translator.shape, translator.dtype),
        in_specs=[HBM],
        out_specs=VMEM,
        scratch_shapes=[pltpu.SemaphoreType.DMA],
        compiler_params=pltpu.CompilerParams(vmem_limit_bytes=56 << 20),
        cost_estimate=pl.CostEstimate(flops=1, bytes_accessed=5 << 20, transcendentals=0),
        name="stage",
    )(source)
    lists = plan_lists(me, tables, list_slots, list_kinds)
    mine, lists, staged = lax.optimization_barrier((mine, lists, staged))
    own = mine.reshape((parent_boxes,) + pattern)
    after = shift(own, "y", -1)
    before = shift(own, "y", 1)
    other = shift(own, "c", 1)
    far_whole, staged, own = lax.optimization_barrier((far_whole, staged, own))
    far = lax.all_to_all(far_whole, SAMP, split_axis=0, concat_axis=0, tiled=True)
    far = far.reshape((parent_boxes,) + pattern)
    params = pltpu.CompilerParams(vmem_limit_bytes=4 << 20)
    cost = pl.CostEstimate(flops=16 << 20, bytes_accessed=8 << 20, transcendentals=0)

    def widen_tables(tables):
        return pl.pallas_call(
            widen_kernel,
            out_shape=pltpu.VMEM(translator.shape, jnp.float32),
            in_specs=[VMEM],
            out_specs=VMEM,
            compiler_params=params,
            cost_estimate=cost,
        )(tables)

    wide = widen_tables(staged)
    shape = (parent_boxes,) + pattern

    def translate(k, wide, blocks, so_far):
        first, last = k == 0, k == len(CUTS) - 2
        field = (jax.ShapeDtypeStruct if last else pltpu.VMEM)(shape, jnp.float32)
        rows = (2 if k >= FAR else 6) * parent_boxes + 1
        out = [field, pltpu.VMEM((rows,) + pattern, jnp.float32)]
        out_specs, scratch, aliases = [HBM if last else VMEM, VMEM], [], {}
        if first:
            out.append(jax.ShapeDtypeStruct(shape, jnp.bfloat16))
            out_specs.append(HBM)
            scratch = [pltpu.SemaphoreType.DMA]
            operands = blocks
        elif k == FAR:
            operands = [so_far[0], *blocks]
        else:
            operands = [so_far[0], *blocks, so_far[1]]
            aliases = {1 + len(operands): 1}
        if last:
            scratch = [pltpu.VMEM(shape, jnp.float32), pltpu.SemaphoreType.DMA((4,))]
        return pl.pallas_call(
            functools.partial(class_kernel, k),
            out_shape=out,
            in_specs=[SMEM] + [VMEM] * (1 + len(operands)),
            out_specs=out_specs,
            scratch_shapes=scratch,
            input_output_aliases=aliases,
            compiler_params=params,
            cost_estimate=cost,
        )(lists, wide, *operands)

    *state, parents = translate(0, wide, [own, other], None)
    after, before, *state = lax.optimization_barrier((after, before, *state))
    across = [shift(after, "c", 1), shift(before, "c", 1)]
    state = translate(1, wide, [after, before], state)
    state = translate(2, wide, across, state)
    far, staged, *state = lax.optimization_barrier((far, staged, *state))
    across = shift(far, "c", 1)
    wide = widen_tables(staged)
    state = translate(3, wide, [far], state)
    field, _ = translate(4, wide, [across], state)
    return parents, field


def solution(mesh):
    y_count, x_count = 4, 4
    fine = Mesh(
        mesh.devices.reshape(y_count, mesh.shape["box"] // y_count, x_count, -1),
        BOX + SAMP,
    )
    return jax.shard_map(
        local,
        mesh=fine,
        in_specs=(
            P(BOX, None, SAMP, None),
            P(),
            P(),
            P(None, None, SAMP, None),
            P(BOX, None, None),
            P(BOX, None),
            P(BOX, None),
        ),
        out_specs=(P(BOX, None, SAMP, None), P(BOX, None, SAMP, None)),
        check_vma=False,
    )
```

```python
import functools
import math

import jax
import jax.numpy as jnp
from jax import lax
from jax.experimental import pallas as pl
from jax.experimental.pallas import tpu as pltpu
from jax.sharding import Mesh, PartitionSpec as P


KAPPA_H = 12.0
SAMP = ("x", "z")
BOX = ("y", "c")
WIDTH = 128
ROWS = (0, 2, 4, 0, 1)
FAR = 3
CUTS = (0, 14, 22, 46, 54, 64)
CHUNK = 16
VMEM = pl.BlockSpec(memory_space=pltpu.VMEM)
SMEM = pl.BlockSpec(memory_space=pltpu.SMEM)
HBM = pl.BlockSpec(memory_space=pltpu.HBM)


def phase_tables(polar_total, azimuth_total):
    polar = (jnp.arange(polar_total, dtype=jnp.int32).astype(jnp.float32) + 0.5) * (
        math.pi / polar_total
    )
    azimuth = jnp.arange(azimuth_total, dtype=jnp.int32).astype(jnp.float32) * (
        2.0 * math.pi / azimuth_total
    )
    along_x = KAPPA_H * jnp.sin(polar)[:, None] * jnp.cos(azimuth)[None, :]
    along_y = KAPPA_H * jnp.sin(polar)[:, None] * jnp.sin(azimuth)[None, :]
    along_z = (KAPPA_H * jnp.cos(polar))[:, None]
    parts = (jnp.cos(along_x), jnp.sin(along_x), jnp.cos(along_y), jnp.sin(along_y))
    cos_x, sin_x, cos_y, sin_y = lax.optimization_barrier(parts)
    octant = jnp.arange(4, dtype=jnp.int32)
    sign_x = ((octant & 1) * 2 - 1).astype(jnp.float32)[:, None, None]
    sign_y = ((octant >> 1 & 1) * 2 - 1).astype(jnp.float32)[:, None, None]
    x, y = (cos_x[None], sign_x * sin_x), (cos_y[None], sign_y * sin_y)
    return turn(turn(x, y), (jnp.cos(along_z), -jnp.sin(along_z)))


def turn(a, b):
    return a[0] * b[0] - a[1] * b[1], a[1] * b[0] + a[0] * b[1]


def prepare_kernel(theta_hbm, phi_hbm, turned_ref, phi_ref, theta_ref, sems):
    copies = [
        pltpu.make_async_copy(theta_hbm, theta_ref, sems.at[0]),
        pltpu.make_async_copy(phi_hbm, phi_ref, sems.at[1]),
    ]
    for copy in copies:
        copy.start()
    for copy in copies:
        copy.wait()
    turned_ref[...] = jnp.transpose(theta_ref[...].astype(jnp.float32)).astype(jnp.bfloat16)


def aggregate_kernel(x_ref, theta_ref, phi_ref, cos_ref, sin_ref, out_ref, mid_ref):
    theta = theta_ref[...]
    phi = phi_ref[...]
    chunks = theta.shape[0] // CHUNK
    for p in range(out_ref.shape[1]):
        for o in range(8):
            for r in range(2):
                x = x_ref[:, p * 8 + o, r].reshape(theta.shape[1], phi.shape[0])
                mid = jnp.dot(theta, x, preferred_element_type=jnp.float32).astype(jnp.bfloat16)
                for h in range(chunks):
                    at = (h * 16 + o * 2 + r) * CHUNK
                    mid_ref[at : at + CHUNK, :] = mid[h * CHUNK : (h + 1) * CHUNK]
        for h in range(chunks):
            mid = mid_ref[h * 16 * CHUNK : (h + 1) * 16 * CHUNK, :]
            raised = jnp.dot(mid, phi, preferred_element_type=jnp.float32)
            for s in range(CHUNK // 8):
                row = h * CHUNK + s * 8
                real = imag = None
                for o in range(4):
                    c = cos_ref[o, row : row + 8, :]
                    d = sin_ref[o, row : row + 8, :]
                    ar, ai, br, bi = (
                        raised[k * CHUNK + s * 8 : k * CHUNK + s * 8 + 8]
                        for k in (2 * o, 2 * o + 1, 14 - 2 * o, 15 - 2 * o)
                    )
                    tr = c * (ar + br) - d * (ai - bi)
                    ti = d * (ar - br) + c * (ai + bi)
                    real = tr if real is None else real + tr
                    imag = ti if imag is None else imag + ti
                out_ref[row // 8, p, 0] = real.astype(jnp.bfloat16)
                out_ref[row // 8, p, 1] = imag.astype(jnp.bfloat16)


def stage_kernel(x_ref, out_ref, sem):
    copy = pltpu.make_async_copy(x_ref, out_ref, sem)
    copy.start()
    copy.wait()


def widen_kernel(x_ref, out_ref):
    def widen(k, carry):
        out_ref[k] = x_ref[k].astype(jnp.float32)
        return carry

    lax.fori_loop(0, x_ref.shape[0], widen, 0, unroll=4)


def class_kernel(k, list_ref, trans_ref, *refs):
    first, last = k == 0, k == len(CUTS) - 2
    if first:
        *blocks, out_ref, pool_ref, parents_ref, sem = refs
        store = pltpu.make_async_copy(blocks[0], parents_ref, sem)
        store.start()
    elif last:
        sum_ref, *blocks, _, final_ref, pool_ref, out_ref, sems = refs
    elif k == 1:
        sum_ref, *blocks, later, _, out_ref, pool_ref, later_ref, sem = refs
        fetch = pltpu.make_async_copy(later, later_ref, sem)
        fetch.start()
    elif k == FAR:
        sum_ref, *blocks, out_ref, pool_ref = refs
    else:
        sum_ref, *blocks, _, out_ref, pool_ref = refs
    boxes = out_ref.shape[0]

    def widen_block(block, start):
        def widen(n, carry):
            pool_ref[start + n] = block[n].astype(jnp.float32)
            return carry

        lax.fori_loop(0, boxes, widen, 0, unroll=4)

    for i, block in enumerate(blocks):
        widen_block(block, (ROWS[k] + i) * boxes)
    if k in (0, FAR):
        pool_ref[pool_ref.shape[0] - 1] = jnp.zeros(pool_ref.shape[1:], jnp.float32)

    def add(b, j, acc):
        value = list_ref[b, j]
        at, kind = lax.shift_right_logical(value, 9), value & 511
        sr, si = pool_ref[at, 0], pool_ref[at, 1]
        tr, ti = trans_ref[kind, 0], trans_ref[kind, 1]
        return acc[0] + (tr * sr - ti * si), acc[1] + (tr * si + ti * sr)

    def start(b):
        if first:
            zero = jnp.zeros(out_ref.shape[2:], jnp.float32)
            return zero, zero
        begin = list_ref[boxes + b, k - 1]
        end = CUTS[k] if last else jnp.minimum(list_ref[boxes + b, k], CUTS[k])
        acc = (sum_ref[b, 0], sum_ref[b, 1])
        acc = lax.fori_loop(begin, end, lambda j, acc: add(b, j, acc), acc)
        if k == FAR - 1:
            end = list_ref[boxes + b, k]
            acc = lax.fori_loop(CUTS[FAR], end, lambda j, acc: add(b, j, acc), acc)
        return acc

    def pair(i, carry):
        places = (2 * i, 2 * i + 1)
        acc = [start(b) for b in places]
        for j in range(CUTS[k], CUTS[k + 1]):
            acc = [add(b, CUTS[-1] + j, a) for b, a in zip(places, acc)]
        for b, a in zip(places, acc):
            out_ref[b, 0], out_ref[b, 1] = a
        return carry

    if not last:
        lax.fori_loop(0, boxes // 2, pair, 0)
    else:
        parts = sems.shape[0]
        size = boxes // parts
        copies = []
        for i in range(parts):
            lax.fori_loop(i * size // 2, (i + 1) * size // 2, pair, 0)
            rows = pl.ds(i * size, size)
            out = pltpu.make_async_copy(out_ref.at[rows], final_ref.at[rows], sems.at[i])
            out.start()
            copies.append(out)
        for out in copies:
            out.wait()
    if first:
        store.wait()
    if k == 1:
        fetch.wait()
        widen_block(later_ref, (ROWS[k] + 1) * boxes)


def shift(x, axis, step):
    size = lax.axis_size(axis)
    return lax.ppermute(x, axis, [(i, (i + step) % size) for i in range(size)])


def plan_kernel(me_ref, own_ref, after_ref, before_ref, far_ref, slots_ref, kinds_ref, *rest):
    out_ref, list_ref, sem = rest
    cores, receivers, cap = own_ref.shape
    boxes, entries = slots_ref.shape
    me = me_ref[:, :entries]
    slots = slots_ref[...]
    sender = lax.shift_right_logical(slots, 4)
    dy = (lax.shift_right_logical(sender, 1) - lax.shift_right_logical(me, 1)) & 3
    dc = (sender & 1) ^ (me & 1)
    code = (dy * cores + dc) * cap + (slots & (cap - 1))
    is_me = lax.broadcasted_iota(jnp.int32, (receivers, cap), 0) == me[:receivers, :cap]
    pieces = []
    for table, block, step in (
        (own_ref, 0, 1),
        (after_ref, 3, 1),
        (far_ref, 0, 1),
        (before_ref, 2, 3),
    ):
        for core in range(cores):
            mine = jnp.sum(jnp.where(is_me, table[core], 0), axis=0, keepdims=True)
            pieces.append(mine + (block + step * core) * boxes)
    table = jnp.broadcast_to(jnp.concatenate(pieces, axis=1), (boxes, WIDTH))
    row = jnp.take_along_axis(table, jnp.concatenate([code, code], axis=1), axis=1)
    row = row[:, :entries]
    klass = jnp.where((dy == 3) & (dc == 0), 1, 2)
    klass = jnp.where(dy == 0, 0, jnp.where(dy == 2, 3 + dc, klass))
    first = lax.broadcasted_iota(jnp.int32, (entries, entries), 0)
    second = lax.broadcasted_iota(jnp.int32, (entries, entries), 1)
    ahead = (first < second).astype(jnp.float32)
    lane = lax.broadcasted_iota(jnp.int32, (boxes, WIDTH), 1)
    slot = lane - entries
    spot = jnp.zeros_like(slots)
    begin = jnp.zeros((boxes, 1), jnp.int32)
    keep = slot < 0
    ends = jnp.zeros((boxes, WIDTH), jnp.int32)
    for k in range(len(CUTS) - 1):
        mine = klass == k
        inside = jnp.dot(mine.astype(jnp.float32), ahead, preferred_element_type=jnp.float32)
        spot = jnp.where(mine, begin + inside.astype(jnp.int32), spot)
        begin = begin + jnp.sum(mine.astype(jnp.int32), axis=1, keepdims=True)
        here = (slot >= CUTS[k]) & (slot < CUTS[k + 1]) & (slot < begin)
        if k < FAR:
            near_end = begin
        else:
            here = here & (slot >= near_end)
        keep = keep | here
        ends = jnp.where(lane == k, begin, ends)
    value = jnp.transpose((row * 512 + kinds_ref[...]).astype(jnp.float32)).astype(jnp.int32)
    spot = jnp.transpose(spot.astype(jnp.float32)).astype(jnp.int32)
    target = lax.broadcasted_iota(jnp.int32, (entries, WIDTH), 1) & (entries - 1)
    for b in range(boxes):
        got = jnp.where(spot[:, b : b + 1] == target, value[:, b : b + 1], 0)
        list_ref[b : b + 1, :] = jnp.sum(got, axis=0, keepdims=True)
    zero_row = jnp.where(slot < CUTS[FAR], 6 * boxes, 2 * boxes)
    list_ref[:boxes, :] = jnp.where(keep, list_ref[:boxes, :], zero_row * 512)
    list_ref[boxes:, :] = ends
    copy = pltpu.make_async_copy(list_ref, out_ref, sem)
    copy.start()
    copy.wait()


def slot_tables(send_index):
    own = jnp.concatenate([send_index, shift(send_index, "c", 1)], axis=0)
    return own, shift(own, "y", -1), shift(own, "y", 1), shift(own, "y", 2)


def plan_lists(me, tables, list_slots, list_kinds):
    boxes = list_slots.shape[0]
    return pl.pallas_call(
        plan_kernel,
        out_shape=pltpu.SMEM((2 * boxes, WIDTH), jnp.int32),
        in_specs=[VMEM] * 7,
        out_specs=SMEM,
        scratch_shapes=[pltpu.VMEM((2 * boxes, WIDTH), jnp.int32), pltpu.SemaphoreType.DMA],
        compiler_params=pltpu.CompilerParams(vmem_limit_bytes=4 << 20),
        cost_estimate=pl.CostEstimate(flops=1 << 20, bytes_accessed=1 << 20, transcendentals=0),
        name="plan",
    )(me, *tables, list_slots, list_kinds)


def local(children, interp_theta, interp_phi, translator, send_index, list_slots, list_kinds):
    samp_count = lax.axis_size(SAMP)
    polar_total = interp_theta.shape[1]
    azimuth_total = interp_phi.shape[1]
    child_boxes, _, rows, child_azimuth = children.shape
    own_children = child_boxes // samp_count
    parent_boxes = child_boxes // 8
    out_rows = polar_total // samp_count
    pattern = (2, out_rows, azimuth_total)

    x = children.reshape(samp_count, own_children, 2, rows, child_azimuth)
    x = lax.all_to_all(x, SAMP, split_axis=0, concat_axis=0, tiled=True)

    cosine, sine = phase_tables(polar_total, azimuth_total)
    theta, phi = pl.pallas_call(
        prepare_kernel,
        out_shape=[
            pltpu.VMEM(interp_theta.shape[::-1], jnp.bfloat16),
            pltpu.VMEM(interp_phi.shape, jnp.bfloat16),
        ],
        in_specs=[HBM] * 2,
        out_specs=[VMEM] * 2,
        scratch_shapes=[
            pltpu.VMEM(interp_theta.shape, jnp.bfloat16),
            pltpu.SemaphoreType.DMA((2,)),
        ],
        compiler_params=pltpu.CompilerParams(vmem_limit_bytes=61 << 20),
        cost_estimate=pl.CostEstimate(flops=1 << 20, bytes_accessed=1 << 18, transcendentals=0),
        name="prepare",
    )(interp_theta, interp_phi)
    me = lax.axis_index("y") * lax.axis_size("c") + lax.axis_index("c")
    me = jnp.broadcast_to(me.astype(jnp.int32), (parent_boxes, WIDTH))
    tables = slot_tables(send_index)
    x, theta, phi, me, *tables = lax.optimization_barrier((x, theta, phi, me, *tables))
    mine = pl.pallas_call(
        aggregate_kernel,
        out_shape=jax.ShapeDtypeStruct((samp_count, own_children // 8) + pattern, jnp.bfloat16),
        in_specs=[VMEM] * 5,
        out_specs=VMEM,
        scratch_shapes=[
            pltpu.VMEM((16 * polar_total, child_azimuth), jnp.bfloat16),
        ],
        compiler_params=pltpu.CompilerParams(vmem_limit_bytes=12 << 20),
        cost_estimate=pl.CostEstimate(flops=335 << 20, bytes_accessed=4 << 20, transcendentals=0),
        name="aggregate",
    )(x, theta, phi, cosine, sine)
    source, mine = lax.optimization_barrier((translator, mine))
    whole = mine
    mine = lax.all_to_all(whole, SAMP, split_axis=0, concat_axis=0, tiled=True)
    far_whole = shift(whole, "y", 2)
    staged = pl.pallas_call(
        stage_kernel,
        out_shape=pltpu.VMEM(translator.shape, translator.dtype),
        in_specs=[HBM],
        out_specs=VMEM,
        scratch_shapes=[pltpu.SemaphoreType.DMA],
        compiler_params=pltpu.CompilerParams(vmem_limit_bytes=56 << 20),
        cost_estimate=pl.CostEstimate(flops=1, bytes_accessed=5 << 20, transcendentals=0),
        name="stage",
    )(source)
    lists = plan_lists(me, tables, list_slots, list_kinds)
    mine, lists, staged = lax.optimization_barrier((mine, lists, staged))
    own = mine.reshape((parent_boxes,) + pattern)
    after = shift(own, "y", -1)
    before = shift(own, "y", 1)
    other = shift(own, "c", 1)
    far_whole, staged, own = lax.optimization_barrier((far_whole, staged, own))
    far = lax.all_to_all(far_whole, SAMP, split_axis=0, concat_axis=0, tiled=True)
    far = far.reshape((parent_boxes,) + pattern)
    params = pltpu.CompilerParams(vmem_limit_bytes=4 << 20)
    cost = pl.CostEstimate(flops=16 << 20, bytes_accessed=8 << 20, transcendentals=0)

    def widen_tables(tables):
        return pl.pallas_call(
            widen_kernel,
            out_shape=pltpu.VMEM(translator.shape, jnp.float32),
            in_specs=[VMEM],
            out_specs=VMEM,
            compiler_params=params,
            cost_estimate=cost,
        )(tables)

    wide = widen_tables(staged)
    shape = (parent_boxes,) + pattern

    def translate(k, wide, blocks, so_far):
        first, last = k == 0, k == len(CUTS) - 2
        field = (jax.ShapeDtypeStruct if last else pltpu.VMEM)(shape, jnp.float32)
        rows = (2 if k >= FAR else 6) * parent_boxes + 1
        out = [field, pltpu.VMEM((rows,) + pattern, jnp.float32)]
        out_specs, scratch, aliases = [HBM if last else VMEM, VMEM], [], {}
        if first:
            out.append(jax.ShapeDtypeStruct(shape, jnp.bfloat16))
            out_specs.append(HBM)
            scratch = [pltpu.SemaphoreType.DMA]
            operands = blocks
        elif k == FAR:
            operands = [so_far[0], *blocks]
        else:
            operands = [so_far[0], *blocks, so_far[1]]
            aliases = {1 + len(operands): 1}
        kinds = [VMEM] * len(operands)
        if k == 1:
            kinds[-2] = HBM
            scratch = [pltpu.VMEM(shape, jnp.bfloat16), pltpu.SemaphoreType.DMA]
        if last:
            scratch = [pltpu.VMEM(shape, jnp.float32), pltpu.SemaphoreType.DMA((4,))]
        return pl.pallas_call(
            functools.partial(class_kernel, k),
            out_shape=out,
            in_specs=[SMEM, VMEM] + kinds,
            out_specs=out_specs,
            scratch_shapes=scratch,
            input_output_aliases=aliases,
            compiler_params=params,
            cost_estimate=cost,
        )(lists, wide, *operands)

    *state, parents = translate(0, wide, [own, other], None)
    after, before, *state = lax.optimization_barrier((after, before, *state))
    across = [shift(after, "c", 1), shift(before, "c", 1)]
    state = translate(1, wide, [before, after], state)
    state = translate(2, wide, across, state)
    far, staged, *state = lax.optimization_barrier((far, staged, *state))
    across = shift(far, "c", 1)
    wide = widen_tables(staged)
    state = translate(3, wide, [far], state)
    field, _ = translate(4, wide, [across], state)
    return parents, field


def solution(mesh):
    y_count, x_count = 4, 4
    fine = Mesh(
        mesh.devices.reshape(y_count, mesh.shape["box"] // y_count, x_count, -1),
        BOX + SAMP,
    )
    return jax.shard_map(
        local,
        mesh=fine,
        in_specs=(
            P(BOX, None, SAMP, None),
            P(),
            P(),
            P(None, None, SAMP, None),
            P(BOX, None, None),
            P(BOX, None),
            P(BOX, None),
        ),
        out_specs=(P(BOX, None, SAMP, None), P(BOX, None, SAMP, None)),
        check_vma=False,
    )
```

```python
import functools
import math

import jax
import jax.numpy as jnp
from jax import lax
from jax.experimental import pallas as pl
from jax.experimental.pallas import tpu as pltpu
from jax.sharding import Mesh, PartitionSpec as P


KAPPA_H = 12.0
SAMP = ("x", "z")
BOX = ("y", "c")
WIDTH = 128
ROWS = (0, 2, 4, 0, 1)
FAR = 3
CUTS = (0, 14, 22, 46, 54, 64)
CHUNK = 16
VMEM = pl.BlockSpec(memory_space=pltpu.VMEM)
SMEM = pl.BlockSpec(memory_space=pltpu.SMEM)
HBM = pl.BlockSpec(memory_space=pltpu.HBM)


def phase_tables(polar_total, azimuth_total):
    polar = (jnp.arange(polar_total, dtype=jnp.int32).astype(jnp.float32) + 0.5) * (
        math.pi / polar_total
    )
    azimuth = jnp.arange(azimuth_total, dtype=jnp.int32).astype(jnp.float32) * (
        2.0 * math.pi / azimuth_total
    )
    along_x = KAPPA_H * jnp.sin(polar)[:, None] * jnp.cos(azimuth)[None, :]
    along_y = KAPPA_H * jnp.sin(polar)[:, None] * jnp.sin(azimuth)[None, :]
    along_z = (KAPPA_H * jnp.cos(polar))[:, None]
    parts = (jnp.cos(along_x), jnp.sin(along_x), jnp.cos(along_y), jnp.sin(along_y))
    cos_x, sin_x, cos_y, sin_y = lax.optimization_barrier(parts)
    octant = jnp.arange(4, dtype=jnp.int32)
    sign_x = ((octant & 1) * 2 - 1).astype(jnp.float32)[:, None, None]
    sign_y = ((octant >> 1 & 1) * 2 - 1).astype(jnp.float32)[:, None, None]
    x, y = (cos_x[None], sign_x * sin_x), (cos_y[None], sign_y * sin_y)
    return turn(turn(x, y), (jnp.cos(along_z), -jnp.sin(along_z)))


def turn(a, b):
    return a[0] * b[0] - a[1] * b[1], a[1] * b[0] + a[0] * b[1]


def prepare_kernel(theta_hbm, phi_hbm, turned_ref, phi_ref, theta_ref, sems):
    copies = [
        pltpu.make_async_copy(theta_hbm, theta_ref, sems.at[0]),
        pltpu.make_async_copy(phi_hbm, phi_ref, sems.at[1]),
    ]
    for copy in copies:
        copy.start()
    for copy in copies:
        copy.wait()
    turned_ref[...] = jnp.transpose(theta_ref[...].astype(jnp.float32)).astype(jnp.bfloat16)


def aggregate_kernel(x_ref, theta_ref, phi_ref, cos_ref, sin_ref, out_ref, mid_ref):
    theta = theta_ref[...]
    phi = phi_ref[...]
    chunks = theta.shape[0] // CHUNK
    for p in range(out_ref.shape[1]):
        for o in range(8):
            for r in range(2):
                x = x_ref[:, p * 8 + o, r].reshape(theta.shape[1], phi.shape[0])
                mid = jnp.dot(theta, x, preferred_element_type=jnp.float32).astype(jnp.bfloat16)
                for h in range(chunks):
                    at = (h * 16 + o * 2 + r) * CHUNK
                    mid_ref[at : at + CHUNK, :] = mid[h * CHUNK : (h + 1) * CHUNK]
        for h in range(chunks):
            mid = mid_ref[h * 16 * CHUNK : (h + 1) * 16 * CHUNK, :]
            raised = jnp.dot(mid, phi, preferred_element_type=jnp.float32)
            for s in range(CHUNK // 8):
                row = h * CHUNK + s * 8
                real = imag = None
                for o in range(4):
                    c = cos_ref[o, row : row + 8, :]
                    d = sin_ref[o, row : row + 8, :]
                    ar, ai, br, bi = (
                        raised[k * CHUNK + s * 8 : k * CHUNK + s * 8 + 8]
                        for k in (2 * o, 2 * o + 1, 14 - 2 * o, 15 - 2 * o)
                    )
                    tr = c * (ar + br) - d * (ai - bi)
                    ti = d * (ar - br) + c * (ai + bi)
                    real = tr if real is None else real + tr
                    imag = ti if imag is None else imag + ti
                out_ref[row // 8, p, 0] = real.astype(jnp.bfloat16)
                out_ref[row // 8, p, 1] = imag.astype(jnp.bfloat16)


def stage_kernel(x_ref, out_ref, sem):
    copy = pltpu.make_async_copy(x_ref, out_ref, sem)
    copy.start()
    copy.wait()


def widen_kernel(x_ref, out_ref):
    def widen(k, carry):
        out_ref[k] = x_ref[k].astype(jnp.float32)
        return carry

    lax.fori_loop(0, x_ref.shape[0], widen, 0, unroll=4)


def class_kernel(k, list_ref, trans_ref, *refs):
    first, last = k == 0, k == len(CUTS) - 2
    if first:
        *blocks, out_ref, pool_ref, parents_ref, sem = refs
        store = pltpu.make_async_copy(blocks[0], parents_ref, sem)
        store.start()
    elif last:
        sum_ref, *blocks, _, final_ref, pool_ref, out_ref, sems = refs
    elif k == 1:
        sum_ref, *blocks, later, _, out_ref, pool_ref, later_ref, sem = refs
        fetch = pltpu.make_async_copy(later, later_ref, sem)
        fetch.start()
    elif k == FAR:
        sum_ref, *blocks, out_ref, pool_ref = refs
    else:
        sum_ref, *blocks, _, out_ref, pool_ref = refs
    boxes = out_ref.shape[0]

    def widen_block(block, start):
        def widen(n, carry):
            pool_ref[start + n] = block[n].astype(jnp.float32)
            return carry

        lax.fori_loop(0, boxes, widen, 0, unroll=4)

    for i, block in enumerate(blocks):
        widen_block(block, (ROWS[k] + i) * boxes)
    if k in (0, FAR):
        pool_ref[pool_ref.shape[0] - 1] = jnp.zeros(pool_ref.shape[1:], jnp.float32)

    def add(b, j, acc):
        value = list_ref[b, j]
        at, kind = lax.shift_right_logical(value, 9), value & 511
        sr, si = pool_ref[at, 0], pool_ref[at, 1]
        tr, ti = trans_ref[kind, 0], trans_ref[kind, 1]
        return acc[0] + (tr * sr - ti * si), acc[1] + (tr * si + ti * sr)

    def start(b):
        if first:
            zero = jnp.zeros(out_ref.shape[2:], jnp.float32)
            return zero, zero
        begin = list_ref[boxes + b, k - 1]
        end = CUTS[k] if last else jnp.minimum(list_ref[boxes + b, k], CUTS[k])
        acc = (sum_ref[b, 0], sum_ref[b, 1])
        acc = lax.fori_loop(begin, end, lambda j, acc: add(b, j, acc), acc)
        if k == FAR - 1:
            end = list_ref[boxes + b, k]
            acc = lax.fori_loop(CUTS[FAR], end, lambda j, acc: add(b, j, acc), acc)
        return acc

    def pair(i, carry):
        places = (2 * i, 2 * i + 1)
        acc = [start(b) for b in places]
        for j in range(CUTS[k], CUTS[k + 1]):
            acc = [add(b, CUTS[-1] + j, a) for b, a in zip(places, acc)]
        for b, a in zip(places, acc):
            out_ref[b, 0], out_ref[b, 1] = a
        return carry

    if not last:
        lax.fori_loop(0, boxes // 2, pair, 0)
    else:
        parts = sems.shape[0]
        size = boxes // parts
        copies = []
        for i in range(parts):
            lax.fori_loop(i * size // 2, (i + 1) * size // 2, pair, 0)
            rows = pl.ds(i * size, size)
            out = pltpu.make_async_copy(out_ref.at[rows], final_ref.at[rows], sems.at[i])
            out.start()
            copies.append(out)
        for out in copies:
            out.wait()
    if first:
        store.wait()
    if k == 1:
        fetch.wait()
        widen_block(later_ref, (ROWS[k] + 1) * boxes)


def shift(x, axis, step):
    size = lax.axis_size(axis)
    return lax.ppermute(x, axis, [(i, (i + step) % size) for i in range(size)])


def plan_kernel(me_ref, own_ref, after_ref, before_ref, far_ref, slots_ref, kinds_ref, *rest):
    out_ref, list_ref, sem = rest
    cores, receivers, cap = own_ref.shape
    boxes, entries = slots_ref.shape
    me = me_ref[:, :entries]
    slots = slots_ref[...]
    sender = lax.shift_right_logical(slots, 4)
    dy = (lax.shift_right_logical(sender, 1) - lax.shift_right_logical(me, 1)) & 3
    dc = (sender & 1) ^ (me & 1)
    code = (dy * cores + dc) * cap + (slots & (cap - 1))
    is_me = lax.broadcasted_iota(jnp.int32, (receivers, cap), 0) == me[:receivers, :cap]
    pieces = []
    for table, block, step in (
        (own_ref, 0, 1),
        (after_ref, 3, 1),
        (far_ref, 0, 1),
        (before_ref, 2, 3),
    ):
        for core in range(cores):
            mine = jnp.sum(jnp.where(is_me, table[core], 0), axis=0, keepdims=True)
            pieces.append(mine + (block + step * core) * boxes)
    table = jnp.broadcast_to(jnp.concatenate(pieces, axis=1), (boxes, WIDTH))
    row = jnp.take_along_axis(table, jnp.concatenate([code, code], axis=1), axis=1)
    row = row[:, :entries]
    klass = jnp.where((dy == 3) & (dc == 0), 1, 2)
    klass = jnp.where(dy == 0, 0, jnp.where(dy == 2, 3 + dc, klass))
    first = lax.broadcasted_iota(jnp.int32, (entries, entries), 0)
    second = lax.broadcasted_iota(jnp.int32, (entries, entries), 1)
    ahead = (first < second).astype(jnp.float32)
    lane = lax.broadcasted_iota(jnp.int32, (boxes, WIDTH), 1)
    slot = lane - entries
    spot = jnp.zeros_like(slots)
    begin = jnp.zeros((boxes, 1), jnp.int32)
    keep = slot < 0
    ends = jnp.zeros((boxes, WIDTH), jnp.int32)
    for k in range(len(CUTS) - 1):
        mine = klass == k
        inside = jnp.dot(mine.astype(jnp.float32), ahead, preferred_element_type=jnp.float32)
        spot = jnp.where(mine, begin + inside.astype(jnp.int32), spot)
        begin = begin + jnp.sum(mine.astype(jnp.int32), axis=1, keepdims=True)
        here = (slot >= CUTS[k]) & (slot < CUTS[k + 1]) & (slot < begin)
        if k < FAR:
            near_end = begin
        else:
            here = here & (slot >= near_end)
        keep = keep | here
        ends = jnp.where(lane == k, begin, ends)
    value = jnp.transpose((row * 512 + kinds_ref[...]).astype(jnp.float32)).astype(jnp.int32)
    spot = jnp.transpose(spot.astype(jnp.float32)).astype(jnp.int32)
    target = lax.broadcasted_iota(jnp.int32, (entries, WIDTH), 1) & (entries - 1)
    for b in range(boxes):
        got = jnp.where(spot[:, b : b + 1] == target, value[:, b : b + 1], 0)
        list_ref[b : b + 1, :] = jnp.sum(got, axis=0, keepdims=True)
    zero_row = jnp.where(slot < CUTS[FAR], 6 * boxes, 2 * boxes)
    list_ref[:boxes, :] = jnp.where(keep, list_ref[:boxes, :], zero_row * 512)
    list_ref[boxes:, :] = ends
    copy = pltpu.make_async_copy(list_ref, out_ref, sem)
    copy.start()
    copy.wait()


def slot_tables(send_index):
    own = jnp.concatenate([send_index, shift(send_index, "c", 1)], axis=0)
    return own, shift(own, "y", -1), shift(own, "y", 1)


def plan_lists(me, tables, list_slots, list_kinds):
    boxes = list_slots.shape[0]
    return pl.pallas_call(
        plan_kernel,
        out_shape=pltpu.SMEM((2 * boxes, WIDTH), jnp.int32),
        in_specs=[VMEM] * 7,
        out_specs=SMEM,
        scratch_shapes=[pltpu.VMEM((2 * boxes, WIDTH), jnp.int32), pltpu.SemaphoreType.DMA],
        compiler_params=pltpu.CompilerParams(vmem_limit_bytes=4 << 20),
        cost_estimate=pl.CostEstimate(flops=1 << 20, bytes_accessed=1 << 20, transcendentals=0),
        name="plan",
    )(me, *tables, list_slots, list_kinds)


def local(children, interp_theta, interp_phi, translator, send_index, list_slots, list_kinds):
    samp_count = lax.axis_size(SAMP)
    polar_total = interp_theta.shape[1]
    azimuth_total = interp_phi.shape[1]
    child_boxes, _, rows, child_azimuth = children.shape
    own_children = child_boxes // samp_count
    parent_boxes = child_boxes // 8
    out_rows = polar_total // samp_count
    pattern = (2, out_rows, azimuth_total)

    x = children.reshape(samp_count, own_children, 2, rows, child_azimuth)
    x = lax.all_to_all(x, SAMP, split_axis=0, concat_axis=0, tiled=True)

    cosine, sine = phase_tables(polar_total, azimuth_total)
    theta, phi = pl.pallas_call(
        prepare_kernel,
        out_shape=[
            pltpu.VMEM(interp_theta.shape[::-1], jnp.bfloat16),
            pltpu.VMEM(interp_phi.shape, jnp.bfloat16),
        ],
        in_specs=[HBM] * 2,
        out_specs=[VMEM] * 2,
        scratch_shapes=[
            pltpu.VMEM(interp_theta.shape, jnp.bfloat16),
            pltpu.SemaphoreType.DMA((2,)),
        ],
        compiler_params=pltpu.CompilerParams(vmem_limit_bytes=61 << 20),
        cost_estimate=pl.CostEstimate(flops=1 << 20, bytes_accessed=1 << 18, transcendentals=0),
        name="prepare",
    )(interp_theta, interp_phi)
    me = lax.axis_index("y") * lax.axis_size("c") + lax.axis_index("c")
    me = jnp.broadcast_to(me.astype(jnp.int32), (parent_boxes, WIDTH))
    tables = slot_tables(send_index)
    x, theta, phi, me, *tables = lax.optimization_barrier((x, theta, phi, me, *tables))
    mine = pl.pallas_call(
        aggregate_kernel,
        out_shape=jax.ShapeDtypeStruct((samp_count, own_children // 8) + pattern, jnp.bfloat16),
        in_specs=[VMEM] * 5,
        out_specs=VMEM,
        scratch_shapes=[
            pltpu.VMEM((16 * polar_total, child_azimuth), jnp.bfloat16),
        ],
        compiler_params=pltpu.CompilerParams(vmem_limit_bytes=12 << 20),
        cost_estimate=pl.CostEstimate(flops=335 << 20, bytes_accessed=4 << 20, transcendentals=0),
        name="aggregate",
    )(x, theta, phi, cosine, sine)
    source, mine = lax.optimization_barrier((translator, mine))
    whole = mine
    mine = lax.all_to_all(whole, SAMP, split_axis=0, concat_axis=0, tiled=True)
    far_table = shift(tables[0], "y", 2)
    far_whole = shift(whole, "y", 2)
    staged = pl.pallas_call(
        stage_kernel,
        out_shape=pltpu.VMEM(translator.shape, translator.dtype),
        in_specs=[HBM],
        out_specs=VMEM,
        scratch_shapes=[pltpu.SemaphoreType.DMA],
        compiler_params=pltpu.CompilerParams(vmem_limit_bytes=56 << 20),
        cost_estimate=pl.CostEstimate(flops=1, bytes_accessed=5 << 20, transcendentals=0),
        name="stage",
    )(source)
    lists = plan_lists(me, (*tables, far_table), list_slots, list_kinds)
    mine, lists, staged = lax.optimization_barrier((mine, lists, staged))
    own = mine.reshape((parent_boxes,) + pattern)
    after = shift(own, "y", -1)
    before = shift(own, "y", 1)
    other = shift(own, "c", 1)
    far_whole, staged, own = lax.optimization_barrier((far_whole, staged, own))
    far = lax.all_to_all(far_whole, SAMP, split_axis=0, concat_axis=0, tiled=True)
    far = far.reshape((parent_boxes,) + pattern)
    params = pltpu.CompilerParams(vmem_limit_bytes=4 << 20)
    cost = pl.CostEstimate(flops=16 << 20, bytes_accessed=8 << 20, transcendentals=0)

    def widen_tables(tables):
        return pl.pallas_call(
            widen_kernel,
            out_shape=pltpu.VMEM(translator.shape, jnp.float32),
            in_specs=[VMEM],
            out_specs=VMEM,
            compiler_params=params,
            cost_estimate=cost,
        )(tables)

    wide = widen_tables(staged)
    shape = (parent_boxes,) + pattern

    def translate(k, wide, blocks, so_far):
        first, last = k == 0, k == len(CUTS) - 2
        field = (jax.ShapeDtypeStruct if last else pltpu.VMEM)(shape, jnp.float32)
        rows = (2 if k >= FAR else 6) * parent_boxes + 1
        out = [field, pltpu.VMEM((rows,) + pattern, jnp.float32)]
        out_specs, scratch, aliases = [HBM if last else VMEM, VMEM], [], {}
        if first:
            out.append(jax.ShapeDtypeStruct(shape, jnp.bfloat16))
            out_specs.append(HBM)
            scratch = [pltpu.SemaphoreType.DMA]
            operands = blocks
        elif k == FAR:
            operands = [so_far[0], *blocks]
        else:
            operands = [so_far[0], *blocks, so_far[1]]
            aliases = {1 + len(operands): 1}
        kinds = [VMEM] * len(operands)
        if k == 1:
            kinds[-2] = HBM
            scratch = [pltpu.VMEM(shape, jnp.bfloat16), pltpu.SemaphoreType.DMA]
        if last:
            scratch = [pltpu.VMEM(shape, jnp.float32), pltpu.SemaphoreType.DMA((4,))]
        return pl.pallas_call(
            functools.partial(class_kernel, k),
            out_shape=out,
            in_specs=[SMEM, VMEM] + kinds,
            out_specs=out_specs,
            scratch_shapes=scratch,
            input_output_aliases=aliases,
            compiler_params=params,
            cost_estimate=cost,
        )(lists, wide, *operands)

    *state, parents = translate(0, wide, [own, other], None)
    after, before, *state = lax.optimization_barrier((after, before, *state))
    across = [shift(after, "c", 1), shift(before, "c", 1)]
    state = translate(1, wide, [before, after], state)
    state = translate(2, wide, across, state)
    far, staged, *state = lax.optimization_barrier((far, staged, *state))
    across = shift(far, "c", 1)
    wide = widen_tables(staged)
    state = translate(3, wide, [far], state)
    field, _ = translate(4, wide, [across], state)
    return parents, field


def solution(mesh):
    y_count, x_count = 4, 4
    fine = Mesh(
        mesh.devices.reshape(y_count, mesh.shape["box"] // y_count, x_count, -1),
        BOX + SAMP,
    )
    return jax.shard_map(
        local,
        mesh=fine,
        in_specs=(
            P(BOX, None, SAMP, None),
            P(),
            P(),
            P(None, None, SAMP, None),
            P(BOX, None, None),
            P(BOX, None),
            P(BOX, None),
        ),
        out_specs=(P(BOX, None, SAMP, None), P(BOX, None, SAMP, None)),
        check_vma=False,
    )
```
